256 devices in a mesh: row: 16 (over y_hi, x, core), col: 16 (over z, y_lo).
Axes of the slice: x: 4, y: 4 (y_hi: 2, y_lo: 2; y = y_hi * 2 + y_lo), z: 8, core: 2. Of those that a mesh axis runs over, the one named last changes fastest.
Arguments:
- tile_matrix: bfloat16 [2, 1024, 1024], replicated
- tile_inverse: bfloat16 [2, 1024, 1024], replicated, as said below
- block_rows: int32 [16, 16, 4], P('row', 'col'), may hold values from 0 to 1, as said below
- block_cols: int32 [16, 16, 4], P('row', 'col'), may hold values from 0 to 1
- block_tiles: int32 [16, 16, 4], P('row', 'col'), may hold values from 0 to 1
- block_count: int32 [16, 16], P('row', 'col'), may hold values from 2 to 4, as said below
- column_values: float32 [64, 32768], P(None, 'col'), may hold values from -6 to 6
- column_duals: float32 [64, 32768], P(None, 'col'), may hold values from -3 to 3
- unit_cost: float32 [64, 32768], P(None, 'col'), may hold values from 0.1 to 1
- capacity: float32 [64, 32768], P(None, 'col'), may hold values from 0.5 to 3
- row_values: float32 [64, 32768], P(None, 'row'), may hold values from -6 to 6
- row_duals: float32 [64, 32768], P(None, 'row'), may hold values from -3 to 3
- row_lower: float32 [64, 32768], P(None, 'row'), may hold values from -1.5 to -0.2
- row_upper: float32 [64, 32768], P(None, 'row'), may hold values from 0.2 to 1.5
- block_image: float32 [16, 16, 4, 64, 1024], P('row', 'col'), may hold values from -6 to 6
- image_dual: float32 [16, 16, 4, 64, 1024], P('row', 'col'), may hold values from -3 to 3
- input_dual: float32 [16, 16, 4, 64, 1024], P('row', 'col'), may hold values from -3 to 3
Outputs:
- column_solution: float32 [64, 32768], P(None, 'col')
- row_solution: float32 [64, 32768], P(None, 'row')
The draws below stay inside these ranges and needn't reach their ends.
Inputs may be any that keep to these rules, and one draw needn't show every extreme that they name: tile_inverse[t] is the inverse of I + A A^T for A = tile_matrix[t] as given, computed in float32 and rounded. On one device the live slots name different (block_rows, block_cols) pairs. Slots 0 to block_count - 1 of a device are live; some device fills all 4 slots.
All inputs are finite; a program needn't handle non-finite values.
Results may differ from the reference program's by a relative error of at most 0.0035.
Values sent between devices are 32-bit elements; how exact they have to be, the bound alone decides.
A program may use at most 64 MiB of HBM per device.

```python
import math
import jax
import jax.numpy as jnp
from jax import lax

BS = 1024
S = 64
RB_DEV = 2
CB_DEV = 2
NT = 2
ITERS = 2
NBLK = 4
ROW_DEVS = 16
COL_DEVS = 16
NR = 32768
NC = 32768
N_ROW = 16
N_COL = 16


def tile_pair(key):
    base_key = jax.random.fold_in(key, 11)
    raw_tiles = jax.random.normal(base_key, (NT, BS, BS), jnp.float32)
    matrix = (raw_tiles / math.sqrt(BS)).astype(jnp.bfloat16)
    rounded = matrix.astype(jnp.float32)
    gram = jnp.einsum('tik,tjk->tij', rounded, rounded, precision=lax.Precision.HIGHEST)
    identity = jnp.broadcast_to(jnp.eye(BS, dtype=jnp.float32), (NT, BS, BS))
    inverse = jnp.linalg.solve(identity + gram, identity)
    return (matrix, inverse.astype(jnp.bfloat16))


def draw_tile_matrix(key, part):
    return tile_pair(key)[0]


def draw_tile_inverse(key, part):
    return tile_pair(key)[1]


def block_positions(key):
    base_key = jax.random.fold_in(key, 23)
    raw_scores = jax.random.randint(base_key, (ROW_DEVS, COL_DEVS, NBLK), 0, 1048576, dtype=jnp.int32)
    slot_ids = jnp.broadcast_to(jnp.arange(NBLK, dtype=jnp.int32), (ROW_DEVS, COL_DEVS, NBLK))
    scores = raw_scores * NBLK + slot_ids
    sorted_scores, ordering = lax.sort_key_val(scores, slot_ids, dimension=2)
    ordering = ordering.astype(jnp.int32)
    return (ordering // CB_DEV, ordering % CB_DEV)


def draw_block_rows(key, part):
    return block_positions(key)[0].astype(jnp.int32)


def draw_block_cols(key, part):
    return block_positions(key)[1].astype(jnp.int32)


def draw_block_count(key, part):
    base_key = jax.random.fold_in(key, 37)
    levels = jax.random.randint(base_key, (ROW_DEVS, COL_DEVS), 0, 8, dtype=jnp.int32)
    counted = jnp.where(levels < 2, 2, jnp.where(levels < 5, 3, 4)).astype(jnp.int32)
    counted = jnp.minimum(counted, NBLK).astype(jnp.int32)
    chosen = jax.random.randint(jax.random.fold_in(base_key, 1), (), 0, ROW_DEVS * COL_DEVS, dtype=jnp.int32)
    flat_index = jnp.arange(ROW_DEVS * COL_DEVS, dtype=jnp.int32).reshape(ROW_DEVS, COL_DEVS)
    return jnp.where(flat_index == chosen, NBLK, counted).astype(jnp.int32)


def touch_ends(array, own_key, least, top_value):
    longest = array.shape.index(max(array.shape))
    spots = []
    for shift in (0, 1):
        where = [jax.random.randint(jax.random.fold_in(own_key, axis), (), 0, length) for axis, length in enumerate(array.shape)]
        where[longest] = (where[longest] + shift) % array.shape[longest]
        spots.append(tuple(where))
    return array.at[spots[0]].set(least).at[spots[1]].set(top_value)


def shard_levels(key, extent, pieces, least, high):
    loudness = 1.0
    for axis_at, parts in pieces:
        draws = jax.random.uniform(jax.random.fold_in(jax.random.fold_in(key, 6), axis_at), (parts,), jnp.float32, least / len(pieces), high / len(pieces))
        loudness = loudness * jnp.repeat(jnp.exp(draws), extent[axis_at] // parts).reshape((-1,) + (1,) * (len(extent) - 1 - axis_at))
    return loudness


def gaussian(own_key, extent, scale, most, split=(), kind=jnp.bfloat16):
    values = scale * jax.random.normal(own_key, extent, jnp.float32)
    if split:
        values = values * shard_levels(own_key, extent, split, -0.22, 0.18)
    return jnp.clip(values, -most, most).astype(kind)


def setup_inputs(seed: int = 0) -> dict:
    key_list = jax.random.split(jax.random.key(seed), 18)
    return {
        "tile_matrix": draw_tile_matrix(jax.random.fold_in(key_list[17], 71), 0),
        "tile_inverse": draw_tile_inverse(jax.random.fold_in(key_list[17], 71), 0),
        "block_rows": draw_block_rows(jax.random.fold_in(key_list[17], 71), 0),
        "block_cols": draw_block_cols(jax.random.fold_in(key_list[17], 71), 0),
        "block_tiles": touch_ends(jax.random.randint(key_list[4], (ROW_DEVS, COL_DEVS, NBLK), 0, NT), jax.random.fold_in(key_list[4], 1), 0, NT - 1).astype(jnp.int32),
        "block_count": draw_block_count(jax.random.fold_in(key_list[17], 71), 0),
        "column_values": gaussian(key_list[6], (S, NC), 1.0, 6.0, ((1, 16),), jnp.float32),
        "column_duals": gaussian(key_list[7], (S, NC), 0.5, 3.0, ((1, 16),), jnp.float32),
        "unit_cost": jnp.clip(0.1 + 0.9 * jax.random.uniform(key_list[8], (S, NC), jnp.float32) ** shard_levels(key_list[8], (S, NC), ((1, 16),), -0.2, 0.2), 0.1, 1.0),
        "capacity": jnp.clip(jnp.exp(math.log(3.0) - 1.7917595 * jax.random.uniform(key_list[9], (S, NC), jnp.float32) ** shard_levels(key_list[9], (S, NC), ((1, 16),), -0.2, 0.2)), 0.5, 3.0),
        "row_values": gaussian(key_list[10], (S, NR), 1.0, 6.0, ((1, 16),), jnp.float32),
        "row_duals": gaussian(key_list[11], (S, NR), 0.5, 3.0, ((1, 16),), jnp.float32),
        "row_lower": jnp.clip(-1.5 + 1.3 * jax.random.uniform(key_list[12], (S, NR), jnp.float32) ** shard_levels(key_list[12], (S, NR), ((1, 16),), -0.2, 0.2), -1.5, -0.2),
        "row_upper": jnp.clip(0.2 + 1.3 * jax.random.uniform(key_list[13], (S, NR), jnp.float32) ** shard_levels(key_list[13], (S, NR), ((1, 16),), -0.2, 0.2), 0.2, 1.5),
        "block_image": gaussian(key_list[14], (ROW_DEVS, COL_DEVS, NBLK, S, BS), 1.0, 6.0, ((0, 16), (1, 16)), jnp.float32),
        "image_dual": gaussian(key_list[15], (ROW_DEVS, COL_DEVS, NBLK, S, BS), 0.5, 3.0, ((0, 16), (1, 16)), jnp.float32),
        "input_dual": gaussian(key_list[16], (ROW_DEVS, COL_DEVS, NBLK, S, BS), 0.5, 3.0, ((0, 16), (1, 16)), jnp.float32),
    }


def round_half(values):
    return lax.optimization_barrier(values.astype(jnp.bfloat16)).astype(jnp.float32)

def reference(tile_matrix, tile_inverse, block_rows, block_cols, block_tiles, block_count, column_values, column_duals, unit_cost, capacity, row_values, row_duals, row_lower, row_upper, block_image, image_dual, input_dual):
    slot_total = N_ROW * N_COL * NBLK
    row_grid = RB_DEV * N_ROW
    col_grid = CB_DEV * N_COL
    row_index = jnp.arange(N_ROW, dtype=jnp.int32)[:, None, None]
    col_index = jnp.arange(N_COL, dtype=jnp.int32)[None, :, None]
    global_rows = (row_index * RB_DEV + block_rows).reshape(-1).astype(jnp.int32)
    global_cols = (col_index * CB_DEV + block_cols).reshape(-1).astype(jnp.int32)
    tile_ids = block_tiles.reshape(-1).astype(jnp.int32)
    live_slot = (jnp.arange(NBLK, dtype=jnp.int32)[None, None, :] < block_count[:, :, None]).reshape(-1)
    live_float = live_slot.astype(jnp.float32)
    col_count = jnp.zeros((col_grid,), jnp.float32).at[global_cols].add(live_float)
    row_count = jnp.zeros((row_grid,), jnp.float32).at[global_rows].add(live_float)
    col_denom = 1.0 + jnp.repeat(col_count, BS)
    row_denom = 1.0 + jnp.repeat(row_count, BS)
    images = block_image.reshape(slot_total, S, BS)
    image_duals = image_dual.reshape(slot_total, S, BS)
    input_duals = input_dual.reshape(slot_total, S, BS)
    matrix_f = tile_matrix.astype(jnp.float32)
    inverse_f = tile_inverse.astype(jnp.float32)
    x_values, x_duals = (column_values, column_duals)
    y_values, y_duals = (row_values, row_duals)
    for iteration in range(ITERS):
        x_half = jnp.clip(x_values - x_duals - unit_cost, 0.0, capacity)
        y_half = jnp.clip(y_values - y_duals, row_lower, row_upper)
        x_blocks = x_values.reshape(S, col_grid, BS)

        def one_slot(carry, item):
            image_k, image_dual_k, input_dual_k, tile_k, column_k, live_k = item

            def active():
                matrix_t = lax.dynamic_index_in_dim(matrix_f, tile_k, 0, keepdims=False)
                inverse_t = lax.dynamic_index_in_dim(inverse_f, tile_k, 0, keepdims=False)
                image_gap = round_half(image_k - image_dual_k)
                x_column = lax.dynamic_index_in_dim(x_blocks, column_k, 1, keepdims=False)
                pulled = jnp.dot(image_gap, matrix_t.T, precision=lax.Precision.HIGHEST)
                merged = round_half(x_column - input_dual_k + pulled)
                x_proj = jnp.dot(merged, inverse_t, precision=lax.Precision.HIGHEST)
                y_proj = jnp.dot(round_half(x_proj), matrix_t, precision=lax.Precision.HIGHEST)
                return (x_proj, y_proj)

            def skipped():
                return (jnp.zeros((S, BS), jnp.float32), jnp.zeros((S, BS), jnp.float32))
            return (carry, lax.cond(live_k, active, skipped))
        carry_out, projected = lax.scan(one_slot, jnp.zeros((), jnp.float32), (images, image_duals, input_duals, tile_ids, global_cols, live_slot))
        x_proj_all, y_proj_all = projected
        col_sum = jnp.zeros((col_grid, S, BS), jnp.float32).at[global_cols].add(live_float[:, None, None] * (x_proj_all + input_duals))
        col_sum = jnp.transpose(col_sum, (1, 0, 2)).reshape(S, col_grid * BS)
        x_new = (x_half + x_duals + col_sum) / col_denom[None, :]
        x_duals = x_duals + x_half - x_new
        x_slots = jnp.transpose(x_new.reshape(S, col_grid, BS)[:, global_cols, :], (1, 0, 2))
        input_duals = input_duals + x_proj_all - x_slots
        row_sum = jnp.zeros((row_grid, S, BS), jnp.float32).at[global_rows].add(live_float[:, None, None] * (y_proj_all + image_duals))
        row_sum = jnp.transpose(row_sum, (1, 0, 2)).reshape(S, row_grid * BS)
        y_anchor = y_half + y_duals
        row_shift = (row_sum - y_anchor) / row_denom[None, :]
        y_new = y_anchor + row_shift
        y_duals = y_duals + y_half - y_new
        shift_slots = jnp.transpose(row_shift.reshape(S, row_grid, BS)[:, global_rows, :], (1, 0, 2))
        new_images = y_proj_all + image_duals - shift_slots
        image_duals = image_duals + y_proj_all - new_images
        images = new_images
        x_values, y_values = (x_new, y_new)
    column_solution = jnp.clip(x_values - x_duals - unit_cost, 0.0, capacity)
    row_solution = jnp.clip(y_values - y_duals, row_lower, row_upper)
    return (column_solution, row_solution)
```

```python
import functools

import jax
import jax.numpy as jnp
from jax import lax
from jax.experimental import pallas as pl
from jax.experimental.pallas import tpu as pltpu
from jax.sharding import PartitionSpec as P

ITERS = 2
MESH = pl.DeviceIdType.MESH
AXES = ("row", "col")


def peer_id(axis, peer):
    if axis == "row":
        return (peer, lax.axis_index("col"))
    return (lax.axis_index("row"), peer)


def reduce_kernel(n, group_axes, *refs):
    groups = len(group_axes)
    ins = refs[:groups]
    outs = refs[groups : 2 * groups]
    scratch = refs[2 * groups :]
    per = [scratch[6 * g : 6 * g + 6] for g in range(groups)]
    barrier = pltpu.get_barrier_semaphore()
    for axis in group_axes:
        me = lax.axis_index(axis)
        for k in range(1, n):
            peer = lax.rem(me + k, n)
            pl.semaphore_signal(barrier, inc=1, device_id=peer_id(axis, peer), device_id_type=MESH)
    pl.semaphore_wait(barrier, groups * (n - 1))

    width = ins[0].shape[1] // n

    def cols(index):
        return pl.ds(pl.multiple_of(index * width, width), width)

    scatter = []
    for g, axis in enumerate(group_axes):
        recv, gathered, s1, r1, s2, r2 = per[g]
        me = lax.axis_index(axis)
        copies = []
        for k in range(1, n):
            peer = lax.rem(me + k, n)
            copy = pltpu.make_async_remote_copy(
                src_ref=ins[g].at[:, cols(peer)],
                dst_ref=recv.at[me],
                send_sem=s1.at[peer],
                recv_sem=r1.at[me],
                device_id=peer_id(axis, peer),
                device_id_type=MESH,
            )
            copy.start()
            copies.append(copy)
        scatter.append(copies)

    gathers = []
    for g, axis in enumerate(group_axes):
        recv, gathered, s1, r1, s2, r2 = per[g]
        me = lax.axis_index(axis)
        for k in range(1, n):
            source = lax.rem(me + n - k, n)
            pltpu.make_async_remote_copy(
                src_ref=ins[g].at[:, cols(source)],
                dst_ref=recv.at[source],
                send_sem=s1.at[source],
                recv_sem=r1.at[source],
                device_id=peer_id(axis, source),
                device_id_type=MESH,
            ).wait_recv()
        total = ins[g][:, cols(me)]
        for k in range(1, n):
            total = total + recv[lax.rem(me + k, n)]
        gathered[me] = total
        copies = []
        for k in range(1, n):
            peer = lax.rem(me + k, n)
            copy = pltpu.make_async_remote_copy(
                src_ref=gathered.at[me],
                dst_ref=gathered.at[me],
                send_sem=s2.at[peer],
                recv_sem=r2.at[me],
                device_id=peer_id(axis, peer),
                device_id_type=MESH,
            )
            copy.start()
            copies.append(copy)
        gathers.append(copies)

    for g, axis in enumerate(group_axes):
        recv, gathered, s1, r1, s2, r2 = per[g]
        me = lax.axis_index(axis)
        for copy in scatter[g]:
            copy.wait_send()
        for k in range(1, n):
            source = lax.rem(me + n - k, n)
            pltpu.make_async_remote_copy(
                src_ref=gathered.at[source],
                dst_ref=gathered.at[source],
                send_sem=s2.at[source],
                recv_sem=r2.at[source],
                device_id=peer_id(axis, source),
                device_id_type=MESH,
            ).wait_recv()
        for copy in gathers[g]:
            copy.wait_send()
        for index in range(n):
            outs[g][:, index * width : (index + 1) * width] = gathered[index]


def all_reduce(arrays, group_axes, n, collective_id):
    shapes = [a.shape for a in arrays]
    width = shapes[0][1] // n
    scratch = []
    for rows, _ in shapes:
        scratch += [
            pltpu.VMEM((n, rows, width), jnp.float32),
            pltpu.VMEM((n, rows, width), jnp.float32),
            pltpu.SemaphoreType.DMA((n,)),
            pltpu.SemaphoreType.DMA((n,)),
            pltpu.SemaphoreType.DMA((n,)),
            pltpu.SemaphoreType.DMA((n,)),
        ]
    return pl.pallas_call(
        functools.partial(reduce_kernel, n, group_axes),
        out_shape=tuple(jax.ShapeDtypeStruct(s, jnp.float32) for s in shapes),
        in_specs=[pl.BlockSpec(memory_space=pltpu.VMEM)] * len(arrays),
        out_specs=tuple(pl.BlockSpec(memory_space=pltpu.VMEM) for _ in arrays),
        scratch_shapes=scratch,
        compiler_params=pltpu.CompilerParams(collective_id=collective_id, has_side_effects=True),
    )(*arrays)


def project_block(
    x_full, matrix_t, inverse_t, image_now, image_gap_dual, input_now, column, block_width
):
    image_gap = (image_now - image_gap_dual).astype(jnp.bfloat16)
    x_column = lax.dynamic_slice_in_dim(x_full, column * block_width, block_width, 1)
    pulled = lax.dot_general(
        image_gap, matrix_t, (((1,), (1,)), ((), ())), preferred_element_type=jnp.float32
    )
    merged_input = (x_column - input_now + pulled).astype(jnp.bfloat16)
    x_proj = jnp.dot(merged_input, inverse_t, preferred_element_type=jnp.float32)
    y_proj = jnp.dot(x_proj.astype(jnp.bfloat16), matrix_t, preferred_element_type=jnp.float32)
    return (x_proj, y_proj)


def per_device(
    tile_matrix,
    tile_inverse,
    block_rows,
    block_cols,
    block_tiles,
    block_count,
    column_values,
    column_duals,
    unit_cost,
    capacity,
    row_values,
    row_duals,
    row_lower,
    row_upper,
    block_image,
    image_dual,
    input_dual,
):
    block_width = tile_matrix.shape[1]
    scenarios = column_values.shape[0]
    col_blocks = column_values.shape[1] // block_width
    row_blocks = row_values.shape[1] // block_width
    slot_total = block_rows.shape[2]
    n_row = lax.axis_size("row")
    n_col = lax.axis_size("col")
    rows_here = block_rows[0, 0]
    cols_here = block_cols[0, 0]
    tiles_here = block_tiles[0, 0]
    live_slot = jnp.arange(slot_total, dtype=jnp.int32) < block_count[0, 0]
    x_own = column_values
    x_dual = column_duals
    y_state = row_values
    y_dual = row_duals
    x_full = column_values
    images = [block_image[0, 0, slot_index] for slot_index in range(slot_total)]
    image_duals = [image_dual[0, 0, slot_index] for slot_index in range(slot_total)]
    input_duals = [input_dual[0, 0, slot_index] for slot_index in range(slot_total)]
    zero_block = jnp.zeros((scenarios, block_width), jnp.float32)
    col_denom = None
    row_denom = None
    for iteration in range(ITERS):
        x_half = jnp.clip(x_own - x_dual - unit_cost, 0.0, capacity)
        y_half = jnp.clip(y_state - y_dual, row_lower, row_upper)
        y_anchor = y_half + y_dual
        col_terms = jnp.zeros((scenarios, col_blocks, block_width), jnp.float32)
        row_terms = jnp.zeros((scenarios, row_blocks, block_width), jnp.float32)
        col_live = jnp.zeros((col_blocks,), jnp.float32)
        row_live = jnp.zeros((row_blocks,), jnp.float32)
        projected = []
        for slot_index in range(slot_total):

            def active(slot_index=slot_index):
                matrix_t = lax.dynamic_index_in_dim(
                    tile_matrix, tiles_here[slot_index], 0, keepdims=False
                )
                inverse_t = lax.dynamic_index_in_dim(
                    tile_inverse, tiles_here[slot_index], 0, keepdims=False
                )
                return project_block(
                    x_full,
                    matrix_t,
                    inverse_t,
                    images[slot_index],
                    image_duals[slot_index],
                    input_duals[slot_index],
                    cols_here[slot_index],
                    block_width,
                )

            def skipped():
                return (zero_block, zero_block)

            x_proj, y_proj = lax.cond(live_slot[slot_index], active, skipped)
            col_pick = (
                (jnp.arange(col_blocks, dtype=jnp.int32) == cols_here[slot_index])
                & live_slot[slot_index]
            ).astype(jnp.float32)
            row_pick = (
                (jnp.arange(row_blocks, dtype=jnp.int32) == rows_here[slot_index])
                & live_slot[slot_index]
            ).astype(jnp.float32)
            col_live = col_live + col_pick
            row_live = row_live + row_pick
            col_terms = (
                col_terms + col_pick[None, :, None] * (x_proj + input_duals[slot_index])[:, None, :]
            )
            row_terms = (
                row_terms + row_pick[None, :, None] * (y_proj + image_duals[slot_index])[:, None, :]
            )
            projected.append((x_proj, y_proj))
        col_terms = col_terms.reshape(scenarios, col_blocks * block_width)
        row_terms = row_terms.reshape(scenarios, row_blocks * block_width)
        if iteration == 0:
            col_extra = jnp.zeros((8, col_blocks * block_width), jnp.float32).at[0].set(
                jnp.repeat(col_live, block_width)
            )
            row_extra = jnp.zeros((8, row_blocks * block_width), jnp.float32).at[0].set(
                jnp.repeat(row_live, block_width)
            )
            col_total, row_total = all_reduce(
                [
                    jnp.concatenate([col_terms, col_extra], axis=0),
                    jnp.concatenate([row_terms, row_extra], axis=0),
                ],
                AXES,
                n_row,
                0,
            )
            col_denom = 1.0 + col_total[scenarios : scenarios + 1]
            row_denom = 1.0 + row_total[scenarios : scenarios + 1]
            col_total = col_total[:scenarios]
            row_total = row_total[:scenarios]
        else:
            col_total, row_total = all_reduce([col_terms, row_terms], AXES, n_row, 1)
        x_own = (x_half + x_dual + col_total) / col_denom
        x_dual = x_dual + x_half - x_own
        x_full = x_own
        shift_full = (row_total - y_anchor) / row_denom
        y_state = y_anchor + shift_full
        y_dual = y_dual + y_half - y_state
        for slot_index in range(slot_total):
            x_proj, y_proj = projected[slot_index]
            x_column = lax.dynamic_slice_in_dim(
                x_full, cols_here[slot_index] * block_width, block_width, 1
            )
            input_duals[slot_index] = input_duals[slot_index] + x_proj - x_column
            shift_rows = lax.dynamic_slice_in_dim(
                shift_full, rows_here[slot_index] * block_width, block_width, 1
            )
            new_image = y_proj + image_duals[slot_index] - shift_rows
            image_duals[slot_index] = image_duals[slot_index] + y_proj - new_image
            images[slot_index] = new_image
    column_final = jnp.clip(x_own - x_dual - unit_cost, 0.0, capacity)
    row_final = jnp.clip(y_state - y_dual, row_lower, row_upper)
    return (column_final, row_final)


def solution(mesh):
    placed = (
        P(),
        P(),
        P("row", "col", None),
        P("row", "col", None),
        P("row", "col", None),
        P("row", "col"),
        P(None, "col"),
        P(None, "col"),
        P(None, "col"),
        P(None, "col"),
        P(None, "row"),
        P(None, "row"),
        P(None, "row"),
        P(None, "row"),
        P("row", "col", None, None, None),
        P("row", "col", None, None, None),
        P("row", "col", None, None, None),
    )
    return jax.shard_map(
        per_device,
        mesh=mesh,
        in_specs=placed,
        out_specs=(P(None, "col"), P(None, "row")),
        check_vma=False,
    )
```

```python
import functools

import jax
import jax.numpy as jnp
from jax import lax
from jax.experimental import pallas as pl
from jax.experimental.pallas import tpu as pltpu
from jax.sharding import PartitionSpec as P

ITERS = 2
MESH = pl.DeviceIdType.MESH
AXES = ("row", "col")


def peer_id(axis, peer):
    if axis == "row":
        return (peer, lax.axis_index("col"))
    return (lax.axis_index("row"), peer)


def reduce_kernel(n, group_axes, *refs):
    groups = len(group_axes)
    ins = refs[:groups]
    outs = refs[groups : 2 * groups]
    scratch = refs[2 * groups :]
    per = [scratch[6 * g : 6 * g + 6] for g in range(groups)]
    barrier = pltpu.get_barrier_semaphore()
    for axis in group_axes:
        me = lax.axis_index(axis)
        for k in range(1, n):
            peer = lax.rem(me + k, n)
            pl.semaphore_signal(barrier, inc=1, device_id=peer_id(axis, peer), device_id_type=MESH)
    pl.semaphore_wait(barrier, groups * (n - 1))

    width = ins[0].shape[1] // n

    def cols(index):
        return pl.ds(pl.multiple_of(index * width, width), width)

    scatter = []
    for g, axis in enumerate(group_axes):
        recv, gathered, s1, r1, s2, r2 = per[g]
        me = lax.axis_index(axis)
        copies = []
        for k in range(1, n):
            peer = lax.rem(me + k, n)
            copy = pltpu.make_async_remote_copy(
                src_ref=ins[g].at[:, cols(peer)],
                dst_ref=recv.at[me],
                send_sem=s1.at[peer],
                recv_sem=r1.at[me],
                device_id=peer_id(axis, peer),
                device_id_type=MESH,
            )
            copy.start()
            copies.append(copy)
        scatter.append(copies)

    gathers = []
    for g, axis in enumerate(group_axes):
        recv, gathered, s1, r1, s2, r2 = per[g]
        me = lax.axis_index(axis)
        for k in range(1, n):
            source = lax.rem(me + n - k, n)
            pltpu.make_async_remote_copy(
                src_ref=ins[g].at[:, cols(source)],
                dst_ref=recv.at[source],
                send_sem=s1.at[source],
                recv_sem=r1.at[source],
                device_id=peer_id(axis, source),
                device_id_type=MESH,
            ).wait_recv()
        total = ins[g][:, cols(me)]
        for k in range(1, n):
            total = total + recv[lax.rem(me + k, n)]
        gathered[me] = total
        copies = []
        for k in range(1, n):
            peer = lax.rem(me + k, n)
            copy = pltpu.make_async_remote_copy(
                src_ref=gathered.at[me],
                dst_ref=gathered.at[me],
                send_sem=s2.at[peer],
                recv_sem=r2.at[me],
                device_id=peer_id(axis, peer),
                device_id_type=MESH,
            )
            copy.start()
            copies.append(copy)
        gathers.append(copies)

    for g, axis in enumerate(group_axes):
        recv, gathered, s1, r1, s2, r2 = per[g]
        me = lax.axis_index(axis)
        for copy in scatter[g]:
            copy.wait_send()
        for k in range(1, n):
            source = lax.rem(me + n - k, n)
            pltpu.make_async_remote_copy(
                src_ref=gathered.at[source],
                dst_ref=gathered.at[source],
                send_sem=s2.at[source],
                recv_sem=r2.at[source],
                device_id=peer_id(axis, source),
                device_id_type=MESH,
            ).wait_recv()
        for copy in gathers[g]:
            copy.wait_send()
        for index in range(n):
            outs[g][:, index * width : (index + 1) * width] = gathered[index]


def all_reduce(arrays, group_axes, n, collective_id):
    shapes = [a.shape for a in arrays]
    width = shapes[0][1] // n
    scratch = []
    for rows, _ in shapes:
        scratch += [
            pltpu.VMEM((n, rows, width), jnp.float32),
            pltpu.VMEM((n, rows, width), jnp.float32),
            pltpu.SemaphoreType.DMA((n,)),
            pltpu.SemaphoreType.DMA((n,)),
            pltpu.SemaphoreType.DMA((n,)),
            pltpu.SemaphoreType.DMA((n,)),
        ]
    return pl.pallas_call(
        functools.partial(reduce_kernel, n, group_axes),
        out_shape=tuple(jax.ShapeDtypeStruct(s, jnp.float32) for s in shapes),
        in_specs=[pl.BlockSpec(memory_space=pltpu.VMEM)] * len(arrays),
        out_specs=tuple(pl.BlockSpec(memory_space=pltpu.VMEM) for _ in arrays),
        scratch_shapes=scratch,
        compiler_params=pltpu.CompilerParams(collective_id=collective_id, has_side_effects=True),
    )(*arrays)


def pick_blocks(full, index, blocks, block_width):
    parts = full.reshape(full.shape[0], blocks, block_width)
    chosen = parts[:, 0][None]
    for b in range(1, blocks):
        chosen = jnp.where((index == b)[:, None, None], parts[:, b][None], chosen)
    return chosen


def by_tile(stacked, matrices, tiles, contract, slots):
    results = [
        lax.dot_general(
            stacked, matrices[t], (((1,), (contract,)), ((), ())),
            preferred_element_type=jnp.float32,
        )
        for t in range(matrices.shape[0])
    ]
    chosen = results[0].reshape(slots, -1, stacked.shape[1])
    for t in range(1, len(results)):
        chosen = jnp.where(
            (tiles == t)[:, None, None], results[t].reshape(slots, -1, stacked.shape[1]), chosen
        )
    return chosen


def per_device(
    tile_matrix,
    tile_inverse,
    block_rows,
    block_cols,
    block_tiles,
    block_count,
    column_values,
    column_duals,
    unit_cost,
    capacity,
    row_values,
    row_duals,
    row_lower,
    row_upper,
    block_image,
    image_dual,
    input_dual,
):
    block_width = tile_matrix.shape[1]
    scenarios = column_values.shape[0]
    col_blocks = column_values.shape[1] // block_width
    row_blocks = row_values.shape[1] // block_width
    slot_total = block_rows.shape[2]
    n_row = lax.axis_size("row")
    rows_here = block_rows[0, 0]
    cols_here = block_cols[0, 0]
    tiles_here = block_tiles[0, 0]
    live_slot = jnp.arange(slot_total, dtype=jnp.int32) < block_count[0, 0]
    x_own = column_values
    x_dual = column_duals
    y_state = row_values
    y_dual = row_duals
    images = block_image[0, 0]
    image_duals = image_dual[0, 0]
    input_duals = input_dual[0, 0]
    col_mask = [(live_slot & (cols_here == b))[:, None, None] for b in range(col_blocks)]
    row_mask = [(live_slot & (rows_here == b))[:, None, None] for b in range(row_blocks)]
    col_denom = None
    row_denom = None
    for iteration in range(ITERS):
        x_half = jnp.clip(x_own - x_dual - unit_cost, 0.0, capacity)
        y_half = jnp.clip(y_state - y_dual, row_lower, row_upper)
        y_anchor = y_half + y_dual
        image_gap = (images - image_duals).astype(jnp.bfloat16).reshape(-1, block_width)
        pulled = by_tile(image_gap, tile_matrix, tiles_here, 1, slot_total)
        x_columns = pick_blocks(x_own, cols_here, col_blocks, block_width)
        merged = (x_columns - input_duals + pulled).astype(jnp.bfloat16).reshape(-1, block_width)
        x_proj = by_tile(merged, tile_inverse, tiles_here, 0, slot_total)
        y_proj = by_tile(
            x_proj.astype(jnp.bfloat16).reshape(-1, block_width), tile_matrix, tiles_here, 0,
            slot_total,
        )
        x_terms = x_proj + input_duals
        y_terms = y_proj + image_duals
        col_terms = jnp.concatenate(
            [jnp.sum(jnp.where(m, x_terms, 0.0), axis=0) for m in col_mask], axis=1
        )
        row_terms = jnp.concatenate(
            [jnp.sum(jnp.where(m, y_terms, 0.0), axis=0) for m in row_mask], axis=1
        )
        if iteration == 0:
            col_live = jnp.stack([jnp.sum(m.astype(jnp.float32)) for m in col_mask])
            row_live = jnp.stack([jnp.sum(m.astype(jnp.float32)) for m in row_mask])
            col_extra = jnp.zeros((8, col_blocks * block_width), jnp.float32).at[0].set(
                jnp.repeat(col_live, block_width)
            )
            row_extra = jnp.zeros((8, row_blocks * block_width), jnp.float32).at[0].set(
                jnp.repeat(row_live, block_width)
            )
            col_total, row_total = all_reduce(
                [
                    jnp.concatenate([col_terms, col_extra], axis=0),
                    jnp.concatenate([row_terms, row_extra], axis=0),
                ],
                AXES,
                n_row,
                0,
            )
            col_denom = 1.0 + col_total[scenarios : scenarios + 1]
            row_denom = 1.0 + row_total[scenarios : scenarios + 1]
            col_total = col_total[:scenarios]
            row_total = row_total[:scenarios]
        else:
            col_total, row_total = all_reduce([col_terms, row_terms], AXES, n_row, 1)
        x_own = (x_half + x_dual + col_total) / col_denom
        x_dual = x_dual + x_half - x_own
        shift_full = (row_total - y_anchor) / row_denom
        y_state = y_anchor + shift_full
        y_dual = y_dual + y_half - y_state
        input_duals = input_duals + x_proj - pick_blocks(x_own, cols_here, col_blocks, block_width)
        new_images = y_proj + image_duals - pick_blocks(shift_full, rows_here, row_blocks, block_width)
        image_duals = image_duals + y_proj - new_images
        images = new_images
    column_final = jnp.clip(x_own - x_dual - unit_cost, 0.0, capacity)
    row_final = jnp.clip(y_state - y_dual, row_lower, row_upper)
    return (column_final, row_final)


def solution(mesh):
    placed = (
        P(),
        P(),
        P("row", "col", None),
        P("row", "col", None),
        P("row", "col", None),
        P("row", "col"),
        P(None, "col"),
        P(None, "col"),
        P(None, "col"),
        P(None, "col"),
        P(None, "row"),
        P(None, "row"),
        P(None, "row"),
        P(None, "row"),
        P("row", "col", None, None, None),
        P("row", "col", None, None, None),
        P("row", "col", None, None, None),
    )
    return jax.shard_map(
        per_device,
        mesh=mesh,
        in_specs=placed,
        out_specs=(P(None, "col"), P(None, "row")),
        check_vma=False,
    )
```

```python
import functools

import jax
import jax.numpy as jnp
from jax import lax
from jax.experimental import pallas as pl
from jax.experimental.pallas import tpu as pltpu
from jax.sharding import PartitionSpec as P

ITERS = 2
MESH = pl.DeviceIdType.MESH
AXES = ("row", "col")


def peer_id(axis, peer):
    if axis == "row":
        return (peer, lax.axis_index("col"))
    return (lax.axis_index("row"), peer)


def reduce_kernel(n, group_axes, *refs):
    groups = len(group_axes)
    ins = refs[:groups]
    outs = refs[groups : 2 * groups]
    scratch = refs[2 * groups :]
    per = [scratch[6 * g : 6 * g + 6] for g in range(groups)]
    barrier = pltpu.get_barrier_semaphore()
    for axis in group_axes:
        me = lax.axis_index(axis)
        for k in range(1, n):
            peer = lax.rem(me + k, n)
            pl.semaphore_signal(barrier, inc=1, device_id=peer_id(axis, peer), device_id_type=MESH)
    pl.semaphore_wait(barrier, groups * (n - 1))

    width = ins[0].shape[1] // n

    def cols(index):
        return pl.ds(pl.multiple_of(index * width, width), width)

    scatter = []
    for g, axis in enumerate(group_axes):
        recv, gathered, s1, r1, s2, r2 = per[g]
        me = lax.axis_index(axis)
        copies = []
        for k in range(1, n):
            peer = lax.rem(me + k, n)
            copy = pltpu.make_async_remote_copy(
                src_ref=ins[g].at[:, cols(peer)],
                dst_ref=recv.at[me],
                send_sem=s1.at[peer],
                recv_sem=r1.at[me],
                device_id=peer_id(axis, peer),
                device_id_type=MESH,
            )
            copy.start()
            copies.append(copy)
        scatter.append(copies)

    gathers = []
    for g, axis in enumerate(group_axes):
        recv, gathered, s1, r1, s2, r2 = per[g]
        me = lax.axis_index(axis)
        for k in range(1, n):
            source = lax.rem(me + n - k, n)
            pltpu.make_async_remote_copy(
                src_ref=ins[g].at[:, cols(source)],
                dst_ref=recv.at[source],
                send_sem=s1.at[source],
                recv_sem=r1.at[source],
                device_id=peer_id(axis, source),
                device_id_type=MESH,
            ).wait_recv()
        total = ins[g][:, cols(me)]
        for k in range(1, n):
            total = total + recv[lax.rem(me + k, n)]
        gathered[me] = total
        copies = []
        for k in range(1, n):
            peer = lax.rem(me + k, n)
            copy = pltpu.make_async_remote_copy(
                src_ref=gathered.at[me],
                dst_ref=gathered.at[me],
                send_sem=s2.at[peer],
                recv_sem=r2.at[me],
                device_id=peer_id(axis, peer),
                device_id_type=MESH,
            )
            copy.start()
            copies.append(copy)
        gathers.append(copies)

    for g, axis in enumerate(group_axes):
        recv, gathered, s1, r1, s2, r2 = per[g]
        me = lax.axis_index(axis)
        for copy in scatter[g]:
            copy.wait_send()
        for k in range(1, n):
            source = lax.rem(me + n - k, n)
            pltpu.make_async_remote_copy(
                src_ref=gathered.at[source],
                dst_ref=gathered.at[source],
                send_sem=s2.at[source],
                recv_sem=r2.at[source],
                device_id=peer_id(axis, source),
                device_id_type=MESH,
            ).wait_recv()
        for copy in gathers[g]:
            copy.wait_send()
        for index in range(n):
            outs[g][:, index * width : (index + 1) * width] = gathered[index]


def all_reduce(arrays, group_axes, n, collective_id):
    shapes = [a.shape for a in arrays]
    width = shapes[0][1] // n
    scratch = []
    for rows, _ in shapes:
        scratch += [
            pltpu.VMEM((n, rows, width), jnp.float32),
            pltpu.VMEM((n, rows, width), jnp.float32),
            pltpu.SemaphoreType.DMA((n,)),
            pltpu.SemaphoreType.DMA((n,)),
            pltpu.SemaphoreType.DMA((n,)),
            pltpu.SemaphoreType.DMA((n,)),
        ]
    return pl.pallas_call(
        functools.partial(reduce_kernel, n, group_axes),
        out_shape=tuple(jax.ShapeDtypeStruct(s, jnp.float32) for s in shapes),
        in_specs=[pl.BlockSpec(memory_space=pltpu.VMEM)] * len(arrays),
        out_specs=tuple(pl.BlockSpec(memory_space=pltpu.VMEM) for _ in arrays),
        scratch_shapes=scratch,
        compiler_params=pltpu.CompilerParams(collective_id=collective_id, has_side_effects=True),
    )(*arrays)


def pick_blocks(full, index, blocks, block_width):
    chosen = full[None, :, :block_width]
    for b in range(1, blocks):
        chosen = jnp.where(
            (index == b)[:, None, None], full[None, :, b * block_width : (b + 1) * block_width], chosen
        )
    return chosen


def by_tile(stacked, matrices, tiles, contract, slots):
    results = [
        lax.dot_general(
            stacked, matrices[t], (((1,), (contract,)), ((), ())),
            preferred_element_type=jnp.float32,
        )
        for t in range(matrices.shape[0])
    ]
    chosen = results[0].reshape(slots, -1, stacked.shape[1])
    for t in range(1, len(results)):
        chosen = jnp.where(
            (tiles == t)[:, None, None], results[t].reshape(slots, -1, stacked.shape[1]), chosen
        )
    return chosen


def live_rows(live_slot, index, blocks, block_width):
    lane_block = lax.broadcasted_iota(jnp.int32, (8, blocks * block_width), 1) // block_width
    first_row = lax.broadcasted_iota(jnp.int32, (8, blocks * block_width), 0) == 0
    total = jnp.zeros((8, blocks * block_width), jnp.float32)
    for k in range(index.shape[0]):
        total = total + jnp.where(first_row & live_slot[k] & (lane_block == index[k]), 1.0, 0.0)
    return total


def per_device(
    tile_matrix,
    tile_inverse,
    block_rows,
    block_cols,
    block_tiles,
    block_count,
    column_values,
    column_duals,
    unit_cost,
    capacity,
    row_values,
    row_duals,
    row_lower,
    row_upper,
    block_image,
    image_dual,
    input_dual,
):
    block_width = tile_matrix.shape[1]
    scenarios = column_values.shape[0]
    col_blocks = column_values.shape[1] // block_width
    row_blocks = row_values.shape[1] // block_width
    slot_total = block_rows.shape[2]
    n_row = lax.axis_size("row")
    rows_here = block_rows[0, 0]
    cols_here = block_cols[0, 0]
    tiles_here = block_tiles[0, 0]
    live_slot = jnp.arange(slot_total, dtype=jnp.int32) < block_count[0, 0]
    x_own = column_values
    x_dual = column_duals
    y_state = row_values
    y_dual = row_duals
    images = block_image[0, 0]
    image_duals = image_dual[0, 0]
    input_duals = input_dual[0, 0]
    col_mask = [(live_slot & (cols_here == b))[:, None, None] for b in range(col_blocks)]
    row_mask = [(live_slot & (rows_here == b))[:, None, None] for b in range(row_blocks)]
    col_denom = None
    row_denom = None
    for iteration in range(ITERS):
        x_half = jnp.clip(x_own - x_dual - unit_cost, 0.0, capacity)
        y_half = jnp.clip(y_state - y_dual, row_lower, row_upper)
        y_anchor = y_half + y_dual
        image_gap = (images - image_duals).astype(jnp.bfloat16).reshape(-1, block_width)
        pulled = by_tile(image_gap, tile_matrix, tiles_here, 1, slot_total)
        x_columns = pick_blocks(x_own, cols_here, col_blocks, block_width)
        merged = (x_columns - input_duals + pulled).astype(jnp.bfloat16).reshape(-1, block_width)
        x_proj = by_tile(merged, tile_inverse, tiles_here, 0, slot_total)
        y_proj = by_tile(
            x_proj.astype(jnp.bfloat16).reshape(-1, block_width), tile_matrix, tiles_here, 0,
            slot_total,
        )
        x_terms = x_proj + input_duals
        y_terms = y_proj + image_duals
        col_terms = jnp.concatenate(
            [jnp.sum(jnp.where(m, x_terms, 0.0), axis=0) for m in col_mask], axis=1
        )
        row_terms = jnp.concatenate(
            [jnp.sum(jnp.where(m, y_terms, 0.0), axis=0) for m in row_mask], axis=1
        )
        if iteration == 0:
            col_extra = live_rows(live_slot, cols_here, col_blocks, block_width)
            row_extra = live_rows(live_slot, rows_here, row_blocks, block_width)
            col_total, row_total = all_reduce(
                [
                    jnp.concatenate([col_terms, col_extra], axis=0),
                    jnp.concatenate([row_terms, row_extra], axis=0),
                ],
                AXES,
                n_row,
                0,
            )
            col_denom = 1.0 + col_total[scenarios : scenarios + 1]
            row_denom = 1.0 + row_total[scenarios : scenarios + 1]
            col_total = col_total[:scenarios]
            row_total = row_total[:scenarios]
        else:
            col_total, row_total = all_reduce([col_terms, row_terms], AXES, n_row, 1)
        x_own = (x_half + x_dual + col_total) / col_denom
        x_dual = x_dual + x_half - x_own
        shift_full = (row_total - y_anchor) / row_denom
        y_state = y_anchor + shift_full
        y_dual = y_dual + y_half - y_state
        input_duals = input_duals + x_proj - pick_blocks(x_own, cols_here, col_blocks, block_width)
        new_images = y_proj + image_duals - pick_blocks(shift_full, rows_here, row_blocks, block_width)
        image_duals = image_duals + y_proj - new_images
        images = new_images
    column_final = jnp.clip(x_own - x_dual - unit_cost, 0.0, capacity)
    row_final = jnp.clip(y_state - y_dual, row_lower, row_upper)
    return (column_final, row_final)


def solution(mesh):
    placed = (
        P(),
        P(),
        P("row", "col", None),
        P("row", "col", None),
        P("row", "col", None),
        P("row", "col"),
        P(None, "col"),
        P(None, "col"),
        P(None, "col"),
        P(None, "col"),
        P(None, "row"),
        P(None, "row"),
        P(None, "row"),
        P(None, "row"),
        P("row", "col", None, None, None),
        P("row", "col", None, None, None),
        P("row", "col", None, None, None),
    )
    return jax.shard_map(
        per_device,
        mesh=mesh,
        in_specs=placed,
        out_specs=(P(None, "col"), P(None, "row")),
        check_vma=False,
    )
```

```python
import functools

import jax
import jax.numpy as jnp
from jax import lax
from jax.experimental import pallas as pl
from jax.experimental.pallas import tpu as pltpu
from jax.sharding import PartitionSpec as P

ITERS = 2
MESH = pl.DeviceIdType.MESH
AXES = ("row", "col")


def peer_id(axis, peer):
    if axis == "row":
        return (peer, lax.axis_index("col"))
    return (lax.axis_index("row"), peer)


def reduce_kernel(n, group_axes, *refs):
    groups = len(group_axes)
    ins = refs[:groups]
    outs = refs[groups : 2 * groups]
    scratch = refs[2 * groups :]
    per = [scratch[6 * g : 6 * g + 6] for g in range(groups)]
    barrier = pltpu.get_barrier_semaphore()
    for axis in group_axes:
        me = lax.axis_index(axis)
        for k in range(1, n):
            peer = lax.rem(me + k, n)
            pl.semaphore_signal(barrier, inc=1, device_id=peer_id(axis, peer), device_id_type=MESH)
    pl.semaphore_wait(barrier, groups * (n - 1))

    width = ins[0].shape[2]

    def cols(index):
        return pl.ds(pl.multiple_of(index * width, width), width)

    scatter = []
    for g, axis in enumerate(group_axes):
        recv, gathered, s1, r1, s2, r2 = per[g]
        me = lax.axis_index(axis)
        copies = []
        for k in range(1, n):
            peer = lax.rem(me + k, n)
            copy = pltpu.make_async_remote_copy(
                src_ref=ins[g].at[peer],
                dst_ref=recv.at[me],
                send_sem=s1.at[peer],
                recv_sem=r1.at[me],
                device_id=peer_id(axis, peer),
                device_id_type=MESH,
            )
            copy.start()
            copies.append(copy)
        scatter.append(copies)

    gathers = []
    for g, axis in enumerate(group_axes):
        recv, gathered, s1, r1, s2, r2 = per[g]
        me = lax.axis_index(axis)
        for k in range(1, n):
            source = lax.rem(me + n - k, n)
            pltpu.make_async_remote_copy(
                src_ref=ins[g].at[source],
                dst_ref=recv.at[source],
                send_sem=s1.at[source],
                recv_sem=r1.at[source],
                device_id=peer_id(axis, source),
                device_id_type=MESH,
            ).wait_recv()
        total = ins[g][me]
        for k in range(1, n):
            total = total + recv[lax.rem(me + k, n)]
        gathered[me] = total
        copies = []
        for k in range(1, n):
            peer = lax.rem(me + k, n)
            copy = pltpu.make_async_remote_copy(
                src_ref=gathered.at[me],
                dst_ref=gathered.at[me],
                send_sem=s2.at[peer],
                recv_sem=r2.at[me],
                device_id=peer_id(axis, peer),
                device_id_type=MESH,
            )
            copy.start()
            copies.append(copy)
        gathers.append(copies)

    for g, axis in enumerate(group_axes):
        recv, gathered, s1, r1, s2, r2 = per[g]
        me = lax.axis_index(axis)
        for copy in scatter[g]:
            copy.wait_send()
        for k in range(1, n):
            source = lax.rem(me + n - k, n)
            pltpu.make_async_remote_copy(
                src_ref=gathered.at[source],
                dst_ref=gathered.at[source],
                send_sem=s2.at[source],
                recv_sem=r2.at[source],
                device_id=peer_id(axis, source),
                device_id_type=MESH,
            ).wait_recv()
        for copy in gathers[g]:
            copy.wait_send()
        for index in range(n):
            outs[g][:, index * width : (index + 1) * width] = gathered[index]


def all_reduce(arrays, group_axes, n, collective_id):
    shapes = [a.shape for a in arrays]
    width = shapes[0][1] // n
    arrays = [a.reshape(a.shape[0], n, width).transpose(1, 0, 2) for a in arrays]
    scratch = []
    for rows, _ in shapes:
        scratch += [
            pltpu.VMEM((n, rows, width), jnp.float32),
            pltpu.VMEM((n, rows, width), jnp.float32),
            pltpu.SemaphoreType.DMA((n,)),
            pltpu.SemaphoreType.DMA((n,)),
            pltpu.SemaphoreType.DMA((n,)),
            pltpu.SemaphoreType.DMA((n,)),
        ]
    return pl.pallas_call(
        functools.partial(reduce_kernel, n, group_axes),
        out_shape=tuple(jax.ShapeDtypeStruct(s, jnp.float32) for s in shapes),
        in_specs=[pl.BlockSpec(memory_space=pltpu.VMEM)] * len(arrays),
        out_specs=tuple(pl.BlockSpec(memory_space=pltpu.VMEM) for _ in arrays),
        scratch_shapes=scratch,
        compiler_params=pltpu.CompilerParams(collective_id=collective_id, has_side_effects=True),
    )(*arrays)


def pick_blocks(full, index, blocks, block_width):
    chosen = full[None, :, :block_width]
    for b in range(1, blocks):
        chosen = jnp.where(
            (index == b)[:, None, None], full[None, :, b * block_width : (b + 1) * block_width], chosen
        )
    return chosen


def by_tile(stacked, matrices, tiles, contract, slots):
    results = [
        lax.dot_general(
            stacked, matrices[t], (((1,), (contract,)), ((), ())),
            preferred_element_type=jnp.float32,
        )
        for t in range(matrices.shape[0])
    ]
    chosen = results[0].reshape(slots, -1, stacked.shape[1])
    for t in range(1, len(results)):
        chosen = jnp.where(
            (tiles == t)[:, None, None], results[t].reshape(slots, -1, stacked.shape[1]), chosen
        )
    return chosen


def live_rows(live_slot, index, blocks, block_width):
    lane_block = lax.broadcasted_iota(jnp.int32, (8, blocks * block_width), 1) // block_width
    first_row = lax.broadcasted_iota(jnp.int32, (8, blocks * block_width), 0) == 0
    total = jnp.zeros((8, blocks * block_width), jnp.float32)
    for k in range(index.shape[0]):
        total = total + jnp.where(first_row & live_slot[k] & (lane_block == index[k]), 1.0, 0.0)
    return total


def per_device(
    tile_matrix,
    tile_inverse,
    block_rows,
    block_cols,
    block_tiles,
    block_count,
    column_values,
    column_duals,
    unit_cost,
    capacity,
    row_values,
    row_duals,
    row_lower,
    row_upper,
    block_image,
    image_dual,
    input_dual,
):
    block_width = tile_matrix.shape[1]
    scenarios = column_values.shape[0]
    col_blocks = column_values.shape[1] // block_width
    row_blocks = row_values.shape[1] // block_width
    slot_total = block_rows.shape[2]
    n_row = lax.axis_size("row")
    rows_here = block_rows[0, 0]
    cols_here = block_cols[0, 0]
    tiles_here = block_tiles[0, 0]
    live_slot = jnp.arange(slot_total, dtype=jnp.int32) < block_count[0, 0]
    x_own = column_values
    x_dual = column_duals
    y_state = row_values
    y_dual = row_duals
    images = block_image[0, 0]
    image_duals = image_dual[0, 0]
    input_duals = input_dual[0, 0]
    col_mask = [(live_slot & (cols_here == b))[:, None, None] for b in range(col_blocks)]
    row_mask = [(live_slot & (rows_here == b))[:, None, None] for b in range(row_blocks)]
    col_denom = None
    row_denom = None
    for iteration in range(ITERS):
        x_half = jnp.clip(x_own - x_dual - unit_cost, 0.0, capacity)
        y_half = jnp.clip(y_state - y_dual, row_lower, row_upper)
        y_anchor = y_half + y_dual
        image_gap = (images - image_duals).astype(jnp.bfloat16).reshape(-1, block_width)
        pulled = by_tile(image_gap, tile_matrix, tiles_here, 1, slot_total)
        x_columns = pick_blocks(x_own, cols_here, col_blocks, block_width)
        merged = (x_columns - input_duals + pulled).astype(jnp.bfloat16).reshape(-1, block_width)
        x_proj = by_tile(merged, tile_inverse, tiles_here, 0, slot_total)
        y_proj = by_tile(
            x_proj.astype(jnp.bfloat16).reshape(-1, block_width), tile_matrix, tiles_here, 0,
            slot_total,
        )
        x_terms = x_proj + input_duals
        y_terms = y_proj + image_duals
        col_terms = jnp.concatenate(
            [jnp.sum(jnp.where(m, x_terms, 0.0), axis=0) for m in col_mask], axis=1
        )
        row_terms = jnp.concatenate(
            [jnp.sum(jnp.where(m, y_terms, 0.0), axis=0) for m in row_mask], axis=1
        )
        if iteration == 0:
            col_extra = live_rows(live_slot, cols_here, col_blocks, block_width)
            row_extra = live_rows(live_slot, rows_here, row_blocks, block_width)
            col_total, row_total = all_reduce(
                [
                    jnp.concatenate([col_terms, col_extra], axis=0),
                    jnp.concatenate([row_terms, row_extra], axis=0),
                ],
                AXES,
                n_row,
                0,
            )
            col_denom = 1.0 + col_total[scenarios : scenarios + 1]
            row_denom = 1.0 + row_total[scenarios : scenarios + 1]
            col_total = col_total[:scenarios]
            row_total = row_total[:scenarios]
        else:
            col_total, row_total = all_reduce([col_terms, row_terms], AXES, n_row, 1)
        x_own = (x_half + x_dual + col_total) / col_denom
        x_dual = x_dual + x_half - x_own
        shift_full = (row_total - y_anchor) / row_denom
        y_state = y_anchor + shift_full
        y_dual = y_dual + y_half - y_state
        input_duals = input_duals + x_proj - pick_blocks(x_own, cols_here, col_blocks, block_width)
        new_images = y_proj + image_duals - pick_blocks(shift_full, rows_here, row_blocks, block_width)
        image_duals = image_duals + y_proj - new_images
        images = new_images
    column_final = jnp.clip(x_own - x_dual - unit_cost, 0.0, capacity)
    row_final = jnp.clip(y_state - y_dual, row_lower, row_upper)
    return (column_final, row_final)


def solution(mesh):
    placed = (
        P(),
        P(),
        P("row", "col", None),
        P("row", "col", None),
        P("row", "col", None),
        P("row", "col"),
        P(None, "col"),
        P(None, "col"),
        P(None, "col"),
        P(None, "col"),
        P(None, "row"),
        P(None, "row"),
        P(None, "row"),
        P(None, "row"),
        P("row", "col", None, None, None),
        P("row", "col", None, None, None),
        P("row", "col", None, None, None),
    )
    return jax.shard_map(
        per_device,
        mesh=mesh,
        in_specs=placed,
        out_specs=(P(None, "col"), P(None, "row")),
        check_vma=False,
    )
```

```python
import functools

import jax
import jax.numpy as jnp
from jax import lax
from jax.experimental import pallas as pl
from jax.experimental.pallas import tpu as pltpu
from jax.sharding import PartitionSpec as P

ITERS = 2
MESH = pl.DeviceIdType.MESH
AXES = ("row", "col")


def peer_id(axis, peer):
    if axis == "row":
        return (peer, lax.axis_index("col"))
    return (lax.axis_index("row"), peer)


def reduce_kernel(n, group_axes, block_width, with_counts, *refs):
    groups = len(group_axes)
    if with_counts:
        info, refs = refs[0], refs[1:]
    ins = refs[:groups]
    outs = refs[groups : 2 * groups]
    scratch = refs[2 * groups :]
    size = 7 if with_counts else 6
    per = [scratch[size * g : size * g + 6] for g in range(groups)]
    width = ins[0].shape[2]
    sources = list(ins)
    if with_counts:
        slots = (info.shape[0] - 1) // groups
        live = info[groups * slots]
        for g in range(groups):
            send = scratch[size * g + 6]
            data_rows = ins[g].shape[1]
            extra = send.shape[1] - data_rows
            for p in range(n):
                block = (p * width) // block_width
                count = jnp.int32(0)
                for k in range(slots):
                    count = count + jnp.where(
                        (k < live) & (info[g * slots + k] == block), 1, 0
                    ).astype(jnp.int32)
                send[p, :data_rows, :] = ins[g][p]
                send[p, data_rows:, :] = jnp.full((extra, width), count, jnp.int32).astype(
                    jnp.float32
                )
            sources[g] = send
    barrier = pltpu.get_barrier_semaphore()
    for axis in group_axes:
        me = lax.axis_index(axis)
        for k in range(1, n):
            peer = lax.rem(me + k, n)
            pl.semaphore_signal(barrier, inc=1, device_id=peer_id(axis, peer), device_id_type=MESH)
    pl.semaphore_wait(barrier, groups * (n - 1))

    scatter = []
    for g, axis in enumerate(group_axes):
        recv, gathered, s1, r1, s2, r2 = per[g]
        me = lax.axis_index(axis)
        copies = []
        for k in range(1, n):
            peer = lax.rem(me + k, n)
            copy = pltpu.make_async_remote_copy(
                src_ref=sources[g].at[peer],
                dst_ref=recv.at[me],
                send_sem=s1.at[peer],
                recv_sem=r1.at[me],
                device_id=peer_id(axis, peer),
                device_id_type=MESH,
            )
            copy.start()
            copies.append(copy)
        scatter.append(copies)

    gathers = []
    for g, axis in enumerate(group_axes):
        recv, gathered, s1, r1, s2, r2 = per[g]
        me = lax.axis_index(axis)
        for k in range(1, n):
            source = lax.rem(me + n - k, n)
            pltpu.make_async_remote_copy(
                src_ref=sources[g].at[source],
                dst_ref=recv.at[source],
                send_sem=s1.at[source],
                recv_sem=r1.at[source],
                device_id=peer_id(axis, source),
                device_id_type=MESH,
            ).wait_recv()
        total = sources[g][me]
        for k in range(1, n):
            total = total + recv[lax.rem(me + k, n)]
        gathered[me] = total
        copies = []
        for k in range(1, n):
            peer = lax.rem(me + k, n)
            copy = pltpu.make_async_remote_copy(
                src_ref=gathered.at[me],
                dst_ref=gathered.at[me],
                send_sem=s2.at[peer],
                recv_sem=r2.at[me],
                device_id=peer_id(axis, peer),
                device_id_type=MESH,
            )
            copy.start()
            copies.append(copy)
        gathers.append(copies)

    for g, axis in enumerate(group_axes):
        recv, gathered, s1, r1, s2, r2 = per[g]
        me = lax.axis_index(axis)
        for copy in scatter[g]:
            copy.wait_send()
        for k in range(1, n):
            source = lax.rem(me + n - k, n)
            pltpu.make_async_remote_copy(
                src_ref=gathered.at[source],
                dst_ref=gathered.at[source],
                send_sem=s2.at[source],
                recv_sem=r2.at[source],
                device_id=peer_id(axis, source),
                device_id_type=MESH,
            ).wait_recv()
        for copy in gathers[g]:
            copy.wait_send()
        for index in range(n):
            outs[g][:, index * width : (index + 1) * width] = gathered[index]


def all_reduce(arrays, group_axes, n, collective_id, block_width, info=None):
    extra = 0 if info is None else 8
    shapes = [(a.shape[0] + extra, a.shape[1]) for a in arrays]
    width = shapes[0][1] // n
    arrays = [a.reshape(a.shape[0], n, width).transpose(1, 0, 2) for a in arrays]
    scratch = []
    for rows, _ in shapes:
        scratch += [
            pltpu.VMEM((n, rows, width), jnp.float32),
            pltpu.VMEM((n, rows, width), jnp.float32),
            pltpu.SemaphoreType.DMA((n,)),
            pltpu.SemaphoreType.DMA((n,)),
            pltpu.SemaphoreType.DMA((n,)),
            pltpu.SemaphoreType.DMA((n,)),
        ]
        if info is not None:
            scratch.append(pltpu.VMEM((n, rows, width), jnp.float32))
    in_specs = [pl.BlockSpec(memory_space=pltpu.VMEM)] * len(arrays)
    if info is not None:
        in_specs = [pl.BlockSpec(memory_space=pltpu.SMEM)] + in_specs
        arrays = [info] + arrays
    return pl.pallas_call(
        functools.partial(reduce_kernel, n, group_axes, block_width, info is not None),
        out_shape=tuple(jax.ShapeDtypeStruct(s, jnp.float32) for s in shapes),
        in_specs=in_specs,
        out_specs=tuple(pl.BlockSpec(memory_space=pltpu.VMEM) for _ in shapes),
        scratch_shapes=scratch,
        compiler_params=pltpu.CompilerParams(collective_id=collective_id, has_side_effects=True),
    )(*arrays)


def pick_blocks(full, index, blocks, block_width):
    chosen = full[None, :, :block_width]
    for b in range(1, blocks):
        chosen = jnp.where(
            (index == b)[:, None, None], full[None, :, b * block_width : (b + 1) * block_width], chosen
        )
    return chosen


def by_tile(stacked, matrices, tiles, contract, slots):
    results = [
        lax.dot_general(
            stacked, matrices[t], (((1,), (contract,)), ((), ())),
            preferred_element_type=jnp.float32,
        )
        for t in range(matrices.shape[0])
    ]
    chosen = results[0].reshape(slots, -1, stacked.shape[1])
    for t in range(1, len(results)):
        chosen = jnp.where(
            (tiles == t)[:, None, None], results[t].reshape(slots, -1, stacked.shape[1]), chosen
        )
    return chosen


def per_device(
    tile_matrix,
    tile_inverse,
    block_rows,
    block_cols,
    block_tiles,
    block_count,
    column_values,
    column_duals,
    unit_cost,
    capacity,
    row_values,
    row_duals,
    row_lower,
    row_upper,
    block_image,
    image_dual,
    input_dual,
):
    block_width = tile_matrix.shape[1]
    scenarios = column_values.shape[0]
    col_blocks = column_values.shape[1] // block_width
    row_blocks = row_values.shape[1] // block_width
    slot_total = block_rows.shape[2]
    n_row = lax.axis_size("row")
    rows_here = block_rows[0, 0]
    cols_here = block_cols[0, 0]
    tiles_here = block_tiles[0, 0]
    live_slot = jnp.arange(slot_total, dtype=jnp.int32) < block_count[0, 0]
    x_own = column_values
    x_dual = column_duals
    y_state = row_values
    y_dual = row_duals
    images = block_image[0, 0]
    image_duals = image_dual[0, 0]
    input_duals = input_dual[0, 0]
    col_mask = [(live_slot & (cols_here == b))[:, None, None] for b in range(col_blocks)]
    row_mask = [(live_slot & (rows_here == b))[:, None, None] for b in range(row_blocks)]
    col_denom = None
    row_denom = None
    for iteration in range(ITERS):
        x_half = jnp.clip(x_own - x_dual - unit_cost, 0.0, capacity)
        y_half = jnp.clip(y_state - y_dual, row_lower, row_upper)
        y_anchor = y_half + y_dual
        image_gap = (images - image_duals).astype(jnp.bfloat16).reshape(-1, block_width)
        pulled = by_tile(image_gap, tile_matrix, tiles_here, 1, slot_total)
        x_columns = pick_blocks(x_own, cols_here, col_blocks, block_width)
        merged = (x_columns - input_duals + pulled).astype(jnp.bfloat16).reshape(-1, block_width)
        x_proj = by_tile(merged, tile_inverse, tiles_here, 0, slot_total)
        y_proj = by_tile(
            x_proj.astype(jnp.bfloat16).reshape(-1, block_width), tile_matrix, tiles_here, 0,
            slot_total,
        )
        x_terms = x_proj + input_duals
        y_terms = y_proj + image_duals
        col_terms = jnp.concatenate(
            [jnp.sum(jnp.where(m, x_terms, 0.0), axis=0) for m in col_mask], axis=1
        )
        row_terms = jnp.concatenate(
            [jnp.sum(jnp.where(m, y_terms, 0.0), axis=0) for m in row_mask], axis=1
        )
        if iteration == 0:
            slot_info = jnp.concatenate([cols_here, rows_here, block_count[0, 0][None]])
            col_total, row_total = all_reduce(
                [col_terms, row_terms], AXES, n_row, 0, block_width, slot_info
            )
            col_denom = 1.0 + col_total[scenarios : scenarios + 1]
            row_denom = 1.0 + row_total[scenarios : scenarios + 1]
            col_total = col_total[:scenarios]
            row_total = row_total[:scenarios]
        else:
            col_total, row_total = all_reduce([col_terms, row_terms], AXES, n_row, 1, block_width)
        x_own = (x_half + x_dual + col_total) / col_denom
        x_dual = x_dual + x_half - x_own
        shift_full = (row_total - y_anchor) / row_denom
        y_state = y_anchor + shift_full
        y_dual = y_dual + y_half - y_state
        input_duals = input_duals + x_proj - pick_blocks(x_own, cols_here, col_blocks, block_width)
        new_images = y_proj + image_duals - pick_blocks(shift_full, rows_here, row_blocks, block_width)
        image_duals = image_duals + y_proj - new_images
        images = new_images
    column_final = jnp.clip(x_own - x_dual - unit_cost, 0.0, capacity)
    row_final = jnp.clip(y_state - y_dual, row_lower, row_upper)
    return (column_final, row_final)


def solution(mesh):
    placed = (
        P(),
        P(),
        P("row", "col", None),
        P("row", "col", None),
        P("row", "col", None),
        P("row", "col"),
        P(None, "col"),
        P(None, "col"),
        P(None, "col"),
        P(None, "col"),
        P(None, "row"),
        P(None, "row"),
        P(None, "row"),
        P(None, "row"),
        P("row", "col", None, None, None),
        P("row", "col", None, None, None),
        P("row", "col", None, None, None),
    )
    return jax.shard_map(
        per_device,
        mesh=mesh,
        in_specs=placed,
        out_specs=(P(None, "col"), P(None, "row")),
        check_vma=False,
    )
```

```python
import functools

import jax
import jax.numpy as jnp
from jax import lax
from jax.experimental import pallas as pl
from jax.experimental.pallas import tpu as pltpu
from jax.sharding import PartitionSpec as P

ITERS = 2
MESH = pl.DeviceIdType.MESH
AXES = ("row", "col")


def peer_id(axis, peer):
    if axis == "row":
        return (peer, lax.axis_index("col"))
    return (lax.axis_index("row"), peer)


def reduce_kernel(n, group_axes, block_width, with_counts, *refs):
    groups = len(group_axes)
    if with_counts:
        info, refs = refs[0], refs[1:]
    ins = refs[:groups]
    outs = refs[groups : 2 * groups]
    scratch = refs[2 * groups :]
    size = 7 if with_counts else 6
    per = [scratch[size * g : size * g + 6] for g in range(groups)]
    width = ins[0].shape[1] // n
    sources = list(ins)

    def cols(index):
        return pl.ds(pl.multiple_of(index * width, width), width)

    def piece(ref, index):
        if len(ref.shape) == 3:
            return ref.at[index]
        return ref.at[:, cols(index)]

    if with_counts:
        slots = (info.shape[0] - 1) // groups
        live = info[groups * slots]
        for g in range(groups):
            send = scratch[size * g + 6]
            data_rows = ins[g].shape[0]
            extra = send.shape[1] - data_rows
            for p in range(n):
                block = (p * width) // block_width
                count = jnp.int32(0)
                for k in range(slots):
                    count = count + jnp.where(
                        (k < live) & (info[g * slots + k] == block), 1, 0
                    ).astype(jnp.int32)
                send[p, :data_rows, :] = ins[g][:, p * width : (p + 1) * width]
                send[p, data_rows:, :] = jnp.full((extra, width), count, jnp.int32).astype(
                    jnp.float32
                )
            sources[g] = send
    barrier = pltpu.get_barrier_semaphore()
    for axis in group_axes:
        me = lax.axis_index(axis)
        for k in range(1, n):
            peer = lax.rem(me + k, n)
            pl.semaphore_signal(barrier, inc=1, device_id=peer_id(axis, peer), device_id_type=MESH)
    pl.semaphore_wait(barrier, groups * (n - 1))

    scatter = []
    for g, axis in enumerate(group_axes):
        recv, gathered, s1, r1, s2, r2 = per[g]
        me = lax.axis_index(axis)
        copies = []
        for k in range(1, n):
            peer = lax.rem(me + k, n)
            copy = pltpu.make_async_remote_copy(
                src_ref=piece(sources[g], peer),
                dst_ref=recv.at[me],
                send_sem=s1.at[peer],
                recv_sem=r1.at[me],
                device_id=peer_id(axis, peer),
                device_id_type=MESH,
            )
            copy.start()
            copies.append(copy)
        scatter.append(copies)

    gathers = []
    for g, axis in enumerate(group_axes):
        recv, gathered, s1, r1, s2, r2 = per[g]
        me = lax.axis_index(axis)
        for k in range(1, n):
            source = lax.rem(me + n - k, n)
            pltpu.make_async_remote_copy(
                src_ref=piece(sources[g], source),
                dst_ref=recv.at[source],
                send_sem=s1.at[source],
                recv_sem=r1.at[source],
                device_id=peer_id(axis, source),
                device_id_type=MESH,
            ).wait_recv()
        total = piece(sources[g], me)[...]
        for k in range(1, n):
            total = total + recv[lax.rem(me + k, n)]
        gathered[me] = total
        copies = []
        for k in range(1, n):
            peer = lax.rem(me + k, n)
            copy = pltpu.make_async_remote_copy(
                src_ref=gathered.at[me],
                dst_ref=gathered.at[me],
                send_sem=s2.at[peer],
                recv_sem=r2.at[me],
                device_id=peer_id(axis, peer),
                device_id_type=MESH,
            )
            copy.start()
            copies.append(copy)
        gathers.append(copies)

    for g, axis in enumerate(group_axes):
        recv, gathered, s1, r1, s2, r2 = per[g]
        me = lax.axis_index(axis)
        for copy in scatter[g]:
            copy.wait_send()
        for k in range(1, n):
            source = lax.rem(me + n - k, n)
            pltpu.make_async_remote_copy(
                src_ref=gathered.at[source],
                dst_ref=gathered.at[source],
                send_sem=s2.at[source],
                recv_sem=r2.at[source],
                device_id=peer_id(axis, source),
                device_id_type=MESH,
            ).wait_recv()
        for copy in gathers[g]:
            copy.wait_send()
        for index in range(n):
            outs[g][:, index * width : (index + 1) * width] = gathered[index]


def all_reduce(arrays, group_axes, n, collective_id, block_width, info=None):
    extra = 0 if info is None else 8
    shapes = [(a.shape[0] + extra, a.shape[1]) for a in arrays]
    width = shapes[0][1] // n
    scratch = []
    for rows, _ in shapes:
        scratch += [
            pltpu.VMEM((n, rows, width), jnp.float32),
            pltpu.VMEM((n, rows, width), jnp.float32),
            pltpu.SemaphoreType.DMA((n,)),
            pltpu.SemaphoreType.DMA((n,)),
            pltpu.SemaphoreType.DMA((n,)),
            pltpu.SemaphoreType.DMA((n,)),
        ]
        if info is not None:
            scratch.append(pltpu.VMEM((n, rows, width), jnp.float32))
    in_specs = [pl.BlockSpec(memory_space=pltpu.VMEM)] * len(arrays)
    if info is not None:
        in_specs = [pl.BlockSpec(memory_space=pltpu.SMEM)] + in_specs
        arrays = [info] + arrays
    return pl.pallas_call(
        functools.partial(reduce_kernel, n, group_axes, block_width, info is not None),
        out_shape=tuple(jax.ShapeDtypeStruct(s, jnp.float32) for s in shapes),
        in_specs=in_specs,
        out_specs=tuple(pl.BlockSpec(memory_space=pltpu.VMEM) for _ in shapes),
        scratch_shapes=scratch,
        compiler_params=pltpu.CompilerParams(collective_id=collective_id, has_side_effects=True),
    )(*arrays)


def pick_blocks(full, index, blocks, block_width):
    chosen = full[None, :, :block_width]
    for b in range(1, blocks):
        chosen = jnp.where(
            (index == b)[:, None, None], full[None, :, b * block_width : (b + 1) * block_width], chosen
        )
    return chosen


def by_tile(stacked, matrices, tiles, contract, slots):
    results = [
        lax.dot_general(
            stacked, matrices[t], (((1,), (contract,)), ((), ())),
            preferred_element_type=jnp.float32,
        )
        for t in range(matrices.shape[0])
    ]
    chosen = results[0].reshape(slots, -1, stacked.shape[1])
    for t in range(1, len(results)):
        chosen = jnp.where(
            (tiles == t)[:, None, None], results[t].reshape(slots, -1, stacked.shape[1]), chosen
        )
    return chosen


def per_device(
    tile_matrix,
    tile_inverse,
    block_rows,
    block_cols,
    block_tiles,
    block_count,
    column_values,
    column_duals,
    unit_cost,
    capacity,
    row_values,
    row_duals,
    row_lower,
    row_upper,
    block_image,
    image_dual,
    input_dual,
):
    block_width = tile_matrix.shape[1]
    scenarios = column_values.shape[0]
    col_blocks = column_values.shape[1] // block_width
    row_blocks = row_values.shape[1] // block_width
    slot_total = block_rows.shape[2]
    n_row = lax.axis_size("row")
    rows_here = block_rows[0, 0]
    cols_here = block_cols[0, 0]
    tiles_here = block_tiles[0, 0]
    live_slot = jnp.arange(slot_total, dtype=jnp.int32) < block_count[0, 0]
    x_own = column_values
    x_dual = column_duals
    y_state = row_values
    y_dual = row_duals
    images = block_image[0, 0]
    image_duals = image_dual[0, 0]
    input_duals = input_dual[0, 0]
    col_mask = [(live_slot & (cols_here == b))[:, None, None] for b in range(col_blocks)]
    row_mask = [(live_slot & (rows_here == b))[:, None, None] for b in range(row_blocks)]
    col_denom = None
    row_denom = None
    for iteration in range(ITERS):
        x_half = jnp.clip(x_own - x_dual - unit_cost, 0.0, capacity)
        y_half = jnp.clip(y_state - y_dual, row_lower, row_upper)
        y_anchor = y_half + y_dual
        image_gap = (images - image_duals).astype(jnp.bfloat16).reshape(-1, block_width)
        pulled = by_tile(image_gap, tile_matrix, tiles_here, 1, slot_total)
        x_columns = pick_blocks(x_own, cols_here, col_blocks, block_width)
        merged = (x_columns - input_duals + pulled).astype(jnp.bfloat16).reshape(-1, block_width)
        x_proj = by_tile(merged, tile_inverse, tiles_here, 0, slot_total)
        y_proj = by_tile(
            x_proj.astype(jnp.bfloat16).reshape(-1, block_width), tile_matrix, tiles_here, 0,
            slot_total,
        )
        x_terms = x_proj + input_duals
        y_terms = y_proj + image_duals
        col_terms = jnp.concatenate(
            [jnp.sum(jnp.where(m, x_terms, 0.0), axis=0) for m in col_mask], axis=1
        )
        row_terms = jnp.concatenate(
            [jnp.sum(jnp.where(m, y_terms, 0.0), axis=0) for m in row_mask], axis=1
        )
        if iteration == 0:
            slot_info = jnp.concatenate([cols_here, rows_here, block_count[0, 0][None]])
            col_total, row_total = all_reduce(
                [col_terms, row_terms], AXES, n_row, 0, block_width, slot_info
            )
            col_denom = 1.0 + col_total[scenarios : scenarios + 1]
            row_denom = 1.0 + row_total[scenarios : scenarios + 1]
            col_total = col_total[:scenarios]
            row_total = row_total[:scenarios]
        else:
            col_total, row_total = all_reduce([col_terms, row_terms], AXES, n_row, 1, block_width)
        x_own = (x_half + x_dual + col_total) / col_denom
        x_dual = x_dual + x_half - x_own
        shift_full = (row_total - y_anchor) / row_denom
        y_state = y_anchor + shift_full
        y_dual = y_dual + y_half - y_state
        input_duals = input_duals + x_proj - pick_blocks(x_own, cols_here, col_blocks, block_width)
        new_images = y_proj + image_duals - pick_blocks(shift_full, rows_here, row_blocks, block_width)
        image_duals = image_duals + y_proj - new_images
        images = new_images
    column_final = jnp.clip(x_own - x_dual - unit_cost, 0.0, capacity)
    row_final = jnp.clip(y_state - y_dual, row_lower, row_upper)
    return (column_final, row_final)


def solution(mesh):
    placed = (
        P(),
        P(),
        P("row", "col", None),
        P("row", "col", None),
        P("row", "col", None),
        P("row", "col"),
        P(None, "col"),
        P(None, "col"),
        P(None, "col"),
        P(None, "col"),
        P(None, "row"),
        P(None, "row"),
        P(None, "row"),
        P(None, "row"),
        P("row", "col", None, None, None),
        P("row", "col", None, None, None),
        P("row", "col", None, None, None),
    )
    return jax.shard_map(
        per_device,
        mesh=mesh,
        in_specs=placed,
        out_specs=(P(None, "col"), P(None, "row")),
        check_vma=False,
    )
```

```python
import functools

import jax
import jax.numpy as jnp
from jax import lax
from jax.experimental import pallas as pl
from jax.experimental.pallas import tpu as pltpu
from jax.sharding import PartitionSpec as P

ITERS = 2
MESH = pl.DeviceIdType.MESH
AXES = ("row", "col")


def peer_id(axis, peer):
    if axis == "row":
        return (peer, lax.axis_index("col"))
    return (lax.axis_index("row"), peer)


def reduce_kernel(n, group_axes, block_width, with_counts, *refs):
    groups = len(group_axes)
    if with_counts:
        info, refs = refs[0], refs[1:]
    ins = refs[:groups]
    outs = refs[groups : 2 * groups]
    scratch = refs[2 * groups :]
    size = 7 if with_counts else 6
    per = [scratch[size * g : size * g + 6] for g in range(groups)]
    width = ins[0].shape[1] // n
    sources = list(ins)

    def cols(index):
        return pl.ds(pl.multiple_of(index * width, width), width)

    def piece(ref, index):
        if len(ref.shape) == 3:
            return ref.at[index]
        return ref.at[:, cols(index)]

    if with_counts:
        slots = (info.shape[0] - 1) // groups
        live = info[groups * slots]
        for g in range(groups):
            send = scratch[size * g + 6]
            data_rows = ins[g].shape[0]
            extra = send.shape[1] - data_rows
            for p in range(n):
                block = (p * width) // block_width
                count = jnp.int32(0)
                for k in range(slots):
                    count = count + jnp.where(
                        (k < live) & (info[g * slots + k] == block), 1, 0
                    ).astype(jnp.int32)
                send[p, :data_rows, :] = ins[g][:, p * width : (p + 1) * width]
                send[p, data_rows:, :] = jnp.full((extra, width), count, jnp.int32).astype(
                    jnp.float32
                )
            sources[g] = send
    barrier = pltpu.get_barrier_semaphore()
    for axis in group_axes:
        me = lax.axis_index(axis)
        for k in range(1, n):
            peer = lax.rem(me + k, n)
            pl.semaphore_signal(barrier, inc=1, device_id=peer_id(axis, peer), device_id_type=MESH)
    pl.semaphore_wait(barrier, groups * (n - 1))

    scatter = []
    for g, axis in enumerate(group_axes):
        recv, gathered, s1, r1, s2, r2 = per[g]
        me = lax.axis_index(axis)
        copies = []
        for k in range(1, n):
            peer = lax.rem(me + k, n)
            copy = pltpu.make_async_remote_copy(
                src_ref=piece(sources[g], peer),
                dst_ref=recv.at[me],
                send_sem=s1.at[peer],
                recv_sem=r1.at[me],
                device_id=peer_id(axis, peer),
                device_id_type=MESH,
            )
            copy.start()
            copies.append(copy)
        scatter.append(copies)

    gathers = []
    for g, axis in enumerate(group_axes):
        recv, gathered, s1, r1, s2, r2 = per[g]
        me = lax.axis_index(axis)
        for k in range(1, n):
            source = lax.rem(me + n - k, n)
            pltpu.make_async_remote_copy(
                src_ref=piece(sources[g], source),
                dst_ref=recv.at[source],
                send_sem=s1.at[source],
                recv_sem=r1.at[source],
                device_id=peer_id(axis, source),
                device_id_type=MESH,
            ).wait_recv()
        total = piece(sources[g], me)[...]
        for k in range(1, n):
            total = total + recv[lax.rem(me + k, n)]
        outs[g][:, cols(me)] = total
        copies = []
        for k in range(1, n):
            peer = lax.rem(me + k, n)
            copy = pltpu.make_async_remote_copy(
                src_ref=outs[g].at[:, cols(me)],
                dst_ref=outs[g].at[:, cols(me)],
                send_sem=s2.at[peer],
                recv_sem=r2.at[me],
                device_id=peer_id(axis, peer),
                device_id_type=MESH,
            )
            copy.start()
            copies.append(copy)
        gathers.append(copies)

    for g, axis in enumerate(group_axes):
        recv, gathered, s1, r1, s2, r2 = per[g]
        me = lax.axis_index(axis)
        for copy in scatter[g]:
            copy.wait_send()
        for k in range(1, n):
            source = lax.rem(me + n - k, n)
            pltpu.make_async_remote_copy(
                src_ref=outs[g].at[:, cols(source)],
                dst_ref=outs[g].at[:, cols(source)],
                send_sem=s2.at[source],
                recv_sem=r2.at[source],
                device_id=peer_id(axis, source),
                device_id_type=MESH,
            ).wait_recv()
        for copy in gathers[g]:
            copy.wait_send()


def all_reduce(arrays, group_axes, n, collective_id, block_width, info=None):
    extra = 0 if info is None else 8
    shapes = [(a.shape[0] + extra, a.shape[1]) for a in arrays]
    width = shapes[0][1] // n
    scratch = []
    for rows, _ in shapes:
        scratch += [
            pltpu.VMEM((n, rows, width), jnp.float32),
            pltpu.VMEM((n, rows, width), jnp.float32),
            pltpu.SemaphoreType.DMA((n,)),
            pltpu.SemaphoreType.DMA((n,)),
            pltpu.SemaphoreType.DMA((n,)),
            pltpu.SemaphoreType.DMA((n,)),
        ]
        if info is not None:
            scratch.append(pltpu.VMEM((n, rows, width), jnp.float32))
    in_specs = [pl.BlockSpec(memory_space=pltpu.VMEM)] * len(arrays)
    if info is not None:
        in_specs = [pl.BlockSpec(memory_space=pltpu.SMEM)] + in_specs
        arrays = [info] + arrays
    return pl.pallas_call(
        functools.partial(reduce_kernel, n, group_axes, block_width, info is not None),
        out_shape=tuple(jax.ShapeDtypeStruct(s, jnp.float32) for s in shapes),
        in_specs=in_specs,
        out_specs=tuple(pl.BlockSpec(memory_space=pltpu.VMEM) for _ in shapes),
        scratch_shapes=scratch,
        compiler_params=pltpu.CompilerParams(collective_id=collective_id, has_side_effects=True),
    )(*arrays)


def pick_blocks(full, index, blocks, block_width):
    chosen = full[None, :, :block_width]
    for b in range(1, blocks):
        chosen = jnp.where(
            (index == b)[:, None, None], full[None, :, b * block_width : (b + 1) * block_width], chosen
        )
    return chosen


def by_tile(stacked, matrices, tiles, contract, slots):
    results = [
        lax.dot_general(
            stacked, matrices[t], (((1,), (contract,)), ((), ())),
            preferred_element_type=jnp.float32,
        )
        for t in range(matrices.shape[0])
    ]
    chosen = results[0].reshape(slots, -1, stacked.shape[1])
    for t in range(1, len(results)):
        chosen = jnp.where(
            (tiles == t)[:, None, None], results[t].reshape(slots, -1, stacked.shape[1]), chosen
        )
    return chosen


def per_device(
    tile_matrix,
    tile_inverse,
    block_rows,
    block_cols,
    block_tiles,
    block_count,
    column_values,
    column_duals,
    unit_cost,
    capacity,
    row_values,
    row_duals,
    row_lower,
    row_upper,
    block_image,
    image_dual,
    input_dual,
):
    block_width = tile_matrix.shape[1]
    scenarios = column_values.shape[0]
    col_blocks = column_values.shape[1] // block_width
    row_blocks = row_values.shape[1] // block_width
    slot_total = block_rows.shape[2]
    n_row = lax.axis_size("row")
    rows_here = block_rows[0, 0]
    cols_here = block_cols[0, 0]
    tiles_here = block_tiles[0, 0]
    live_slot = jnp.arange(slot_total, dtype=jnp.int32) < block_count[0, 0]
    x_own = column_values
    x_dual = column_duals
    y_state = row_values
    y_dual = row_duals
    images = block_image[0, 0]
    image_duals = image_dual[0, 0]
    input_duals = input_dual[0, 0]
    col_mask = [(live_slot & (cols_here == b))[:, None, None] for b in range(col_blocks)]
    row_mask = [(live_slot & (rows_here == b))[:, None, None] for b in range(row_blocks)]
    col_denom = None
    row_denom = None
    for iteration in range(ITERS):
        x_half = jnp.clip(x_own - x_dual - unit_cost, 0.0, capacity)
        y_half = jnp.clip(y_state - y_dual, row_lower, row_upper)
        y_anchor = y_half + y_dual
        image_gap = (images - image_duals).astype(jnp.bfloat16).reshape(-1, block_width)
        pulled = by_tile(image_gap, tile_matrix, tiles_here, 1, slot_total)
        x_columns = pick_blocks(x_own, cols_here, col_blocks, block_width)
        merged = (x_columns - input_duals + pulled).astype(jnp.bfloat16).reshape(-1, block_width)
        x_proj = by_tile(merged, tile_inverse, tiles_here, 0, slot_total)
        y_proj = by_tile(
            x_proj.astype(jnp.bfloat16).reshape(-1, block_width), tile_matrix, tiles_here, 0,
            slot_total,
        )
        x_terms = x_proj + input_duals
        y_terms = y_proj + image_duals
        col_terms = jnp.concatenate(
            [jnp.sum(jnp.where(m, x_terms, 0.0), axis=0) for m in col_mask], axis=1
        )
        row_terms = jnp.concatenate(
            [jnp.sum(jnp.where(m, y_terms, 0.0), axis=0) for m in row_mask], axis=1
        )
        if iteration == 0:
            slot_info = jnp.concatenate([cols_here, rows_here, block_count[0, 0][None]])
            col_total, row_total = all_reduce(
                [col_terms, row_terms], AXES, n_row, 0, block_width, slot_info
            )
            col_denom = 1.0 + col_total[scenarios : scenarios + 1]
            row_denom = 1.0 + row_total[scenarios : scenarios + 1]
            col_total = col_total[:scenarios]
            row_total = row_total[:scenarios]
        else:
            col_total, row_total = all_reduce([col_terms, row_terms], AXES, n_row, 1, block_width)
        x_own = (x_half + x_dual + col_total) / col_denom
        x_dual = x_dual + x_half - x_own
        shift_full = (row_total - y_anchor) / row_denom
        y_state = y_anchor + shift_full
        y_dual = y_dual + y_half - y_state
        input_duals = input_duals + x_proj - pick_blocks(x_own, cols_here, col_blocks, block_width)
        new_images = y_proj + image_duals - pick_blocks(shift_full, rows_here, row_blocks, block_width)
        image_duals = image_duals + y_proj - new_images
        images = new_images
    column_final = jnp.clip(x_own - x_dual - unit_cost, 0.0, capacity)
    row_final = jnp.clip(y_state - y_dual, row_lower, row_upper)
    return (column_final, row_final)


def solution(mesh):
    placed = (
        P(),
        P(),
        P("row", "col", None),
        P("row", "col", None),
        P("row", "col", None),
        P("row", "col"),
        P(None, "col"),
        P(None, "col"),
        P(None, "col"),
        P(None, "col"),
        P(None, "row"),
        P(None, "row"),
        P(None, "row"),
        P(None, "row"),
        P("row", "col", None, None, None),
        P("row", "col", None, None, None),
        P("row", "col", None, None, None),
    )
    return jax.shard_map(
        per_device,
        mesh=mesh,
        in_specs=placed,
        out_specs=(P(None, "col"), P(None, "row")),
        check_vma=False,
    )
```

```python
import functools

import jax
import jax.numpy as jnp
from jax import lax
from jax.experimental import pallas as pl
from jax.experimental.pallas import tpu as pltpu
from jax.sharding import PartitionSpec as P

ITERS = 2
MESH = pl.DeviceIdType.MESH
AXES = ("row", "col")


def peer_id(axis, peer):
    if axis == "row":
        return (peer, lax.axis_index("col"))
    return (lax.axis_index("row"), peer)


def reduce_kernel(n, group_axes, block_width, with_counts, finish, *refs):
    groups = len(group_axes)
    if with_counts:
        info, refs = refs[0], refs[1:]
    ins = refs[:groups]
    refs = refs[groups:]
    operands = []
    if finish is not None:
        for g in range(groups):
            operands.append(refs[: finish[g][1]])
            refs = refs[finish[g][1] :]
    outs = refs[:groups]
    scratch = refs[groups:]
    size = 7 if with_counts else 6
    per = [scratch[size * g : size * g + 6] for g in range(groups)]
    width = ins[0].shape[1] // n
    sources = list(ins)

    def cols(index):
        return pl.ds(pl.multiple_of(index * width, width), width)

    def piece(ref, index):
        if len(ref.shape) == 3:
            return ref.at[index]
        return ref.at[:, cols(index)]

    if with_counts:
        slots = (info.shape[0] - 1) // groups
        live = info[groups * slots]
        for g in range(groups):
            send = scratch[size * g + 6]
            data_rows = ins[g].shape[0]
            extra = send.shape[1] - data_rows
            for p in range(n):
                block = (p * width) // block_width
                count = jnp.int32(0)
                for k in range(slots):
                    count = count + jnp.where(
                        (k < live) & (info[g * slots + k] == block), 1, 0
                    ).astype(jnp.int32)
                send[p, :data_rows, :] = ins[g][:, p * width : (p + 1) * width]
                send[p, data_rows:, :] = jnp.full((extra, width), count, jnp.int32).astype(
                    jnp.float32
                )
            sources[g] = send
    barrier = pltpu.get_barrier_semaphore()
    for axis in group_axes:
        me = lax.axis_index(axis)
        for k in range(1, n):
            peer = lax.rem(me + k, n)
            pl.semaphore_signal(barrier, inc=1, device_id=peer_id(axis, peer), device_id_type=MESH)
    pl.semaphore_wait(barrier, groups * (n - 1))

    scatter = []
    for g, axis in enumerate(group_axes):
        recv, gathered, s1, r1, s2, r2 = per[g]
        me = lax.axis_index(axis)
        copies = []
        for k in range(1, n):
            peer = lax.rem(me + k, n)
            copy = pltpu.make_async_remote_copy(
                src_ref=piece(sources[g], peer),
                dst_ref=recv.at[me],
                send_sem=s1.at[peer],
                recv_sem=r1.at[me],
                device_id=peer_id(axis, peer),
                device_id_type=MESH,
            )
            copy.start()
            copies.append(copy)
        scatter.append(copies)

    gathers = []
    for g, axis in enumerate(group_axes):
        recv, gathered, s1, r1, s2, r2 = per[g]
        me = lax.axis_index(axis)
        for k in range(1, n):
            source = lax.rem(me + n - k, n)
            pltpu.make_async_remote_copy(
                src_ref=piece(sources[g], source),
                dst_ref=recv.at[source],
                send_sem=s1.at[source],
                recv_sem=r1.at[source],
                device_id=peer_id(axis, source),
                device_id_type=MESH,
            ).wait_recv()
        total = piece(sources[g], me)[...]
        for k in range(1, n):
            total = total + recv[lax.rem(me + k, n)]
        if finish is not None:
            total = finish[g][0](total, *[ref[:, cols(me)] for ref in operands[g]])
        outs[g][:, cols(me)] = total
        copies = []
        for k in range(1, n):
            peer = lax.rem(me + k, n)
            copy = pltpu.make_async_remote_copy(
                src_ref=outs[g].at[:, cols(me)],
                dst_ref=outs[g].at[:, cols(me)],
                send_sem=s2.at[peer],
                recv_sem=r2.at[me],
                device_id=peer_id(axis, peer),
                device_id_type=MESH,
            )
            copy.start()
            copies.append(copy)
        gathers.append(copies)

    for g, axis in enumerate(group_axes):
        recv, gathered, s1, r1, s2, r2 = per[g]
        me = lax.axis_index(axis)
        for copy in scatter[g]:
            copy.wait_send()
        for k in range(1, n):
            source = lax.rem(me + n - k, n)
            pltpu.make_async_remote_copy(
                src_ref=outs[g].at[:, cols(source)],
                dst_ref=outs[g].at[:, cols(source)],
                send_sem=s2.at[source],
                recv_sem=r2.at[source],
                device_id=peer_id(axis, source),
                device_id_type=MESH,
            ).wait_recv()
        for copy in gathers[g]:
            copy.wait_send()


def all_reduce(arrays, group_axes, n, collective_id, block_width, info=None, finish=None):
    extra = 0 if info is None else 8
    shapes = [(a.shape[0] + extra, a.shape[1]) for a in arrays]
    width = shapes[0][1] // n
    scratch = []
    for rows, _ in shapes:
        scratch += [
            pltpu.VMEM((n, rows, width), jnp.float32),
            pltpu.VMEM((n, rows, width), jnp.float32),
            pltpu.SemaphoreType.DMA((n,)),
            pltpu.SemaphoreType.DMA((n,)),
            pltpu.SemaphoreType.DMA((n,)),
            pltpu.SemaphoreType.DMA((n,)),
        ]
        if info is not None:
            scratch.append(pltpu.VMEM((n, rows, width), jnp.float32))
    rules = None
    if finish is not None:
        rules = tuple((rule, len(extra)) for rule, extra in finish)
        arrays = arrays + [a for _, extra in finish for a in extra]
    in_specs = [pl.BlockSpec(memory_space=pltpu.VMEM)] * len(arrays)
    if info is not None:
        in_specs = [pl.BlockSpec(memory_space=pltpu.SMEM)] + in_specs
        arrays = [info] + arrays
    return pl.pallas_call(
        functools.partial(reduce_kernel, n, group_axes, block_width, info is not None, rules),
        out_shape=tuple(jax.ShapeDtypeStruct(s, jnp.float32) for s in shapes),
        in_specs=in_specs,
        out_specs=tuple(pl.BlockSpec(memory_space=pltpu.VMEM) for _ in shapes),
        scratch_shapes=scratch,
        compiler_params=pltpu.CompilerParams(collective_id=collective_id, has_side_effects=True),
    )(*arrays)


def column_rule(total, x_half, x_dual, cost, capacity, denom):
    x_own = (x_half + x_dual + total) / denom
    x_dual = x_dual + x_half - x_own
    return jnp.minimum(jnp.maximum(x_own - x_dual - cost, 0.0), capacity)


def row_rule(total, y_half, y_dual, lower, upper, denom):
    y_anchor = y_half + y_dual
    y_state = y_anchor + (total - y_anchor) / denom
    y_dual = y_dual + y_half - y_state
    return jnp.minimum(jnp.maximum(y_state - y_dual, lower), upper)


def pick_blocks(full, index, blocks, block_width):
    chosen = full[None, :, :block_width]
    for b in range(1, blocks):
        chosen = jnp.where(
            (index == b)[:, None, None], full[None, :, b * block_width : (b + 1) * block_width], chosen
        )
    return chosen


def by_tile(stacked, matrices, tiles, contract, slots):
    results = [
        lax.dot_general(
            stacked, matrices[t], (((1,), (contract,)), ((), ())),
            preferred_element_type=jnp.float32,
        )
        for t in range(matrices.shape[0])
    ]
    chosen = results[0].reshape(slots, -1, stacked.shape[1])
    for t in range(1, len(results)):
        chosen = jnp.where(
            (tiles == t)[:, None, None], results[t].reshape(slots, -1, stacked.shape[1]), chosen
        )
    return chosen


def per_device(
    tile_matrix,
    tile_inverse,
    block_rows,
    block_cols,
    block_tiles,
    block_count,
    column_values,
    column_duals,
    unit_cost,
    capacity,
    row_values,
    row_duals,
    row_lower,
    row_upper,
    block_image,
    image_dual,
    input_dual,
):
    block_width = tile_matrix.shape[1]
    scenarios = column_values.shape[0]
    col_blocks = column_values.shape[1] // block_width
    row_blocks = row_values.shape[1] // block_width
    slot_total = block_rows.shape[2]
    n_row = lax.axis_size("row")
    rows_here = block_rows[0, 0]
    cols_here = block_cols[0, 0]
    tiles_here = block_tiles[0, 0]
    live_slot = jnp.arange(slot_total, dtype=jnp.int32) < block_count[0, 0]
    x_own = column_values
    x_dual = column_duals
    y_state = row_values
    y_dual = row_duals
    images = block_image[0, 0]
    image_duals = image_dual[0, 0]
    input_duals = input_dual[0, 0]
    col_mask = [(live_slot & (cols_here == b))[:, None, None] for b in range(col_blocks)]
    row_mask = [(live_slot & (rows_here == b))[:, None, None] for b in range(row_blocks)]
    col_denom = None
    row_denom = None
    for iteration in range(ITERS):
        x_half = jnp.clip(x_own - x_dual - unit_cost, 0.0, capacity)
        y_half = jnp.clip(y_state - y_dual, row_lower, row_upper)
        y_anchor = y_half + y_dual
        image_gap = (images - image_duals).astype(jnp.bfloat16).reshape(-1, block_width)
        pulled = by_tile(image_gap, tile_matrix, tiles_here, 1, slot_total)
        x_columns = pick_blocks(x_own, cols_here, col_blocks, block_width)
        merged = (x_columns - input_duals + pulled).astype(jnp.bfloat16).reshape(-1, block_width)
        x_proj = by_tile(merged, tile_inverse, tiles_here, 0, slot_total)
        y_proj = by_tile(
            x_proj.astype(jnp.bfloat16).reshape(-1, block_width), tile_matrix, tiles_here, 0,
            slot_total,
        )
        x_terms = x_proj + input_duals
        y_terms = y_proj + image_duals
        col_terms = jnp.concatenate(
            [jnp.sum(jnp.where(m, x_terms, 0.0), axis=0) for m in col_mask], axis=1
        )
        row_terms = jnp.concatenate(
            [jnp.sum(jnp.where(m, y_terms, 0.0), axis=0) for m in row_mask], axis=1
        )
        if iteration == 0:
            slot_info = jnp.concatenate([cols_here, rows_here, block_count[0, 0][None]])
            col_total, row_total = all_reduce(
                [col_terms, row_terms], AXES, n_row, 0, block_width, slot_info
            )
            col_denom = 1.0 + col_total[scenarios : scenarios + 1]
            row_denom = 1.0 + row_total[scenarios : scenarios + 1]
            col_total = col_total[:scenarios]
            row_total = row_total[:scenarios]
        elif iteration == ITERS - 1:
            return all_reduce(
                [col_terms, row_terms],
                AXES,
                n_row,
                1,
                block_width,
                finish=[
                    (column_rule, [x_half, x_dual, unit_cost, capacity, col_denom]),
                    (row_rule, [y_half, y_dual, row_lower, row_upper, row_denom]),
                ],
            )
        else:
            col_total, row_total = all_reduce([col_terms, row_terms], AXES, n_row, 2, block_width)
        x_own = (x_half + x_dual + col_total) / col_denom
        x_dual = x_dual + x_half - x_own
        shift_full = (row_total - y_anchor) / row_denom
        y_state = y_anchor + shift_full
        y_dual = y_dual + y_half - y_state
        input_duals = input_duals + x_proj - pick_blocks(x_own, cols_here, col_blocks, block_width)
        new_images = y_proj + image_duals - pick_blocks(shift_full, rows_here, row_blocks, block_width)
        image_duals = image_duals + y_proj - new_images
        images = new_images
    column_final = jnp.clip(x_own - x_dual - unit_cost, 0.0, capacity)
    row_final = jnp.clip(y_state - y_dual, row_lower, row_upper)
    return (column_final, row_final)


def solution(mesh):
    placed = (
        P(),
        P(),
        P("row", "col", None),
        P("row", "col", None),
        P("row", "col", None),
        P("row", "col"),
        P(None, "col"),
        P(None, "col"),
        P(None, "col"),
        P(None, "col"),
        P(None, "row"),
        P(None, "row"),
        P(None, "row"),
        P(None, "row"),
        P("row", "col", None, None, None),
        P("row", "col", None, None, None),
        P("row", "col", None, None, None),
    )
    return jax.shard_map(
        per_device,
        mesh=mesh,
        in_specs=placed,
        out_specs=(P(None, "col"), P(None, "row")),
        check_vma=False,
    )
```

```python
import functools

import jax
import jax.numpy as jnp
from jax import lax
from jax.experimental import pallas as pl
from jax.experimental.pallas import tpu as pltpu
from jax.sharding import PartitionSpec as P

ITERS = 2
MESH = pl.DeviceIdType.MESH
AXES = ("row", "col")


def peer_id(axis, peer):
    if axis == "row":
        return (peer, lax.axis_index("col"))
    return (lax.axis_index("row"), peer)


def reduce_kernel(n, group_axes, block_width, with_counts, *refs):
    groups = len(group_axes)
    if with_counts:
        info, refs = refs[0], refs[1:]
    ins = refs[:groups]
    outs = refs[groups : 2 * groups]
    scratch = refs[2 * groups :]
    size = 7 if with_counts else 6
    per = [scratch[size * g : size * g + 6] for g in range(groups)]
    width = ins[0].shape[1] // n
    sources = list(ins)

    def cols(index):
        return pl.ds(pl.multiple_of(index * width, width), width)

    def piece(ref, index):
        if len(ref.shape) == 3:
            return ref.at[index]
        return ref.at[:, cols(index)]

    if with_counts:
        slots = (info.shape[0] - 1) // groups
        live = info[groups * slots]
        for g in range(groups):
            send = scratch[size * g + 6]
            data_rows = ins[g].shape[0]
            extra = send.shape[1] - data_rows
            for p in range(n):
                block = (p * width) // block_width
                count = jnp.int32(0)
                for k in range(slots):
                    count = count + jnp.where(
                        (k < live) & (info[g * slots + k] == block), 1, 0
                    ).astype(jnp.int32)
                send[p, :data_rows, :] = ins[g][:, p * width : (p + 1) * width]
                send[p, data_rows:, :] = jnp.full((extra, width), count, jnp.int32).astype(
                    jnp.float32
                )
            sources[g] = send
    issue_order = sorted(range(groups), key=lambda g: group_axes[g] != "col")
    barrier = pltpu.get_barrier_semaphore()
    for axis in [group_axes[g] for g in issue_order]:
        me = lax.axis_index(axis)
        for k in range(1, n):
            peer = lax.rem(me + k, n)
            pl.semaphore_signal(barrier, inc=1, device_id=peer_id(axis, peer), device_id_type=MESH)
    pl.semaphore_wait(barrier, groups * (n - 1))

    scatter = [None] * groups
    for g in issue_order:
        axis = group_axes[g]
        recv, gathered, s1, r1, s2, r2 = per[g]
        me = lax.axis_index(axis)
        copies = []
        for k in range(1, n):
            peer = lax.rem(me + k, n)
            copy = pltpu.make_async_remote_copy(
                src_ref=piece(sources[g], peer),
                dst_ref=recv.at[me],
                send_sem=s1.at[peer],
                recv_sem=r1.at[me],
                device_id=peer_id(axis, peer),
                device_id_type=MESH,
            )
            copy.start()
            copies.append(copy)
        scatter[g] = copies

    gathers = []
    for g, axis in enumerate(group_axes):
        recv, gathered, s1, r1, s2, r2 = per[g]
        me = lax.axis_index(axis)
        for k in range(1, n):
            source = lax.rem(me + n - k, n)
            pltpu.make_async_remote_copy(
                src_ref=piece(sources[g], source),
                dst_ref=recv.at[source],
                send_sem=s1.at[source],
                recv_sem=r1.at[source],
                device_id=peer_id(axis, source),
                device_id_type=MESH,
            ).wait_recv()
        total = piece(sources[g], me)[...]
        for k in range(1, n):
            total = total + recv[lax.rem(me + k, n)]
        outs[g][:, cols(me)] = total
        copies = []
        for k in range(1, n):
            peer = lax.rem(me + k, n)
            copy = pltpu.make_async_remote_copy(
                src_ref=outs[g].at[:, cols(me)],
                dst_ref=outs[g].at[:, cols(me)],
                send_sem=s2.at[peer],
                recv_sem=r2.at[me],
                device_id=peer_id(axis, peer),
                device_id_type=MESH,
            )
            copy.start()
            copies.append(copy)
        gathers.append(copies)

    for g, axis in enumerate(group_axes):
        recv, gathered, s1, r1, s2, r2 = per[g]
        me = lax.axis_index(axis)
        for copy in scatter[g]:
            copy.wait_send()
        for k in range(1, n):
            source = lax.rem(me + n - k, n)
            pltpu.make_async_remote_copy(
                src_ref=outs[g].at[:, cols(source)],
                dst_ref=outs[g].at[:, cols(source)],
                send_sem=s2.at[source],
                recv_sem=r2.at[source],
                device_id=peer_id(axis, source),
                device_id_type=MESH,
            ).wait_recv()
        for copy in gathers[g]:
            copy.wait_send()


def all_reduce(arrays, group_axes, n, collective_id, block_width, info=None):
    extra = 0 if info is None else 8
    shapes = [(a.shape[0] + extra, a.shape[1]) for a in arrays]
    width = shapes[0][1] // n
    scratch = []
    for rows, _ in shapes:
        scratch += [
            pltpu.VMEM((n, rows, width), jnp.float32),
            pltpu.VMEM((n, rows, width), jnp.float32),
            pltpu.SemaphoreType.DMA((n,)),
            pltpu.SemaphoreType.DMA((n,)),
            pltpu.SemaphoreType.DMA((n,)),
            pltpu.SemaphoreType.DMA((n,)),
        ]
        if info is not None:
            scratch.append(pltpu.VMEM((n, rows, width), jnp.float32))
    in_specs = [pl.BlockSpec(memory_space=pltpu.VMEM)] * len(arrays)
    if info is not None:
        in_specs = [pl.BlockSpec(memory_space=pltpu.SMEM)] + in_specs
        arrays = [info] + arrays
    return pl.pallas_call(
        functools.partial(reduce_kernel, n, group_axes, block_width, info is not None),
        out_shape=tuple(jax.ShapeDtypeStruct(s, jnp.float32) for s in shapes),
        in_specs=in_specs,
        out_specs=tuple(pl.BlockSpec(memory_space=pltpu.VMEM) for _ in shapes),
        scratch_shapes=scratch,
        compiler_params=pltpu.CompilerParams(collective_id=collective_id, has_side_effects=True),
    )(*arrays)


def pick_blocks(full, index, blocks, block_width):
    chosen = full[None, :, :block_width]
    for b in range(1, blocks):
        chosen = jnp.where(
            (index == b)[:, None, None], full[None, :, b * block_width : (b + 1) * block_width], chosen
        )
    return chosen


def by_tile(stacked, matrices, tiles, contract, slots):
    results = [
        lax.dot_general(
            stacked, matrices[t], (((1,), (contract,)), ((), ())),
            preferred_element_type=jnp.float32,
        )
        for t in range(matrices.shape[0])
    ]
    chosen = results[0].reshape(slots, -1, stacked.shape[1])
    for t in range(1, len(results)):
        chosen = jnp.where(
            (tiles == t)[:, None, None], results[t].reshape(slots, -1, stacked.shape[1]), chosen
        )
    return chosen


def per_device(
    tile_matrix,
    tile_inverse,
    block_rows,
    block_cols,
    block_tiles,
    block_count,
    column_values,
    column_duals,
    unit_cost,
    capacity,
    row_values,
    row_duals,
    row_lower,
    row_upper,
    block_image,
    image_dual,
    input_dual,
):
    block_width = tile_matrix.shape[1]
    scenarios = column_values.shape[0]
    col_blocks = column_values.shape[1] // block_width
    row_blocks = row_values.shape[1] // block_width
    slot_total = block_rows.shape[2]
    n_row = lax.axis_size("row")
    rows_here = block_rows[0, 0]
    cols_here = block_cols[0, 0]
    tiles_here = block_tiles[0, 0]
    live_slot = jnp.arange(slot_total, dtype=jnp.int32) < block_count[0, 0]
    x_own = column_values
    x_dual = column_duals
    y_state = row_values
    y_dual = row_duals
    images = block_image[0, 0]
    image_duals = image_dual[0, 0]
    input_duals = input_dual[0, 0]
    col_mask = [(live_slot & (cols_here == b))[:, None, None] for b in range(col_blocks)]
    row_mask = [(live_slot & (rows_here == b))[:, None, None] for b in range(row_blocks)]
    col_denom = None
    row_denom = None
    for iteration in range(ITERS):
        x_half = jnp.clip(x_own - x_dual - unit_cost, 0.0, capacity)
        y_half = jnp.clip(y_state - y_dual, row_lower, row_upper)
        y_anchor = y_half + y_dual
        image_gap = (images - image_duals).astype(jnp.bfloat16).reshape(-1, block_width)
        pulled = by_tile(image_gap, tile_matrix, tiles_here, 1, slot_total)
        x_columns = pick_blocks(x_own, cols_here, col_blocks, block_width)
        merged = (x_columns - input_duals + pulled).astype(jnp.bfloat16).reshape(-1, block_width)
        x_proj = by_tile(merged, tile_inverse, tiles_here, 0, slot_total)
        y_proj = by_tile(
            x_proj.astype(jnp.bfloat16).reshape(-1, block_width), tile_matrix, tiles_here, 0,
            slot_total,
        )
        x_terms = x_proj + input_duals
        y_terms = y_proj + image_duals
        col_terms = jnp.concatenate(
            [jnp.sum(jnp.where(m, x_terms, 0.0), axis=0) for m in col_mask], axis=1
        )
        row_terms = jnp.concatenate(
            [jnp.sum(jnp.where(m, y_terms, 0.0), axis=0) for m in row_mask], axis=1
        )
        if iteration == 0:
            slot_info = jnp.concatenate([cols_here, rows_here, block_count[0, 0][None]])
            col_total, row_total = all_reduce(
                [col_terms, row_terms], AXES, n_row, 0, block_width, slot_info
            )
            col_denom = 1.0 + col_total[scenarios : scenarios + 1]
            row_denom = 1.0 + row_total[scenarios : scenarios + 1]
            col_total = col_total[:scenarios]
            row_total = row_total[:scenarios]
        else:
            col_total, row_total = all_reduce([col_terms, row_terms], AXES, n_row, 1, block_width)
        x_own = (x_half + x_dual + col_total) / col_denom
        x_dual = x_dual + x_half - x_own
        shift_full = (row_total - y_anchor) / row_denom
        y_state = y_anchor + shift_full
        y_dual = y_dual + y_half - y_state
        input_duals = input_duals + x_proj - pick_blocks(x_own, cols_here, col_blocks, block_width)
        new_images = y_proj + image_duals - pick_blocks(shift_full, rows_here, row_blocks, block_width)
        image_duals = image_duals + y_proj - new_images
        images = new_images
    column_final = jnp.clip(x_own - x_dual - unit_cost, 0.0, capacity)
    row_final = jnp.clip(y_state - y_dual, row_lower, row_upper)
    return (column_final, row_final)


def solution(mesh):
    placed = (
        P(),
        P(),
        P("row", "col", None),
        P("row", "col", None),
        P("row", "col", None),
        P("row", "col"),
        P(None, "col"),
        P(None, "col"),
        P(None, "col"),
        P(None, "col"),
        P(None, "row"),
        P(None, "row"),
        P(None, "row"),
        P(None, "row"),
        P("row", "col", None, None, None),
        P("row", "col", None, None, None),
        P("row", "col", None, None, None),
    )
    return jax.shard_map(
        per_device,
        mesh=mesh,
        in_specs=placed,
        out_specs=(P(None, "col"), P(None, "row")),
        check_vma=False,
    )
```

```python
import functools

import jax
import jax.numpy as jnp
from jax import lax
from jax.experimental import pallas as pl
from jax.experimental.pallas import tpu as pltpu
from jax.sharding import PartitionSpec as P

ITERS = 2
MESH = pl.DeviceIdType.MESH
AXES = ("row", "col")


def peer_id(axis, peer):
    if axis == "row":
        return (peer, lax.axis_index("col"))
    return (lax.axis_index("row"), peer)


def reduce_kernel(n, group_axes, block_width, with_counts, blocks, *refs):
    groups = len(group_axes)
    if with_counts:
        info, refs = refs[0], refs[1:]
    ins = [refs[g * blocks : (g + 1) * blocks] for g in range(groups)]
    refs = refs[groups * blocks :]
    outs = refs[:groups]
    scratch = refs[groups:]
    size = 7 if with_counts else 6
    per = [scratch[size * g : size * g + 6] for g in range(groups)]
    width = blocks * block_width // n
    per_block = block_width // width
    chunked = [False] * groups

    def cols(index):
        return pl.ds(pl.multiple_of(index * width, width), width)

    def piece(g, index, b=0):
        if chunked[g]:
            return scratch[size * g + 6].at[index]
        offset = pl.multiple_of(lax.rem(index, per_block) * width, width)
        return ins[g][b].at[:, pl.ds(offset, width)]

    def start_from(g, index, make):
        if chunked[g]:
            make(piece(g, index)).start()
            return
        for b in range(blocks):

            @pl.when(index // per_block == b)
            def _():
                make(piece(g, index, b)).start()

    def load(g, index):
        if chunked[g]:
            return piece(g, index)[...]
        value = piece(g, index, 0)[...]
        for b in range(1, blocks):
            value = jnp.where(index // per_block == b, piece(g, index, b)[...], value)
        return value

    if with_counts:
        slots = (info.shape[0] - 1) // groups
        live = info[groups * slots]
        for g in range(groups):
            send = scratch[size * g + 6]
            data_rows = ins[g][0].shape[0]
            extra = send.shape[1] - data_rows
            for p in range(n):
                block = (p * width) // block_width
                count = jnp.int32(0)
                for k in range(slots):
                    count = count + jnp.where(
                        (k < live) & (info[g * slots + k] == block), 1, 0
                    ).astype(jnp.int32)
                part, offset = divmod(p, per_block)
                send[p, :data_rows, :] = ins[g][part][:, offset * width : (offset + 1) * width]
                send[p, data_rows:, :] = jnp.full((extra, width), count, jnp.int32).astype(
                    jnp.float32
                )
            chunked[g] = True
    issue_order = sorted(range(groups), key=lambda g: group_axes[g] != "col")
    barrier = pltpu.get_barrier_semaphore()
    for axis in [group_axes[g] for g in issue_order]:
        me = lax.axis_index(axis)
        for k in range(1, n):
            peer = lax.rem(me + k, n)
            pl.semaphore_signal(barrier, inc=1, device_id=peer_id(axis, peer), device_id_type=MESH)
    pl.semaphore_wait(barrier, groups * (n - 1))

    scatter = [None] * groups
    for g in issue_order:
        axis = group_axes[g]
        recv, gathered, s1, r1, s2, r2 = per[g]
        me = lax.axis_index(axis)
        copies = []
        for k in range(1, n):
            peer = lax.rem(me + k, n)
            def make(src, peer=peer, recv=recv, s1=s1, r1=r1, me=me, axis=axis):
                return pltpu.make_async_remote_copy(
                    src_ref=src,
                    dst_ref=recv.at[me],
                    send_sem=s1.at[peer],
                    recv_sem=r1.at[me],
                    device_id=peer_id(axis, peer),
                    device_id_type=MESH,
                )

            start_from(g, peer, make)
            copies.append(make(piece(g, peer)))
        scatter[g] = copies

    gathers = []
    for g, axis in enumerate(group_axes):
        recv, gathered, s1, r1, s2, r2 = per[g]
        me = lax.axis_index(axis)
        for k in range(1, n):
            source = lax.rem(me + n - k, n)
            pltpu.make_async_remote_copy(
                src_ref=piece(g, source),
                dst_ref=recv.at[source],
                send_sem=s1.at[source],
                recv_sem=r1.at[source],
                device_id=peer_id(axis, source),
                device_id_type=MESH,
            ).wait_recv()
        total = load(g, me)
        for k in range(1, n):
            total = total + recv[lax.rem(me + k, n)]
        outs[g][:, cols(me)] = total
        copies = []
        for k in range(1, n):
            peer = lax.rem(me + k, n)
            copy = pltpu.make_async_remote_copy(
                src_ref=outs[g].at[:, cols(me)],
                dst_ref=outs[g].at[:, cols(me)],
                send_sem=s2.at[peer],
                recv_sem=r2.at[me],
                device_id=peer_id(axis, peer),
                device_id_type=MESH,
            )
            copy.start()
            copies.append(copy)
        gathers.append(copies)

    for g, axis in enumerate(group_axes):
        recv, gathered, s1, r1, s2, r2 = per[g]
        me = lax.axis_index(axis)
        for copy in scatter[g]:
            copy.wait_send()
        for k in range(1, n):
            source = lax.rem(me + n - k, n)
            pltpu.make_async_remote_copy(
                src_ref=outs[g].at[:, cols(source)],
                dst_ref=outs[g].at[:, cols(source)],
                send_sem=s2.at[source],
                recv_sem=r2.at[source],
                device_id=peer_id(axis, source),
                device_id_type=MESH,
            ).wait_recv()
        for copy in gathers[g]:
            copy.wait_send()


def all_reduce(arrays, group_axes, n, collective_id, block_width, info=None):
    extra = 0 if info is None else 8
    blocks = len(arrays[0])
    shapes = [(a[0].shape[0] + extra, blocks * a[0].shape[1]) for a in arrays]
    width = shapes[0][1] // n
    scratch = []
    for rows, _ in shapes:
        scratch += [
            pltpu.VMEM((n, rows, width), jnp.float32),
            pltpu.VMEM((n, rows, width), jnp.float32),
            pltpu.SemaphoreType.DMA((n,)),
            pltpu.SemaphoreType.DMA((n,)),
            pltpu.SemaphoreType.DMA((n,)),
            pltpu.SemaphoreType.DMA((n,)),
        ]
        if info is not None:
            scratch.append(pltpu.VMEM((n, rows, width), jnp.float32))
    arrays = [block for group in arrays for block in group]
    in_specs = [pl.BlockSpec(memory_space=pltpu.VMEM)] * len(arrays)
    if info is not None:
        in_specs = [pl.BlockSpec(memory_space=pltpu.SMEM)] + in_specs
        arrays = [info] + arrays
    return pl.pallas_call(
        functools.partial(reduce_kernel, n, group_axes, block_width, info is not None, blocks),
        out_shape=tuple(jax.ShapeDtypeStruct(s, jnp.float32) for s in shapes),
        in_specs=in_specs,
        out_specs=tuple(pl.BlockSpec(memory_space=pltpu.VMEM) for _ in shapes),
        scratch_shapes=scratch,
        compiler_params=pltpu.CompilerParams(collective_id=collective_id, has_side_effects=True),
    )(*arrays)


def pick_blocks(full, index, blocks, block_width):
    chosen = full[None, :, :block_width]
    for b in range(1, blocks):
        chosen = jnp.where(
            (index == b)[:, None, None], full[None, :, b * block_width : (b + 1) * block_width], chosen
        )
    return chosen


def by_tile(stacked, matrices, tiles, contract, slots):
    results = [
        lax.dot_general(
            stacked, matrices[t], (((1,), (contract,)), ((), ())),
            preferred_element_type=jnp.float32,
        )
        for t in range(matrices.shape[0])
    ]
    chosen = results[0].reshape(slots, -1, stacked.shape[1])
    for t in range(1, len(results)):
        chosen = jnp.where(
            (tiles == t)[:, None, None], results[t].reshape(slots, -1, stacked.shape[1]), chosen
        )
    return chosen


def per_device(
    tile_matrix,
    tile_inverse,
    block_rows,
    block_cols,
    block_tiles,
    block_count,
    column_values,
    column_duals,
    unit_cost,
    capacity,
    row_values,
    row_duals,
    row_lower,
    row_upper,
    block_image,
    image_dual,
    input_dual,
):
    block_width = tile_matrix.shape[1]
    scenarios = column_values.shape[0]
    col_blocks = column_values.shape[1] // block_width
    row_blocks = row_values.shape[1] // block_width
    slot_total = block_rows.shape[2]
    n_row = lax.axis_size("row")
    rows_here = block_rows[0, 0]
    cols_here = block_cols[0, 0]
    tiles_here = block_tiles[0, 0]
    live_slot = jnp.arange(slot_total, dtype=jnp.int32) < block_count[0, 0]
    x_own = column_values
    x_dual = column_duals
    y_state = row_values
    y_dual = row_duals
    images = block_image[0, 0]
    image_duals = image_dual[0, 0]
    input_duals = input_dual[0, 0]
    col_mask = [(live_slot & (cols_here == b))[:, None, None] for b in range(col_blocks)]
    row_mask = [(live_slot & (rows_here == b))[:, None, None] for b in range(row_blocks)]
    col_denom = None
    row_denom = None
    for iteration in range(ITERS):
        x_half = jnp.clip(x_own - x_dual - unit_cost, 0.0, capacity)
        y_half = jnp.clip(y_state - y_dual, row_lower, row_upper)
        y_anchor = y_half + y_dual
        image_gap = (images - image_duals).astype(jnp.bfloat16).reshape(-1, block_width)
        pulled = by_tile(image_gap, tile_matrix, tiles_here, 1, slot_total)
        x_columns = pick_blocks(x_own, cols_here, col_blocks, block_width)
        merged = (x_columns - input_duals + pulled).astype(jnp.bfloat16).reshape(-1, block_width)
        x_proj = by_tile(merged, tile_inverse, tiles_here, 0, slot_total)
        y_proj = by_tile(
            x_proj.astype(jnp.bfloat16).reshape(-1, block_width), tile_matrix, tiles_here, 0,
            slot_total,
        )
        x_terms = x_proj + input_duals
        y_terms = y_proj + image_duals
        col_terms = [jnp.sum(jnp.where(m, x_terms, 0.0), axis=0) for m in col_mask]
        row_terms = [jnp.sum(jnp.where(m, y_terms, 0.0), axis=0) for m in row_mask]
        if iteration == 0:
            slot_info = jnp.concatenate([cols_here, rows_here, block_count[0, 0][None]])
            col_total, row_total = all_reduce(
                [col_terms, row_terms], AXES, n_row, 0, block_width, slot_info
            )
            col_denom = 1.0 + col_total[scenarios : scenarios + 1]
            row_denom = 1.0 + row_total[scenarios : scenarios + 1]
            col_total = col_total[:scenarios]
            row_total = row_total[:scenarios]
        else:
            col_total, row_total = all_reduce([col_terms, row_terms], AXES, n_row, 1, block_width)
        x_own = (x_half + x_dual + col_total) / col_denom
        x_dual = x_dual + x_half - x_own
        shift_full = (row_total - y_anchor) / row_denom
        y_state = y_anchor + shift_full
        y_dual = y_dual + y_half - y_state
        input_duals = input_duals + x_proj - pick_blocks(x_own, cols_here, col_blocks, block_width)
        new_images = y_proj + image_duals - pick_blocks(shift_full, rows_here, row_blocks, block_width)
        image_duals = image_duals + y_proj - new_images
        images = new_images
    column_final = jnp.clip(x_own - x_dual - unit_cost, 0.0, capacity)
    row_final = jnp.clip(y_state - y_dual, row_lower, row_upper)
    return (column_final, row_final)


def solution(mesh):
    placed = (
        P(),
        P(),
        P("row", "col", None),
        P("row", "col", None),
        P("row", "col", None),
        P("row", "col"),
        P(None, "col"),
        P(None, "col"),
        P(None, "col"),
        P(None, "col"),
        P(None, "row"),
        P(None, "row"),
        P(None, "row"),
        P(None, "row"),
        P("row", "col", None, None, None),
        P("row", "col", None, None, None),
        P("row", "col", None, None, None),
    )
    return jax.shard_map(
        per_device,
        mesh=mesh,
        in_specs=placed,
        out_specs=(P(None, "col"), P(None, "row")),
        check_vma=False,
    )
```

```python
import functools

import jax
import jax.numpy as jnp
from jax import lax
from jax.experimental import pallas as pl
from jax.experimental.pallas import tpu as pltpu
from jax.sharding import PartitionSpec as P

ITERS = 2
MESH = pl.DeviceIdType.MESH
AXES = ("row", "col")


def peer_id(axis, peer):
    if axis == "row":
        return (peer, lax.axis_index("col"))
    return (lax.axis_index("row"), peer)


def reduce_kernel(n, group_axes, block_width, with_counts, *refs):
    groups = len(group_axes)
    if with_counts:
        info, refs = refs[0], refs[1:]
    ins = refs[:groups]
    outs = refs[groups : 2 * groups]
    scratch = refs[2 * groups :]
    size = 7 if with_counts else 6
    per = [scratch[size * g : size * g + 6] for g in range(groups)]
    width = ins[0].shape[1] // n
    sources = list(ins)

    def cols(index):
        return pl.ds(pl.multiple_of(index * width, width), width)

    def piece(ref, index):
        if len(ref.shape) == 3:
            return ref.at[index]
        return ref.at[:, cols(index)]

    if with_counts:
        slots = (info.shape[0] - 1) // groups
        live = info[groups * slots]
        for g in range(groups):
            send = scratch[size * g + 6]
            data_rows = ins[g].shape[0]
            extra = send.shape[1] - data_rows
            for p in range(n):
                block = (p * width) // block_width
                count = jnp.int32(0)
                for k in range(slots):
                    count = count + jnp.where(
                        (k < live) & (info[g * slots + k] == block), 1, 0
                    ).astype(jnp.int32)
                send[p, :data_rows, :] = ins[g][:, p * width : (p + 1) * width]
                send[p, data_rows:, :] = jnp.full((extra, width), count, jnp.int32).astype(
                    jnp.float32
                )
            sources[g] = send
    issue_order = sorted(range(groups), key=lambda g: group_axes[g] != "col")
    barrier = pltpu.get_barrier_semaphore()
    for axis in [group_axes[g] for g in issue_order]:
        me = lax.axis_index(axis)
        for k in range(1, n):
            peer = lax.rem(me + k, n)
            pl.semaphore_signal(barrier, inc=1, device_id=peer_id(axis, peer), device_id_type=MESH)
    pl.semaphore_wait(barrier, groups * (n - 1))

    scatter = [None] * groups
    for g in issue_order:
        axis = group_axes[g]
        recv, gathered, s1, r1, s2, r2 = per[g]
        me = lax.axis_index(axis)
        copies = []
        for k in range(1, n):
            peer = lax.rem(me + k, n)
            copy = pltpu.make_async_remote_copy(
                src_ref=piece(sources[g], peer),
                dst_ref=recv.at[me],
                send_sem=s1.at[peer],
                recv_sem=r1.at[me],
                device_id=peer_id(axis, peer),
                device_id_type=MESH,
            )
            copy.start()
            copies.append(copy)
        scatter[g] = copies

    gathers = [None] * groups
    for g in issue_order:
        axis = group_axes[g]
        recv, gathered, s1, r1, s2, r2 = per[g]
        me = lax.axis_index(axis)
        for k in range(1, n):
            source = lax.rem(me + n - k, n)
            pltpu.make_async_remote_copy(
                src_ref=piece(sources[g], source),
                dst_ref=recv.at[source],
                send_sem=s1.at[source],
                recv_sem=r1.at[source],
                device_id=peer_id(axis, source),
                device_id_type=MESH,
            ).wait_recv()
        total = piece(sources[g], me)[...]
        for k in range(1, n):
            total = total + recv[lax.rem(me + k, n)]
        outs[g][:, cols(me)] = total
        copies = []
        for k in range(1, n):
            peer = lax.rem(me + k, n)
            copy = pltpu.make_async_remote_copy(
                src_ref=outs[g].at[:, cols(me)],
                dst_ref=outs[g].at[:, cols(me)],
                send_sem=s2.at[peer],
                recv_sem=r2.at[me],
                device_id=peer_id(axis, peer),
                device_id_type=MESH,
            )
            copy.start()
            copies.append(copy)
        gathers[g] = copies

    for g, axis in enumerate(group_axes):
        recv, gathered, s1, r1, s2, r2 = per[g]
        me = lax.axis_index(axis)
        for copy in scatter[g]:
            copy.wait_send()
        for k in range(1, n):
            source = lax.rem(me + n - k, n)
            pltpu.make_async_remote_copy(
                src_ref=outs[g].at[:, cols(source)],
                dst_ref=outs[g].at[:, cols(source)],
                send_sem=s2.at[source],
                recv_sem=r2.at[source],
                device_id=peer_id(axis, source),
                device_id_type=MESH,
            ).wait_recv()
        for copy in gathers[g]:
            copy.wait_send()


def all_reduce(arrays, group_axes, n, collective_id, block_width, info=None):
    extra = 0 if info is None else 8
    shapes = [(a.shape[0] + extra, a.shape[1]) for a in arrays]
    width = shapes[0][1] // n
    scratch = []
    for rows, _ in shapes:
        scratch += [
            pltpu.VMEM((n, rows, width), jnp.float32),
            pltpu.VMEM((n, rows, width), jnp.float32),
            pltpu.SemaphoreType.DMA((n,)),
            pltpu.SemaphoreType.DMA((n,)),
            pltpu.SemaphoreType.DMA((n,)),
            pltpu.SemaphoreType.DMA((n,)),
        ]
        if info is not None:
            scratch.append(pltpu.VMEM((n, rows, width), jnp.float32))
    in_specs = [pl.BlockSpec(memory_space=pltpu.VMEM)] * len(arrays)
    if info is not None:
        in_specs = [pl.BlockSpec(memory_space=pltpu.SMEM)] + in_specs
        arrays = [info] + arrays
    return pl.pallas_call(
        functools.partial(reduce_kernel, n, group_axes, block_width, info is not None),
        out_shape=tuple(jax.ShapeDtypeStruct(s, jnp.float32) for s in shapes),
        in_specs=in_specs,
        out_specs=tuple(pl.BlockSpec(memory_space=pltpu.VMEM) for _ in shapes),
        scratch_shapes=scratch,
        compiler_params=pltpu.CompilerParams(collective_id=collective_id, has_side_effects=True),
    )(*arrays)


def pick_blocks(full, index, blocks, block_width):
    chosen = full[None, :, :block_width]
    for b in range(1, blocks):
        chosen = jnp.where(
            (index == b)[:, None, None], full[None, :, b * block_width : (b + 1) * block_width], chosen
        )
    return chosen


def by_tile(stacked, matrices, tiles, contract, slots):
    results = [
        lax.dot_general(
            stacked, matrices[t], (((1,), (contract,)), ((), ())),
            preferred_element_type=jnp.float32,
        )
        for t in range(matrices.shape[0])
    ]
    chosen = results[0].reshape(slots, -1, stacked.shape[1])
    for t in range(1, len(results)):
        chosen = jnp.where(
            (tiles == t)[:, None, None], results[t].reshape(slots, -1, stacked.shape[1]), chosen
        )
    return chosen


def per_device(
    tile_matrix,
    tile_inverse,
    block_rows,
    block_cols,
    block_tiles,
    block_count,
    column_values,
    column_duals,
    unit_cost,
    capacity,
    row_values,
    row_duals,
    row_lower,
    row_upper,
    block_image,
    image_dual,
    input_dual,
):
    block_width = tile_matrix.shape[1]
    scenarios = column_values.shape[0]
    col_blocks = column_values.shape[1] // block_width
    row_blocks = row_values.shape[1] // block_width
    slot_total = block_rows.shape[2]
    n_row = lax.axis_size("row")
    rows_here = block_rows[0, 0]
    cols_here = block_cols[0, 0]
    tiles_here = block_tiles[0, 0]
    live_slot = jnp.arange(slot_total, dtype=jnp.int32) < block_count[0, 0]
    x_own = column_values
    x_dual = column_duals
    y_state = row_values
    y_dual = row_duals
    images = block_image[0, 0]
    image_duals = image_dual[0, 0]
    input_duals = input_dual[0, 0]
    col_mask = [(live_slot & (cols_here == b))[:, None, None] for b in range(col_blocks)]
    row_mask = [(live_slot & (rows_here == b))[:, None, None] for b in range(row_blocks)]
    col_denom = None
    row_denom = None
    for iteration in range(ITERS):
        x_half = jnp.clip(x_own - x_dual - unit_cost, 0.0, capacity)
        y_half = jnp.clip(y_state - y_dual, row_lower, row_upper)
        y_anchor = y_half + y_dual
        image_gap = (images - image_duals).astype(jnp.bfloat16).reshape(-1, block_width)
        pulled = by_tile(image_gap, tile_matrix, tiles_here, 1, slot_total)
        x_columns = pick_blocks(x_own, cols_here, col_blocks, block_width)
        merged = (x_columns - input_duals + pulled).astype(jnp.bfloat16).reshape(-1, block_width)
        x_proj = by_tile(merged, tile_inverse, tiles_here, 0, slot_total)
        y_proj = by_tile(
            x_proj.astype(jnp.bfloat16).reshape(-1, block_width), tile_matrix, tiles_here, 0,
            slot_total,
        )
        x_terms = x_proj + input_duals
        y_terms = y_proj + image_duals
        col_terms = jnp.concatenate(
            [jnp.sum(jnp.where(m, x_terms, 0.0), axis=0) for m in col_mask], axis=1
        )
        row_terms = jnp.concatenate(
            [jnp.sum(jnp.where(m, y_terms, 0.0), axis=0) for m in row_mask], axis=1
        )
        if iteration == 0:
            slot_info = jnp.concatenate([cols_here, rows_here, block_count[0, 0][None]])
            col_total, row_total = all_reduce(
                [col_terms, row_terms], AXES, n_row, 0, block_width, slot_info
            )
            col_denom = 1.0 + col_total[scenarios : scenarios + 1]
            row_denom = 1.0 + row_total[scenarios : scenarios + 1]
            col_total = col_total[:scenarios]
            row_total = row_total[:scenarios]
        else:
            col_total, row_total = all_reduce([col_terms, row_terms], AXES, n_row, 1, block_width)
        x_own = (x_half + x_dual + col_total) / col_denom
        x_dual = x_dual + x_half - x_own
        shift_full = (row_total - y_anchor) / row_denom
        y_state = y_anchor + shift_full
        y_dual = y_dual + y_half - y_state
        input_duals = input_duals + x_proj - pick_blocks(x_own, cols_here, col_blocks, block_width)
        new_images = y_proj + image_duals - pick_blocks(shift_full, rows_here, row_blocks, block_width)
        image_duals = image_duals + y_proj - new_images
        images = new_images
    column_final = jnp.clip(x_own - x_dual - unit_cost, 0.0, capacity)
    row_final = jnp.clip(y_state - y_dual, row_lower, row_upper)
    return (column_final, row_final)


def solution(mesh):
    placed = (
        P(),
        P(),
        P("row", "col", None),
        P("row", "col", None),
        P("row", "col", None),
        P("row", "col"),
        P(None, "col"),
        P(None, "col"),
        P(None, "col"),
        P(None, "col"),
        P(None, "row"),
        P(None, "row"),
        P(None, "row"),
        P(None, "row"),
        P("row", "col", None, None, None),
        P("row", "col", None, None, None),
        P("row", "col", None, None, None),
    )
    return jax.shard_map(
        per_device,
        mesh=mesh,
        in_specs=placed,
        out_specs=(P(None, "col"), P(None, "row")),
        check_vma=False,
    )
```

```python
import functools

import jax
import jax.numpy as jnp
from jax import lax
from jax.experimental import pallas as pl
from jax.experimental.pallas import tpu as pltpu
from jax.sharding import PartitionSpec as P

ITERS = 2
MESH = pl.DeviceIdType.MESH
AXES = ("row", "col")


def peer_id(axis, peer):
    if axis == "row":
        return (peer, lax.axis_index("col"))
    return (lax.axis_index("row"), peer)


def reduce_kernel(n, group_axes, block_width, with_counts, *refs):
    groups = len(group_axes)
    if with_counts:
        info, refs = refs[0], refs[1:]
    ins = refs[:groups]
    outs = refs[groups : 2 * groups]
    scratch = refs[2 * groups :]
    size = 7 if with_counts else 6
    per = [scratch[size * g : size * g + 6] for g in range(groups)]
    width = ins[0].shape[1] // n
    sources = list(ins)

    def cols(index):
        return pl.ds(pl.multiple_of(index * width, width), width)

    def piece(ref, index):
        if len(ref.shape) == 3:
            return ref.at[index]
        return ref.at[:, cols(index)]

    if with_counts:
        slots = (info.shape[0] - 1) // groups
        live = info[groups * slots]
        for g in range(groups):
            send = scratch[size * g + 6]
            data_rows = ins[g].shape[0]
            extra = send.shape[1] - data_rows
            for p in range(n):
                block = (p * width) // block_width
                count = jnp.int32(0)
                for k in range(slots):
                    count = count + jnp.where(
                        (k < live) & (info[g * slots + k] == block), 1, 0
                    ).astype(jnp.int32)
                send[p, :data_rows, :] = ins[g][:, p * width : (p + 1) * width]
                send[p, data_rows:, :] = jnp.full((extra, width), count, jnp.int32).astype(
                    jnp.float32
                )
            sources[g] = send
    issue_order = sorted(range(groups), key=lambda g: group_axes[g] != "col")
    barrier = pltpu.get_barrier_semaphore()
    for axis in [group_axes[g] for g in issue_order]:
        me = lax.axis_index(axis)
        for k in range(1, n):
            peer = lax.rem(me + k, n)
            pl.semaphore_signal(barrier, inc=1, device_id=peer_id(axis, peer), device_id_type=MESH)
    pl.semaphore_wait(barrier, groups * (n - 1))

    far_first = sorted(range(1, n), key=lambda k: (-min(k, n - k), k))
    scatter = [None] * groups
    for g in issue_order:
        axis = group_axes[g]
        recv, gathered, s1, r1, s2, r2 = per[g]
        me = lax.axis_index(axis)
        copies = []
        for k in far_first:
            peer = lax.rem(me + k, n)
            copy = pltpu.make_async_remote_copy(
                src_ref=piece(sources[g], peer),
                dst_ref=recv.at[me],
                send_sem=s1.at[peer],
                recv_sem=r1.at[me],
                device_id=peer_id(axis, peer),
                device_id_type=MESH,
            )
            copy.start()
            copies.append(copy)
        scatter[g] = copies

    gathers = [None] * groups
    for g in issue_order:
        axis = group_axes[g]
        recv, gathered, s1, r1, s2, r2 = per[g]
        me = lax.axis_index(axis)
        for k in range(1, n):
            source = lax.rem(me + n - k, n)
            pltpu.make_async_remote_copy(
                src_ref=piece(sources[g], source),
                dst_ref=recv.at[source],
                send_sem=s1.at[source],
                recv_sem=r1.at[source],
                device_id=peer_id(axis, source),
                device_id_type=MESH,
            ).wait_recv()
        total = piece(sources[g], me)[...]
        for k in range(1, n):
            total = total + recv[lax.rem(me + k, n)]
        outs[g][:, cols(me)] = total
        copies = []
        for k in far_first:
            peer = lax.rem(me + k, n)
            copy = pltpu.make_async_remote_copy(
                src_ref=outs[g].at[:, cols(me)],
                dst_ref=outs[g].at[:, cols(me)],
                send_sem=s2.at[peer],
                recv_sem=r2.at[me],
                device_id=peer_id(axis, peer),
                device_id_type=MESH,
            )
            copy.start()
            copies.append(copy)
        gathers[g] = copies

    for g, axis in enumerate(group_axes):
        recv, gathered, s1, r1, s2, r2 = per[g]
        me = lax.axis_index(axis)
        for copy in scatter[g]:
            copy.wait_send()
        for k in range(1, n):
            source = lax.rem(me + n - k, n)
            pltpu.make_async_remote_copy(
                src_ref=outs[g].at[:, cols(source)],
                dst_ref=outs[g].at[:, cols(source)],
                send_sem=s2.at[source],
                recv_sem=r2.at[source],
                device_id=peer_id(axis, source),
                device_id_type=MESH,
            ).wait_recv()
        for copy in gathers[g]:
            copy.wait_send()


def all_reduce(arrays, group_axes, n, collective_id, block_width, info=None):
    extra = 0 if info is None else 8
    shapes = [(a.shape[0] + extra, a.shape[1]) for a in arrays]
    width = shapes[0][1] // n
    scratch = []
    for rows, _ in shapes:
        scratch += [
            pltpu.VMEM((n, rows, width), jnp.float32),
            pltpu.VMEM((n, rows, width), jnp.float32),
            pltpu.SemaphoreType.DMA((n,)),
            pltpu.SemaphoreType.DMA((n,)),
            pltpu.SemaphoreType.DMA((n,)),
            pltpu.SemaphoreType.DMA((n,)),
        ]
        if info is not None:
            scratch.append(pltpu.VMEM((n, rows, width), jnp.float32))
    in_specs = [pl.BlockSpec(memory_space=pltpu.VMEM)] * len(arrays)
    if info is not None:
        in_specs = [pl.BlockSpec(memory_space=pltpu.SMEM)] + in_specs
        arrays = [info] + arrays
    return pl.pallas_call(
        functools.partial(reduce_kernel, n, group_axes, block_width, info is not None),
        out_shape=tuple(jax.ShapeDtypeStruct(s, jnp.float32) for s in shapes),
        in_specs=in_specs,
        out_specs=tuple(pl.BlockSpec(memory_space=pltpu.VMEM) for _ in shapes),
        scratch_shapes=scratch,
        compiler_params=pltpu.CompilerParams(collective_id=collective_id, has_side_effects=True),
    )(*arrays)


def pick_blocks(full, index, blocks, block_width):
    chosen = full[None, :, :block_width]
    for b in range(1, blocks):
        chosen = jnp.where(
            (index == b)[:, None, None], full[None, :, b * block_width : (b + 1) * block_width], chosen
        )
    return chosen


def by_tile(stacked, matrices, tiles, contract, slots):
    results = [
        lax.dot_general(
            stacked, matrices[t], (((1,), (contract,)), ((), ())),
            preferred_element_type=jnp.float32,
        )
        for t in range(matrices.shape[0])
    ]
    chosen = results[0].reshape(slots, -1, stacked.shape[1])
    for t in range(1, len(results)):
        chosen = jnp.where(
            (tiles == t)[:, None, None], results[t].reshape(slots, -1, stacked.shape[1]), chosen
        )
    return chosen


def per_device(
    tile_matrix,
    tile_inverse,
    block_rows,
    block_cols,
    block_tiles,
    block_count,
    column_values,
    column_duals,
    unit_cost,
    capacity,
    row_values,
    row_duals,
    row_lower,
    row_upper,
    block_image,
    image_dual,
    input_dual,
):
    block_width = tile_matrix.shape[1]
    scenarios = column_values.shape[0]
    col_blocks = column_values.shape[1] // block_width
    row_blocks = row_values.shape[1] // block_width
    slot_total = block_rows.shape[2]
    n_row = lax.axis_size("row")
    rows_here = block_rows[0, 0]
    cols_here = block_cols[0, 0]
    tiles_here = block_tiles[0, 0]
    live_slot = jnp.arange(slot_total, dtype=jnp.int32) < block_count[0, 0]
    x_own = column_values
    x_dual = column_duals
    y_state = row_values
    y_dual = row_duals
    images = block_image[0, 0]
    image_duals = image_dual[0, 0]
    input_duals = input_dual[0, 0]
    col_mask = [(live_slot & (cols_here == b))[:, None, None] for b in range(col_blocks)]
    row_mask = [(live_slot & (rows_here == b))[:, None, None] for b in range(row_blocks)]
    col_denom = None
    row_denom = None
    for iteration in range(ITERS):
        x_half = jnp.clip(x_own - x_dual - unit_cost, 0.0, capacity)
        y_half = jnp.clip(y_state - y_dual, row_lower, row_upper)
        y_anchor = y_half + y_dual
        image_gap = (images - image_duals).astype(jnp.bfloat16).reshape(-1, block_width)
        pulled = by_tile(image_gap, tile_matrix, tiles_here, 1, slot_total)
        x_columns = pick_blocks(x_own, cols_here, col_blocks, block_width)
        merged = (x_columns - input_duals + pulled).astype(jnp.bfloat16).reshape(-1, block_width)
        x_proj = by_tile(merged, tile_inverse, tiles_here, 0, slot_total)
        y_proj = by_tile(
            x_proj.astype(jnp.bfloat16).reshape(-1, block_width), tile_matrix, tiles_here, 0,
            slot_total,
        )
        x_terms = x_proj + input_duals
        y_terms = y_proj + image_duals
        col_terms = jnp.concatenate(
            [jnp.sum(jnp.where(m, x_terms, 0.0), axis=0) for m in col_mask], axis=1
        )
        row_terms = jnp.concatenate(
            [jnp.sum(jnp.where(m, y_terms, 0.0), axis=0) for m in row_mask], axis=1
        )
        if iteration == 0:
            slot_info = jnp.concatenate([cols_here, rows_here, block_count[0, 0][None]])
            col_total, row_total = all_reduce(
                [col_terms, row_terms], AXES, n_row, 0, block_width, slot_info
            )
            col_denom = 1.0 + col_total[scenarios : scenarios + 1]
            row_denom = 1.0 + row_total[scenarios : scenarios + 1]
            col_total = col_total[:scenarios]
            row_total = row_total[:scenarios]
        else:
            col_total, row_total = all_reduce([col_terms, row_terms], AXES, n_row, 1, block_width)
        x_own = (x_half + x_dual + col_total) / col_denom
        x_dual = x_dual + x_half - x_own
        shift_full = (row_total - y_anchor) / row_denom
        y_state = y_anchor + shift_full
        y_dual = y_dual + y_half - y_state
        input_duals = input_duals + x_proj - pick_blocks(x_own, cols_here, col_blocks, block_width)
        new_images = y_proj + image_duals - pick_blocks(shift_full, rows_here, row_blocks, block_width)
        image_duals = image_duals + y_proj - new_images
        images = new_images
    column_final = jnp.clip(x_own - x_dual - unit_cost, 0.0, capacity)
    row_final = jnp.clip(y_state - y_dual, row_lower, row_upper)
    return (column_final, row_final)


def solution(mesh):
    placed = (
        P(),
        P(),
        P("row", "col", None),
        P("row", "col", None),
        P("row", "col", None),
        P("row", "col"),
        P(None, "col"),
        P(None, "col"),
        P(None, "col"),
        P(None, "col"),
        P(None, "row"),
        P(None, "row"),
        P(None, "row"),
        P(None, "row"),
        P("row", "col", None, None, None),
        P("row", "col", None, None, None),
        P("row", "col", None, None, None),
    )
    return jax.shard_map(
        per_device,
        mesh=mesh,
        in_specs=placed,
        out_specs=(P(None, "col"), P(None, "row")),
        check_vma=False,
    )
```

```python
import functools

import jax
import jax.numpy as jnp
from jax import lax
from jax.experimental import pallas as pl
from jax.experimental.pallas import tpu as pltpu
from jax.sharding import PartitionSpec as P

ITERS = 2
MESH = pl.DeviceIdType.MESH
AXES = ("row", "col")


def peer_id(axis, peer):
    if axis == "row":
        return (peer, lax.axis_index("col"))
    return (lax.axis_index("row"), peer)


def reduce_kernel(n, group_axes, block_width, with_counts, *refs):
    groups = len(group_axes)
    if with_counts:
        info, refs = refs[0], refs[1:]
    ins = refs[:groups]
    outs = refs[groups : 2 * groups]
    scratch = refs[2 * groups :]
    size = 7 if with_counts else 6
    per = [scratch[size * g : size * g + 6] for g in range(groups)]
    width = ins[0].shape[1] // n
    sources = list(ins)

    def cols(index):
        return pl.ds(pl.multiple_of(index * width, width), width)

    def piece(ref, index):
        if len(ref.shape) == 3:
            return ref.at[index]
        return ref.at[:, cols(index)]

    if with_counts:
        slots = (info.shape[0] - 1) // groups
        live = info[groups * slots]
        for g in range(groups):
            send = scratch[size * g + 6]
            data_rows = ins[g].shape[0]
            extra = send.shape[1] - data_rows
            for p in range(n):
                block = (p * width) // block_width
                count = jnp.int32(0)
                for k in range(slots):
                    count = count + jnp.where(
                        (k < live) & (info[g * slots + k] == block), 1, 0
                    ).astype(jnp.int32)
                send[p, :data_rows, :] = ins[g][:, p * width : (p + 1) * width]
                send[p, data_rows:, :] = jnp.full((extra, width), count, jnp.int32).astype(
                    jnp.float32
                )
            sources[g] = send
    issue_order = sorted(range(groups), key=lambda g: group_axes[g] != "col")
    barrier = pltpu.get_barrier_semaphore()
    for axis in [group_axes[g] for g in issue_order]:
        me = lax.axis_index(axis)
        for k in range(1, n):
            peer = lax.rem(me + k, n)
            pl.semaphore_signal(barrier, inc=1, device_id=peer_id(axis, peer), device_id_type=MESH)
    pl.semaphore_wait(barrier, groups * (n - 1))

    def rows_of(g):
        total_rows = outs[g].shape[0]
        first = ((total_rows // 2 + 7) // 8) * 8
        return [(0, first), (first, total_rows - first)]

    def part(ref, index, start, count):
        if len(ref.shape) == 3:
            return ref.at[index, pl.ds(start, count)]
        return ref.at[pl.ds(start, count), cols(index)]

    scatter = [None] * groups
    for g in issue_order:
        axis = group_axes[g]
        recv, gathered, s1, r1, s2, r2 = per[g]
        me = lax.axis_index(axis)
        copies = []
        for h, (start, count) in enumerate(rows_of(g)):
            for k in range(1, n):
                peer = lax.rem(me + k, n)
                copy = pltpu.make_async_remote_copy(
                    src_ref=part(sources[g], peer, start, count),
                    dst_ref=recv.at[me, pl.ds(start, count)],
                    send_sem=s1.at[h, peer],
                    recv_sem=r1.at[h, me],
                    device_id=peer_id(axis, peer),
                    device_id_type=MESH,
                )
                copy.start()
                copies.append(copy)
        scatter[g] = copies

    gathers = [None] * groups
    for g in issue_order:
        axis = group_axes[g]
        recv, gathered, s1, r1, s2, r2 = per[g]
        me = lax.axis_index(axis)
        copies = []
        for h, (start, count) in enumerate(rows_of(g)):
            for k in range(1, n):
                source = lax.rem(me + n - k, n)
                pltpu.make_async_remote_copy(
                    src_ref=part(sources[g], source, start, count),
                    dst_ref=recv.at[source, pl.ds(start, count)],
                    send_sem=s1.at[h, source],
                    recv_sem=r1.at[h, source],
                    device_id=peer_id(axis, source),
                    device_id_type=MESH,
                ).wait_recv()
            total = part(sources[g], me, start, count)[...]
            for k in range(1, n):
                total = total + recv[lax.rem(me + k, n), start : start + count, :]
            outs[g][start : start + count, cols(me)] = total
            for k in range(1, n):
                peer = lax.rem(me + k, n)
                copy = pltpu.make_async_remote_copy(
                    src_ref=part(outs[g], me, start, count),
                    dst_ref=part(outs[g], me, start, count),
                    send_sem=s2.at[h, peer],
                    recv_sem=r2.at[h, me],
                    device_id=peer_id(axis, peer),
                    device_id_type=MESH,
                )
                copy.start()
                copies.append(copy)
        gathers[g] = copies

    for g, axis in enumerate(group_axes):
        recv, gathered, s1, r1, s2, r2 = per[g]
        me = lax.axis_index(axis)
        for copy in scatter[g]:
            copy.wait_send()
        for h, (start, count) in enumerate(rows_of(g)):
            for k in range(1, n):
                source = lax.rem(me + n - k, n)
                pltpu.make_async_remote_copy(
                    src_ref=part(outs[g], source, start, count),
                    dst_ref=part(outs[g], source, start, count),
                    send_sem=s2.at[h, source],
                    recv_sem=r2.at[h, source],
                    device_id=peer_id(axis, source),
                    device_id_type=MESH,
                ).wait_recv()
        for copy in gathers[g]:
            copy.wait_send()


def all_reduce(arrays, group_axes, n, collective_id, block_width, info=None):
    extra = 0 if info is None else 8
    shapes = [(a.shape[0] + extra, a.shape[1]) for a in arrays]
    width = shapes[0][1] // n
    scratch = []
    for rows, _ in shapes:
        scratch += [
            pltpu.VMEM((n, rows, width), jnp.float32),
            pltpu.VMEM((n, rows, width), jnp.float32),
            pltpu.SemaphoreType.DMA((2, n)),
            pltpu.SemaphoreType.DMA((2, n)),
            pltpu.SemaphoreType.DMA((2, n)),
            pltpu.SemaphoreType.DMA((2, n)),
        ]
        if info is not None:
            scratch.append(pltpu.VMEM((n, rows, width), jnp.float32))
    in_specs = [pl.BlockSpec(memory_space=pltpu.VMEM)] * len(arrays)
    if info is not None:
        in_specs = [pl.BlockSpec(memory_space=pltpu.SMEM)] + in_specs
        arrays = [info] + arrays
    return pl.pallas_call(
        functools.partial(reduce_kernel, n, group_axes, block_width, info is not None),
        out_shape=tuple(jax.ShapeDtypeStruct(s, jnp.float32) for s in shapes),
        in_specs=in_specs,
        out_specs=tuple(pl.BlockSpec(memory_space=pltpu.VMEM) for _ in shapes),
        scratch_shapes=scratch,
        compiler_params=pltpu.CompilerParams(collective_id=collective_id, has_side_effects=True),
    )(*arrays)


def pick_blocks(full, index, blocks, block_width):
    chosen = full[None, :, :block_width]
    for b in range(1, blocks):
        chosen = jnp.where(
            (index == b)[:, None, None], full[None, :, b * block_width : (b + 1) * block_width], chosen
        )
    return chosen


def by_tile(stacked, matrices, tiles, contract, slots):
    results = [
        lax.dot_general(
            stacked, matrices[t], (((1,), (contract,)), ((), ())),
            preferred_element_type=jnp.float32,
        )
        for t in range(matrices.shape[0])
    ]
    chosen = results[0].reshape(slots, -1, stacked.shape[1])
    for t in range(1, len(results)):
        chosen = jnp.where(
            (tiles == t)[:, None, None], results[t].reshape(slots, -1, stacked.shape[1]), chosen
        )
    return chosen


def per_device(
    tile_matrix,
    tile_inverse,
    block_rows,
    block_cols,
    block_tiles,
    block_count,
    column_values,
    column_duals,
    unit_cost,
    capacity,
    row_values,
    row_duals,
    row_lower,
    row_upper,
    block_image,
    image_dual,
    input_dual,
):
    block_width = tile_matrix.shape[1]
    scenarios = column_values.shape[0]
    col_blocks = column_values.shape[1] // block_width
    row_blocks = row_values.shape[1] // block_width
    slot_total = block_rows.shape[2]
    n_row = lax.axis_size("row")
    rows_here = block_rows[0, 0]
    cols_here = block_cols[0, 0]
    tiles_here = block_tiles[0, 0]
    live_slot = jnp.arange(slot_total, dtype=jnp.int32) < block_count[0, 0]
    x_own = column_values
    x_dual = column_duals
    y_state = row_values
    y_dual = row_duals
    images = block_image[0, 0]
    image_duals = image_dual[0, 0]
    input_duals = input_dual[0, 0]
    col_mask = [(live_slot & (cols_here == b))[:, None, None] for b in range(col_blocks)]
    row_mask = [(live_slot & (rows_here == b))[:, None, None] for b in range(row_blocks)]
    col_denom = None
    row_denom = None
    for iteration in range(ITERS):
        x_half = jnp.clip(x_own - x_dual - unit_cost, 0.0, capacity)
        y_half = jnp.clip(y_state - y_dual, row_lower, row_upper)
        y_anchor = y_half + y_dual
        image_gap = (images - image_duals).astype(jnp.bfloat16).reshape(-1, block_width)
        pulled = by_tile(image_gap, tile_matrix, tiles_here, 1, slot_total)
        x_columns = pick_blocks(x_own, cols_here, col_blocks, block_width)
        merged = (x_columns - input_duals + pulled).astype(jnp.bfloat16).reshape(-1, block_width)
        x_proj = by_tile(merged, tile_inverse, tiles_here, 0, slot_total)
        y_proj = by_tile(
            x_proj.astype(jnp.bfloat16).reshape(-1, block_width), tile_matrix, tiles_here, 0,
            slot_total,
        )
        x_terms = x_proj + input_duals
        y_terms = y_proj + image_duals
        col_terms = jnp.concatenate(
            [jnp.sum(jnp.where(m, x_terms, 0.0), axis=0) for m in col_mask], axis=1
        )
        row_terms = jnp.concatenate(
            [jnp.sum(jnp.where(m, y_terms, 0.0), axis=0) for m in row_mask], axis=1
        )
        if iteration == 0:
            slot_info = jnp.concatenate([cols_here, rows_here, block_count[0, 0][None]])
            col_total, row_total = all_reduce(
                [col_terms, row_terms], AXES, n_row, 0, block_width, slot_info
            )
            col_denom = 1.0 + col_total[scenarios : scenarios + 1]
            row_denom = 1.0 + row_total[scenarios : scenarios + 1]
            col_total = col_total[:scenarios]
            row_total = row_total[:scenarios]
        else:
            col_total, row_total = all_reduce([col_terms, row_terms], AXES, n_row, 1, block_width)
        x_own = (x_half + x_dual + col_total) / col_denom
        x_dual = x_dual + x_half - x_own
        shift_full = (row_total - y_anchor) / row_denom
        y_state = y_anchor + shift_full
        y_dual = y_dual + y_half - y_state
        input_duals = input_duals + x_proj - pick_blocks(x_own, cols_here, col_blocks, block_width)
        new_images = y_proj + image_duals - pick_blocks(shift_full, rows_here, row_blocks, block_width)
        image_duals = image_duals + y_proj - new_images
        images = new_images
    column_final = jnp.clip(x_own - x_dual - unit_cost, 0.0, capacity)
    row_final = jnp.clip(y_state - y_dual, row_lower, row_upper)
    return (column_final, row_final)


def solution(mesh):
    placed = (
        P(),
        P(),
        P("row", "col", None),
        P("row", "col", None),
        P("row", "col", None),
        P("row", "col"),
        P(None, "col"),
        P(None, "col"),
        P(None, "col"),
        P(None, "col"),
        P(None, "row"),
        P(None, "row"),
        P(None, "row"),
        P(None, "row"),
        P("row", "col", None, None, None),
        P("row", "col", None, None, None),
        P("row", "col", None, None, None),
    )
    return jax.shard_map(
        per_device,
        mesh=mesh,
        in_specs=placed,
        out_specs=(P(None, "col"), P(None, "row")),
        check_vma=False,
    )
```

```python
import functools

import jax
import jax.numpy as jnp
from jax import lax
from jax.experimental import pallas as pl
from jax.experimental.pallas import tpu as pltpu
from jax.sharding import PartitionSpec as P

ITERS = 2
MESH = pl.DeviceIdType.MESH
AXES = ("row", "col")


def peer_id(axis, peer):
    if axis == "row":
        return (peer, lax.axis_index("col"))
    return (lax.axis_index("row"), peer)


def reduce_kernel(n, group_axes, block_width, with_counts, *refs):
    groups = len(group_axes)
    if with_counts:
        info, live_ref, refs = refs[:groups], refs[groups], refs[groups + 1 :]
    ins = refs[:groups]
    outs = refs[groups : 2 * groups]
    scratch = refs[2 * groups :]
    size = 7 if with_counts else 6
    per = [scratch[size * g : size * g + 6] for g in range(groups)]
    width = ins[0].shape[1] // n
    sources = list(ins)

    def cols(index):
        return pl.ds(pl.multiple_of(index * width, width), width)

    def piece(ref, index):
        if len(ref.shape) == 3:
            return ref.at[index]
        return ref.at[:, cols(index)]

    if with_counts:
        slots = info[0].shape[0]
        live = live_ref[0]
        for g in range(groups):
            send = scratch[size * g + 6]
            data_rows = ins[g].shape[0]
            extra = send.shape[1] - data_rows
            for p in range(n):
                block = (p * width) // block_width
                count = jnp.int32(0)
                for k in range(slots):
                    count = count + jnp.where(
                        (k < live) & (info[g][k] == block), 1, 0
                    ).astype(jnp.int32)
                send[p, :data_rows, :] = ins[g][:, p * width : (p + 1) * width]
                send[p, data_rows:, :] = jnp.full((extra, width), count, jnp.int32).astype(
                    jnp.float32
                )
            sources[g] = send
    issue_order = sorted(range(groups), key=lambda g: group_axes[g] != "col")
    barrier = pltpu.get_barrier_semaphore()
    for axis in [group_axes[g] for g in issue_order]:
        me = lax.axis_index(axis)
        for k in range(1, n):
            peer = lax.rem(me + k, n)
            pl.semaphore_signal(barrier, inc=1, device_id=peer_id(axis, peer), device_id_type=MESH)
    pl.semaphore_wait(barrier, groups * (n - 1))

    scatter = [None] * groups
    for g in issue_order:
        axis = group_axes[g]
        recv, gathered, s1, r1, s2, r2 = per[g]
        me = lax.axis_index(axis)
        copies = []
        for k in range(1, n):
            peer = lax.rem(me + k, n)
            copy = pltpu.make_async_remote_copy(
                src_ref=piece(sources[g], peer),
                dst_ref=recv.at[me],
                send_sem=s1.at[peer],
                recv_sem=r1.at[me],
                device_id=peer_id(axis, peer),
                device_id_type=MESH,
            )
            copy.start()
            copies.append(copy)
        scatter[g] = copies

    gathers = [None] * groups
    for g in issue_order:
        axis = group_axes[g]
        recv, gathered, s1, r1, s2, r2 = per[g]
        me = lax.axis_index(axis)
        for k in range(1, n):
            source = lax.rem(me + n - k, n)
            pltpu.make_async_remote_copy(
                src_ref=piece(sources[g], source),
                dst_ref=recv.at[source],
                send_sem=s1.at[source],
                recv_sem=r1.at[source],
                device_id=peer_id(axis, source),
                device_id_type=MESH,
            ).wait_recv()
        total = piece(sources[g], me)[...]
        for k in range(1, n):
            total = total + recv[lax.rem(me + k, n)]
        outs[g][:, cols(me)] = total
        copies = []
        for k in range(1, n):
            peer = lax.rem(me + k, n)
            copy = pltpu.make_async_remote_copy(
                src_ref=outs[g].at[:, cols(me)],
                dst_ref=outs[g].at[:, cols(me)],
                send_sem=s2.at[peer],
                recv_sem=r2.at[me],
                device_id=peer_id(axis, peer),
                device_id_type=MESH,
            )
            copy.start()
            copies.append(copy)
        gathers[g] = copies

    for g, axis in enumerate(group_axes):
        recv, gathered, s1, r1, s2, r2 = per[g]
        me = lax.axis_index(axis)
        for copy in scatter[g]:
            copy.wait_send()
        for k in range(1, n):
            source = lax.rem(me + n - k, n)
            pltpu.make_async_remote_copy(
                src_ref=outs[g].at[:, cols(source)],
                dst_ref=outs[g].at[:, cols(source)],
                send_sem=s2.at[source],
                recv_sem=r2.at[source],
                device_id=peer_id(axis, source),
                device_id_type=MESH,
            ).wait_recv()
        for copy in gathers[g]:
            copy.wait_send()


def all_reduce(arrays, group_axes, n, collective_id, block_width, info=None):
    extra = 0 if info is None else 8
    shapes = [(a.shape[0] + extra, a.shape[1]) for a in arrays]
    width = shapes[0][1] // n
    scratch = []
    for rows, _ in shapes:
        scratch += [
            pltpu.VMEM((n, rows, width), jnp.float32),
            pltpu.VMEM((n, rows, width), jnp.float32),
            pltpu.SemaphoreType.DMA((n,)),
            pltpu.SemaphoreType.DMA((n,)),
            pltpu.SemaphoreType.DMA((n,)),
            pltpu.SemaphoreType.DMA((n,)),
        ]
        if info is not None:
            scratch.append(pltpu.VMEM((n, rows, width), jnp.float32))
    in_specs = [pl.BlockSpec(memory_space=pltpu.VMEM)] * len(arrays)
    if info is not None:
        in_specs = [pl.BlockSpec(memory_space=pltpu.SMEM)] * len(info) + in_specs
        arrays = list(info) + arrays
    return pl.pallas_call(
        functools.partial(reduce_kernel, n, group_axes, block_width, info is not None),
        out_shape=tuple(jax.ShapeDtypeStruct(s, jnp.float32) for s in shapes),
        in_specs=in_specs,
        out_specs=tuple(pl.BlockSpec(memory_space=pltpu.VMEM) for _ in shapes),
        scratch_shapes=scratch,
        compiler_params=pltpu.CompilerParams(collective_id=collective_id, has_side_effects=True),
    )(*arrays)


def pick_blocks(full, index, blocks, block_width):
    chosen = full[None, :, :block_width]
    for b in range(1, blocks):
        chosen = jnp.where(
            (index == b)[:, None, None], full[None, :, b * block_width : (b + 1) * block_width], chosen
        )
    return chosen


def by_tile(stacked, matrices, tiles, contract, slots):
    results = [
        lax.dot_general(
            stacked, matrices[t], (((1,), (contract,)), ((), ())),
            preferred_element_type=jnp.float32,
        )
        for t in range(matrices.shape[0])
    ]
    chosen = results[0].reshape(slots, -1, stacked.shape[1])
    for t in range(1, len(results)):
        chosen = jnp.where(
            (tiles == t)[:, None, None], results[t].reshape(slots, -1, stacked.shape[1]), chosen
        )
    return chosen


def per_device(
    tile_matrix,
    tile_inverse,
    block_rows,
    block_cols,
    block_tiles,
    block_count,
    column_values,
    column_duals,
    unit_cost,
    capacity,
    row_values,
    row_duals,
    row_lower,
    row_upper,
    block_image,
    image_dual,
    input_dual,
):
    block_width = tile_matrix.shape[1]
    scenarios = column_values.shape[0]
    col_blocks = column_values.shape[1] // block_width
    row_blocks = row_values.shape[1] // block_width
    slot_total = block_rows.shape[2]
    n_row = lax.axis_size("row")
    rows_here = block_rows[0, 0]
    cols_here = block_cols[0, 0]
    tiles_here = block_tiles[0, 0]
    live_slot = jnp.arange(slot_total, dtype=jnp.int32) < block_count[0, 0]
    x_own = column_values
    x_dual = column_duals
    y_state = row_values
    y_dual = row_duals
    images = block_image[0, 0]
    image_duals = image_dual[0, 0]
    input_duals = input_dual[0, 0]
    col_mask = [(live_slot & (cols_here == b))[:, None, None] for b in range(col_blocks)]
    row_mask = [(live_slot & (rows_here == b))[:, None, None] for b in range(row_blocks)]
    col_denom = None
    row_denom = None
    for iteration in range(ITERS):
        x_half = jnp.clip(x_own - x_dual - unit_cost, 0.0, capacity)
        y_half = jnp.clip(y_state - y_dual, row_lower, row_upper)
        y_anchor = y_half + y_dual
        image_gap = (images - image_duals).astype(jnp.bfloat16).reshape(-1, block_width)
        pulled = by_tile(image_gap, tile_matrix, tiles_here, 1, slot_total)
        x_columns = pick_blocks(x_own, cols_here, col_blocks, block_width)
        merged = (x_columns - input_duals + pulled).astype(jnp.bfloat16).reshape(-1, block_width)
        x_proj = by_tile(merged, tile_inverse, tiles_here, 0, slot_total)
        y_proj = by_tile(
            x_proj.astype(jnp.bfloat16).reshape(-1, block_width), tile_matrix, tiles_here, 0,
            slot_total,
        )
        x_terms = x_proj + input_duals
        y_terms = y_proj + image_duals
        col_terms = jnp.concatenate(
            [jnp.sum(jnp.where(m, x_terms, 0.0), axis=0) for m in col_mask], axis=1
        )
        row_terms = jnp.concatenate(
            [jnp.sum(jnp.where(m, y_terms, 0.0), axis=0) for m in row_mask], axis=1
        )
        if iteration == 0:
            slot_info = [cols_here, rows_here, block_count.reshape(1)]
            col_total, row_total = all_reduce(
                [col_terms, row_terms], AXES, n_row, 0, block_width, slot_info
            )
            col_denom = 1.0 + col_total[scenarios : scenarios + 1]
            row_denom = 1.0 + row_total[scenarios : scenarios + 1]
            col_total = col_total[:scenarios]
            row_total = row_total[:scenarios]
        else:
            col_total, row_total = all_reduce([col_terms, row_terms], AXES, n_row, 1, block_width)
        x_own = (x_half + x_dual + col_total) / col_denom
        x_dual = x_dual + x_half - x_own
        shift_full = (row_total - y_anchor) / row_denom
        y_state = y_anchor + shift_full
        y_dual = y_dual + y_half - y_state
        input_duals = input_duals + x_proj - pick_blocks(x_own, cols_here, col_blocks, block_width)
        new_images = y_proj + image_duals - pick_blocks(shift_full, rows_here, row_blocks, block_width)
        image_duals = image_duals + y_proj - new_images
        images = new_images
    column_final = jnp.clip(x_own - x_dual - unit_cost, 0.0, capacity)
    row_final = jnp.clip(y_state - y_dual, row_lower, row_upper)
    return (column_final, row_final)


def solution(mesh):
    placed = (
        P(),
        P(),
        P("row", "col", None),
        P("row", "col", None),
        P("row", "col", None),
        P("row", "col"),
        P(None, "col"),
        P(None, "col"),
        P(None, "col"),
        P(None, "col"),
        P(None, "row"),
        P(None, "row"),
        P(None, "row"),
        P(None, "row"),
        P("row", "col", None, None, None),
        P("row", "col", None, None, None),
        P("row", "col", None, None, None),
    )
    return jax.shard_map(
        per_device,
        mesh=mesh,
        in_specs=placed,
        out_specs=(P(None, "col"), P(None, "row")),
        check_vma=False,
    )
```

```python
import functools

import jax
import jax.numpy as jnp
from jax import lax
from jax.experimental import pallas as pl
from jax.experimental.pallas import tpu as pltpu
from jax.sharding import PartitionSpec as P

ITERS = 2
MESH = pl.DeviceIdType.MESH
AXES = ("row", "col")


def peer_id(axis, peer):
    if axis == "row":
        return (peer, lax.axis_index("col"))
    return (lax.axis_index("row"), peer)


def reduce_kernel(n, group_axes, block_width, with_counts, *refs):
    groups = len(group_axes)
    if with_counts:
        info, live_ref, refs = refs[:groups], refs[groups], refs[groups + 1 :]
    ins = refs[:groups]
    outs = refs[groups : 2 * groups]
    scratch = refs[2 * groups :]
    size = 7 if with_counts else 6
    per = [scratch[size * g : size * g + 6] for g in range(groups)]
    width = ins[0].shape[1] // n
    sources = list(ins)

    def cols(index):
        return pl.ds(pl.multiple_of(index * width, width), width)

    def piece(ref, index):
        if len(ref.shape) == 3:
            return ref.at[index]
        return ref.at[:, cols(index)]

    if with_counts:
        slots = info[0].shape[0]
        live = live_ref[0]
        for g in range(groups):
            send = scratch[size * g + 6]
            data_rows = ins[g].shape[0]
            extra = send.shape[1] - data_rows
            for p in range(n):
                block = (p * width) // block_width
                count = jnp.int32(0)
                for k in range(slots):
                    count = count + jnp.where(
                        (k < live) & (info[g][k] == block), 1, 0
                    ).astype(jnp.int32)
                send[p, :data_rows, :] = ins[g][:, p * width : (p + 1) * width]
                send[p, data_rows:, :] = jnp.full((extra, width), count, jnp.int32).astype(
                    jnp.float32
                )
            sources[g] = send
    issue_order = sorted(range(groups), key=lambda g: group_axes[g] != "col")
    barrier = pltpu.get_barrier_semaphore()
    for axis in [group_axes[g] for g in issue_order]:
        me = lax.axis_index(axis)
        for k in range(1, n):
            peer = lax.rem(me + k, n)
            pl.semaphore_signal(barrier, inc=1, device_id=peer_id(axis, peer), device_id_type=MESH)
    pl.semaphore_wait(barrier, groups * (n - 1))

    scatter = [None] * groups
    for g in issue_order:
        axis = group_axes[g]
        recv, gathered, s1, r1, s2, r2 = per[g]
        me = lax.axis_index(axis)
        copies = []
        for k in range(1, n):
            peer = lax.rem(me + k, n)
            copy = pltpu.make_async_remote_copy(
                src_ref=piece(sources[g], peer),
                dst_ref=recv.at[me],
                send_sem=s1.at[peer],
                recv_sem=r1.at[me],
                device_id=peer_id(axis, peer),
                device_id_type=MESH,
            )
            copy.start()
            copies.append(copy)
        scatter[g] = copies

    gathers = [None] * groups
    for g in issue_order:
        axis = group_axes[g]
        recv, gathered, s1, r1, s2, r2 = per[g]
        me = lax.axis_index(axis)
        for k in range(1, n):
            source = lax.rem(me + n - k, n)
            pltpu.make_async_remote_copy(
                src_ref=piece(sources[g], source),
                dst_ref=recv.at[source],
                send_sem=s1.at[source],
                recv_sem=r1.at[source],
                device_id=peer_id(axis, source),
                device_id_type=MESH,
            ).wait_recv()
        total = piece(sources[g], me)[...]
        for k in range(1, n):
            total = total + recv[lax.rem(me + k, n)]
        outs[g][:, cols(me)] = total
        copies = []
        for k in range(1, n):
            peer = lax.rem(me + k, n)
            copy = pltpu.make_async_remote_copy(
                src_ref=outs[g].at[:, cols(me)],
                dst_ref=outs[g].at[:, cols(me)],
                send_sem=s2.at[peer],
                recv_sem=r2.at[me],
                device_id=peer_id(axis, peer),
                device_id_type=MESH,
            )
            copy.start()
            copies.append(copy)
        gathers[g] = copies

    for g, axis in enumerate(group_axes):
        recv, gathered, s1, r1, s2, r2 = per[g]
        me = lax.axis_index(axis)
        for copy in scatter[g]:
            copy.wait_send()
        for k in range(1, n):
            source = lax.rem(me + n - k, n)
            pltpu.make_async_remote_copy(
                src_ref=outs[g].at[:, cols(source)],
                dst_ref=outs[g].at[:, cols(source)],
                send_sem=s2.at[source],
                recv_sem=r2.at[source],
                device_id=peer_id(axis, source),
                device_id_type=MESH,
            ).wait_recv()
        for copy in gathers[g]:
            copy.wait_send()


def all_reduce(arrays, group_axes, n, collective_id, block_width, info=None):
    extra = 0 if info is None else 8
    shapes = [(a.shape[0] + extra, a.shape[1]) for a in arrays]
    width = shapes[0][1] // n
    scratch = []
    for rows, _ in shapes:
        scratch += [
            pltpu.VMEM((n, rows, width), jnp.float32),
            pltpu.VMEM((n, rows, width), jnp.float32),
            pltpu.SemaphoreType.DMA((n,)),
            pltpu.SemaphoreType.DMA((n,)),
            pltpu.SemaphoreType.DMA((n,)),
            pltpu.SemaphoreType.DMA((n,)),
        ]
        if info is not None:
            scratch.append(pltpu.VMEM((n, rows, width), jnp.float32))
    in_specs = [pl.BlockSpec(memory_space=pltpu.VMEM)] * len(arrays)
    if info is not None:
        in_specs = [pl.BlockSpec(memory_space=pltpu.SMEM)] * len(info) + in_specs
        arrays = list(info) + arrays
    return pl.pallas_call(
        functools.partial(reduce_kernel, n, group_axes, block_width, info is not None),
        out_shape=tuple(jax.ShapeDtypeStruct(s, jnp.float32) for s in shapes),
        in_specs=in_specs,
        out_specs=tuple(pl.BlockSpec(memory_space=pltpu.VMEM) for _ in shapes),
        scratch_shapes=scratch,
        compiler_params=pltpu.CompilerParams(
            collective_id=collective_id, has_side_effects=True, vmem_limit_bytes=16 * 1024 * 1024
        ),
    )(*arrays)


def pick_blocks(full, index, blocks, block_width):
    chosen = full[None, :, :block_width]
    for b in range(1, blocks):
        chosen = jnp.where(
            (index == b)[:, None, None], full[None, :, b * block_width : (b + 1) * block_width], chosen
        )
    return chosen


def by_tile(stacked, matrices, tiles, contract, slots):
    results = [
        lax.dot_general(
            stacked, matrices[t], (((1,), (contract,)), ((), ())),
            preferred_element_type=jnp.float32,
        )
        for t in range(matrices.shape[0])
    ]
    chosen = results[0].reshape(slots, -1, stacked.shape[1])
    for t in range(1, len(results)):
        chosen = jnp.where(
            (tiles == t)[:, None, None], results[t].reshape(slots, -1, stacked.shape[1]), chosen
        )
    return chosen


def per_device(
    tile_matrix,
    tile_inverse,
    block_rows,
    block_cols,
    block_tiles,
    block_count,
    column_values,
    column_duals,
    unit_cost,
    capacity,
    row_values,
    row_duals,
    row_lower,
    row_upper,
    block_image,
    image_dual,
    input_dual,
):
    block_width = tile_matrix.shape[1]
    scenarios = column_values.shape[0]
    col_blocks = column_values.shape[1] // block_width
    row_blocks = row_values.shape[1] // block_width
    slot_total = block_rows.shape[2]
    n_row = lax.axis_size("row")
    rows_here = block_rows[0, 0]
    cols_here = block_cols[0, 0]
    tiles_here = block_tiles[0, 0]
    live_slot = jnp.arange(slot_total, dtype=jnp.int32) < block_count[0, 0]
    x_own = column_values
    x_dual = column_duals
    y_state = row_values
    y_dual = row_duals
    images = block_image[0, 0]
    image_duals = image_dual[0, 0]
    input_duals = input_dual[0, 0]
    col_mask = [(live_slot & (cols_here == b))[:, None, None] for b in range(col_blocks)]
    row_mask = [(live_slot & (rows_here == b))[:, None, None] for b in range(row_blocks)]
    col_denom = None
    row_denom = None
    for iteration in range(ITERS):
        x_half = jnp.clip(x_own - x_dual - unit_cost, 0.0, capacity)
        y_half = jnp.clip(y_state - y_dual, row_lower, row_upper)
        y_anchor = y_half + y_dual
        image_gap = (images - image_duals).astype(jnp.bfloat16).reshape(-1, block_width)
        pulled = by_tile(image_gap, tile_matrix, tiles_here, 1, slot_total)
        x_columns = pick_blocks(x_own, cols_here, col_blocks, block_width)
        merged = (x_columns - input_duals + pulled).astype(jnp.bfloat16).reshape(-1, block_width)
        x_proj = by_tile(merged, tile_inverse, tiles_here, 0, slot_total)
        y_proj = by_tile(
            x_proj.astype(jnp.bfloat16).reshape(-1, block_width), tile_matrix, tiles_here, 0,
            slot_total,
        )
        x_terms = x_proj + input_duals
        y_terms = y_proj + image_duals
        col_terms = jnp.concatenate(
            [jnp.sum(jnp.where(m, x_terms, 0.0), axis=0) for m in col_mask], axis=1
        )
        row_terms = jnp.concatenate(
            [jnp.sum(jnp.where(m, y_terms, 0.0), axis=0) for m in row_mask], axis=1
        )
        if iteration == 0:
            slot_info = [cols_here, rows_here, block_count.reshape(1)]
            col_total, row_total = all_reduce(
                [col_terms, row_terms], AXES, n_row, 0, block_width, slot_info
            )
            col_denom = 1.0 + col_total[scenarios : scenarios + 1]
            row_denom = 1.0 + row_total[scenarios : scenarios + 1]
            col_total = col_total[:scenarios]
            row_total = row_total[:scenarios]
        else:
            col_total, row_total = all_reduce([col_terms, row_terms], AXES, n_row, 1, block_width)
        x_own = (x_half + x_dual + col_total) / col_denom
        x_dual = x_dual + x_half - x_own
        shift_full = (row_total - y_anchor) / row_denom
        y_state = y_anchor + shift_full
        y_dual = y_dual + y_half - y_state
        input_duals = input_duals + x_proj - pick_blocks(x_own, cols_here, col_blocks, block_width)
        new_images = y_proj + image_duals - pick_blocks(shift_full, rows_here, row_blocks, block_width)
        image_duals = image_duals + y_proj - new_images
        images = new_images
    column_final = jnp.clip(x_own - x_dual - unit_cost, 0.0, capacity)
    row_final = jnp.clip(y_state - y_dual, row_lower, row_upper)
    return (column_final, row_final)


def solution(mesh):
    placed = (
        P(),
        P(),
        P("row", "col", None),
        P("row", "col", None),
        P("row", "col", None),
        P("row", "col"),
        P(None, "col"),
        P(None, "col"),
        P(None, "col"),
        P(None, "col"),
        P(None, "row"),
        P(None, "row"),
        P(None, "row"),
        P(None, "row"),
        P("row", "col", None, None, None),
        P("row", "col", None, None, None),
        P("row", "col", None, None, None),
    )
    return jax.shard_map(
        per_device,
        mesh=mesh,
        in_specs=placed,
        out_specs=(P(None, "col"), P(None, "row")),
        check_vma=False,
    )
```

```python
import functools

import jax
import jax.numpy as jnp
from jax import lax
from jax.experimental import pallas as pl
from jax.experimental.pallas import tpu as pltpu
from jax.sharding import PartitionSpec as P

ITERS = 2
MESH = pl.DeviceIdType.MESH
AXES = ("row", "col")


def peer_id(axis, peer):
    if axis == "row":
        return (peer, lax.axis_index("col"))
    return (lax.axis_index("row"), peer)


def reduce_kernel(n, group_axes, block_width, with_counts, *refs):
    groups = len(group_axes)
    if with_counts:
        info, live_ref, refs = refs[:groups], refs[groups], refs[groups + 1 :]
    ins = refs[:groups]
    outs = refs[groups : 2 * groups]
    scratch = refs[2 * groups :]
    size = 7 if with_counts else 6
    per = [scratch[size * g : size * g + 6] for g in range(groups)]
    width = ins[0].shape[1] // n
    sources = list(ins)

    def cols(index):
        return pl.ds(pl.multiple_of(index * width, width), width)

    def piece(ref, index):
        if len(ref.shape) == 3:
            return ref.at[index]
        return ref.at[:, cols(index)]

    if with_counts:
        slots = info[0].shape[0]
        live = live_ref[0]
        for g in range(groups):
            send = scratch[size * g + 6]
            data_rows = ins[g].shape[0]
            extra = send.shape[1] - data_rows
            counts = []
            for b in range(extra):
                count = jnp.int32(0)
                for k in range(slots):
                    count = count + jnp.where(
                        (k < live) & (info[g][k] == b), 1, 0
                    ).astype(jnp.int32)
                counts.append(count)
            count_rows = jnp.concatenate(
                [jnp.full((1, width), c, jnp.int32) for c in counts], axis=0
            ).astype(jnp.float32)
            for p in range(n):
                send[p, :data_rows, :] = ins[g][:, p * width : (p + 1) * width]
                send[p, data_rows:, :] = count_rows
            sources[g] = send
    issue_order = sorted(range(groups), key=lambda g: group_axes[g] != "col")
    barrier = pltpu.get_barrier_semaphore()
    for axis in [group_axes[g] for g in issue_order]:
        me = lax.axis_index(axis)
        for k in range(1, n):
            peer = lax.rem(me + k, n)
            pl.semaphore_signal(barrier, inc=1, device_id=peer_id(axis, peer), device_id_type=MESH)
    pl.semaphore_wait(barrier, groups * (n - 1))

    scatter = [None] * groups
    for g in issue_order:
        axis = group_axes[g]
        recv, gathered, s1, r1, s2, r2 = per[g]
        me = lax.axis_index(axis)
        copies = []
        for k in range(1, n):
            peer = lax.rem(me + k, n)
            copy = pltpu.make_async_remote_copy(
                src_ref=piece(sources[g], peer),
                dst_ref=recv.at[me],
                send_sem=s1.at[peer],
                recv_sem=r1.at[me],
                device_id=peer_id(axis, peer),
                device_id_type=MESH,
            )
            copy.start()
            copies.append(copy)
        scatter[g] = copies

    gathers = [None] * groups
    for g in issue_order:
        axis = group_axes[g]
        recv, gathered, s1, r1, s2, r2 = per[g]
        me = lax.axis_index(axis)
        for k in range(1, n):
            source = lax.rem(me + n - k, n)
            pltpu.make_async_remote_copy(
                src_ref=piece(sources[g], source),
                dst_ref=recv.at[source],
                send_sem=s1.at[source],
                recv_sem=r1.at[source],
                device_id=peer_id(axis, source),
                device_id_type=MESH,
            ).wait_recv()
        total = piece(sources[g], me)[...]
        for k in range(1, n):
            total = total + recv[lax.rem(me + k, n)]
        if with_counts:
            data_rows = ins[g].shape[0]
            outs[g][:data_rows, cols(me)] = total[:data_rows]
            blocks = outs[g].shape[1] // block_width
            for b in range(blocks):
                outs[g][data_rows : data_rows + 1, b * block_width : (b + 1) * block_width] = (
                    jnp.tile(total[data_rows + b : data_rows + b + 1, :], (1, block_width // width))
                )
        else:
            outs[g][:, cols(me)] = total
        copies = []
        for k in range(1, n):
            peer = lax.rem(me + k, n)
            copy = pltpu.make_async_remote_copy(
                src_ref=outs[g].at[pl.ds(0, ins[g].shape[0]), cols(me)],
                dst_ref=outs[g].at[pl.ds(0, ins[g].shape[0]), cols(me)],
                send_sem=s2.at[peer],
                recv_sem=r2.at[me],
                device_id=peer_id(axis, peer),
                device_id_type=MESH,
            )
            copy.start()
            copies.append(copy)
        gathers[g] = copies

    for g, axis in enumerate(group_axes):
        recv, gathered, s1, r1, s2, r2 = per[g]
        me = lax.axis_index(axis)
        for copy in scatter[g]:
            copy.wait_send()
        for k in range(1, n):
            source = lax.rem(me + n - k, n)
            pltpu.make_async_remote_copy(
                src_ref=outs[g].at[pl.ds(0, ins[g].shape[0]), cols(source)],
                dst_ref=outs[g].at[pl.ds(0, ins[g].shape[0]), cols(source)],
                send_sem=s2.at[source],
                recv_sem=r2.at[source],
                device_id=peer_id(axis, source),
                device_id_type=MESH,
            ).wait_recv()
        for copy in gathers[g]:
            copy.wait_send()


def all_reduce(arrays, group_axes, n, collective_id, block_width, info=None):
    extra = 0 if info is None else 8
    shapes = [(a.shape[0] + extra, a.shape[1]) for a in arrays]
    width = shapes[0][1] // n
    scratch = []
    for rows, _ in shapes:
        scratch += [
            pltpu.VMEM((n, rows, width), jnp.float32),
            pltpu.VMEM((n, rows, width), jnp.float32),
            pltpu.SemaphoreType.DMA((n,)),
            pltpu.SemaphoreType.DMA((n,)),
            pltpu.SemaphoreType.DMA((n,)),
            pltpu.SemaphoreType.DMA((n,)),
        ]
        if info is not None:
            scratch.append(pltpu.VMEM((n, rows, width), jnp.float32))
    in_specs = [pl.BlockSpec(memory_space=pltpu.VMEM)] * len(arrays)
    if info is not None:
        in_specs = [pl.BlockSpec(memory_space=pltpu.SMEM)] * len(info) + in_specs
        arrays = list(info) + arrays
    return pl.pallas_call(
        functools.partial(reduce_kernel, n, group_axes, block_width, info is not None),
        out_shape=tuple(jax.ShapeDtypeStruct(s, jnp.float32) for s in shapes),
        in_specs=in_specs,
        out_specs=tuple(pl.BlockSpec(memory_space=pltpu.VMEM) for _ in shapes),
        scratch_shapes=scratch,
        compiler_params=pltpu.CompilerParams(
            collective_id=collective_id, has_side_effects=True, vmem_limit_bytes=16 * 1024 * 1024
        ),
    )(*arrays)


def pick_blocks(full, index, blocks, block_width):
    chosen = full[None, :, :block_width]
    for b in range(1, blocks):
        chosen = jnp.where(
            (index == b)[:, None, None], full[None, :, b * block_width : (b + 1) * block_width], chosen
        )
    return chosen


def by_tile(stacked, matrices, tiles, contract, slots):
    results = [
        lax.dot_general(
            stacked, matrices[t], (((1,), (contract,)), ((), ())),
            preferred_element_type=jnp.float32,
        )
        for t in range(matrices.shape[0])
    ]
    chosen = results[0].reshape(slots, -1, stacked.shape[1])
    for t in range(1, len(results)):
        chosen = jnp.where(
            (tiles == t)[:, None, None], results[t].reshape(slots, -1, stacked.shape[1]), chosen
        )
    return chosen


def per_device(
    tile_matrix,
    tile_inverse,
    block_rows,
    block_cols,
    block_tiles,
    block_count,
    column_values,
    column_duals,
    unit_cost,
    capacity,
    row_values,
    row_duals,
    row_lower,
    row_upper,
    block_image,
    image_dual,
    input_dual,
):
    block_width = tile_matrix.shape[1]
    scenarios = column_values.shape[0]
    col_blocks = column_values.shape[1] // block_width
    row_blocks = row_values.shape[1] // block_width
    slot_total = block_rows.shape[2]
    n_row = lax.axis_size("row")
    rows_here = block_rows[0, 0]
    cols_here = block_cols[0, 0]
    tiles_here = block_tiles[0, 0]
    live_slot = jnp.arange(slot_total, dtype=jnp.int32) < block_count[0, 0]
    x_own = column_values
    x_dual = column_duals
    y_state = row_values
    y_dual = row_duals
    images = block_image[0, 0]
    image_duals = image_dual[0, 0]
    input_duals = input_dual[0, 0]
    col_mask = [(live_slot & (cols_here == b))[:, None, None] for b in range(col_blocks)]
    row_mask = [(live_slot & (rows_here == b))[:, None, None] for b in range(row_blocks)]
    col_denom = None
    row_denom = None
    for iteration in range(ITERS):
        x_half = jnp.clip(x_own - x_dual - unit_cost, 0.0, capacity)
        y_half = jnp.clip(y_state - y_dual, row_lower, row_upper)
        y_anchor = y_half + y_dual
        image_gap = (images - image_duals).astype(jnp.bfloat16).reshape(-1, block_width)
        pulled = by_tile(image_gap, tile_matrix, tiles_here, 1, slot_total)
        x_columns = pick_blocks(x_own, cols_here, col_blocks, block_width)
        merged = (x_columns - input_duals + pulled).astype(jnp.bfloat16).reshape(-1, block_width)
        x_proj = by_tile(merged, tile_inverse, tiles_here, 0, slot_total)
        y_proj = by_tile(
            x_proj.astype(jnp.bfloat16).reshape(-1, block_width), tile_matrix, tiles_here, 0,
            slot_total,
        )
        x_terms = x_proj + input_duals
        y_terms = y_proj + image_duals
        col_terms = jnp.concatenate(
            [jnp.sum(jnp.where(m, x_terms, 0.0), axis=0) for m in col_mask], axis=1
        )
        row_terms = jnp.concatenate(
            [jnp.sum(jnp.where(m, y_terms, 0.0), axis=0) for m in row_mask], axis=1
        )
        if iteration == 0:
            slot_info = [cols_here, rows_here, block_count.reshape(1)]
            col_total, row_total = all_reduce(
                [col_terms, row_terms], AXES, n_row, 0, block_width, slot_info
            )
            col_denom = 1.0 + col_total[scenarios : scenarios + 1]
            row_denom = 1.0 + row_total[scenarios : scenarios + 1]
            col_total = col_total[:scenarios]
            row_total = row_total[:scenarios]
        else:
            col_total, row_total = all_reduce([col_terms, row_terms], AXES, n_row, 1, block_width)
        x_own = (x_half + x_dual + col_total) / col_denom
        x_dual = x_dual + x_half - x_own
        shift_full = (row_total - y_anchor) / row_denom
        y_state = y_anchor + shift_full
        y_dual = y_dual + y_half - y_state
        input_duals = input_duals + x_proj - pick_blocks(x_own, cols_here, col_blocks, block_width)
        new_images = y_proj + image_duals - pick_blocks(shift_full, rows_here, row_blocks, block_width)
        image_duals = image_duals + y_proj - new_images
        images = new_images
    column_final = jnp.clip(x_own - x_dual - unit_cost, 0.0, capacity)
    row_final = jnp.clip(y_state - y_dual, row_lower, row_upper)
    return (column_final, row_final)


def solution(mesh):
    placed = (
        P(),
        P(),
        P("row", "col", None),
        P("row", "col", None),
        P("row", "col", None),
        P("row", "col"),
        P(None, "col"),
        P(None, "col"),
        P(None, "col"),
        P(None, "col"),
        P(None, "row"),
        P(None, "row"),
        P(None, "row"),
        P(None, "row"),
        P("row", "col", None, None, None),
        P("row", "col", None, None, None),
        P("row", "col", None, None, None),
    )
    return jax.shard_map(
        per_device,
        mesh=mesh,
        in_specs=placed,
        out_specs=(P(None, "col"), P(None, "row")),
        check_vma=False,
    )
```

```python
import functools

import jax
import jax.numpy as jnp
from jax import lax
from jax.experimental import pallas as pl
from jax.experimental.pallas import tpu as pltpu
from jax.sharding import PartitionSpec as P

ITERS = 2
MESH = pl.DeviceIdType.MESH
AXES = ("row", "col")


def peer_id(axis, peer):
    if axis == "row":
        return (peer, lax.axis_index("col"))
    return (lax.axis_index("row"), peer)


def reduce_kernel(n, group_axes, block_width, with_counts, finish, *refs):
    groups = len(group_axes)
    if with_counts:
        info, live_ref, refs = refs[:groups], refs[groups], refs[groups + 1 :]
    ins = refs[:groups]
    refs = refs[groups:]
    operands = []
    if finish is not None:
        for g in range(groups):
            operands.append(refs[: finish[g][1]])
            refs = refs[finish[g][1] :]
    outs = refs[:groups]
    scratch = refs[groups:]
    size = 7 if with_counts else 6
    per = [scratch[size * g : size * g + 6] for g in range(groups)]
    width = ins[0].shape[1] // n
    sources = list(ins)

    def cols(index):
        return pl.ds(pl.multiple_of(index * width, width), width)

    def piece(ref, index):
        if len(ref.shape) == 3:
            return ref.at[index]
        return ref.at[:, cols(index)]

    if with_counts:
        slots = info[0].shape[0]
        live = live_ref[0]
        for g in range(groups):
            send = scratch[size * g + 6]
            data_rows = ins[g].shape[0]
            extra = send.shape[1] - data_rows
            counts = []
            for b in range(extra):
                count = jnp.int32(0)
                for k in range(slots):
                    count = count + jnp.where(
                        (k < live) & (info[g][k] == b), 1, 0
                    ).astype(jnp.int32)
                counts.append(count)
            count_rows = jnp.concatenate(
                [jnp.full((1, width), c, jnp.int32) for c in counts], axis=0
            ).astype(jnp.float32)
            for p in range(n):
                send[p, :data_rows, :] = ins[g][:, p * width : (p + 1) * width]
                send[p, data_rows:, :] = count_rows
            sources[g] = send
    issue_order = sorted(range(groups), key=lambda g: group_axes[g] != "col")
    barrier = pltpu.get_barrier_semaphore()
    for axis in [group_axes[g] for g in issue_order]:
        me = lax.axis_index(axis)
        for k in range(1, n):
            peer = lax.rem(me + k, n)
            pl.semaphore_signal(barrier, inc=1, device_id=peer_id(axis, peer), device_id_type=MESH)
    pl.semaphore_wait(barrier, groups * (n - 1))

    scatter = [None] * groups
    for g in issue_order:
        axis = group_axes[g]
        recv, gathered, s1, r1, s2, r2 = per[g]
        me = lax.axis_index(axis)
        copies = []
        for k in range(1, n):
            peer = lax.rem(me + k, n)
            copy = pltpu.make_async_remote_copy(
                src_ref=piece(sources[g], peer),
                dst_ref=recv.at[me],
                send_sem=s1.at[peer],
                recv_sem=r1.at[me],
                device_id=peer_id(axis, peer),
                device_id_type=MESH,
            )
            copy.start()
            copies.append(copy)
        scatter[g] = copies

    gathers = [None] * groups
    for g in issue_order:
        axis = group_axes[g]
        recv, gathered, s1, r1, s2, r2 = per[g]
        me = lax.axis_index(axis)
        for k in range(1, n):
            source = lax.rem(me + n - k, n)
            pltpu.make_async_remote_copy(
                src_ref=piece(sources[g], source),
                dst_ref=recv.at[source],
                send_sem=s1.at[source],
                recv_sem=r1.at[source],
                device_id=peer_id(axis, source),
                device_id_type=MESH,
            ).wait_recv()
        total = piece(sources[g], me)[...]
        for k in range(1, n):
            total = total + recv[lax.rem(me + k, n)]
        if with_counts:
            data_rows = ins[g].shape[0]
            outs[g][:data_rows, cols(me)] = total[:data_rows]
            blocks = outs[g].shape[1] // block_width
            for b in range(blocks):
                outs[g][data_rows : data_rows + 1, b * block_width : (b + 1) * block_width] = (
                    jnp.tile(total[data_rows + b : data_rows + b + 1, :], (1, block_width // width))
                )
        else:
            if finish is not None:
                total = finish[g][0](total, *[ref[:, cols(me)] for ref in operands[g]])
            outs[g][:, cols(me)] = total
        copies = []
        for k in range(1, n):
            peer = lax.rem(me + k, n)
            copy = pltpu.make_async_remote_copy(
                src_ref=outs[g].at[pl.ds(0, ins[g].shape[0]), cols(me)],
                dst_ref=outs[g].at[pl.ds(0, ins[g].shape[0]), cols(me)],
                send_sem=s2.at[peer],
                recv_sem=r2.at[me],
                device_id=peer_id(axis, peer),
                device_id_type=MESH,
            )
            copy.start()
            copies.append(copy)
        gathers[g] = copies

    for g, axis in enumerate(group_axes):
        recv, gathered, s1, r1, s2, r2 = per[g]
        me = lax.axis_index(axis)
        for copy in scatter[g]:
            copy.wait_send()
        for k in range(1, n):
            source = lax.rem(me + n - k, n)
            pltpu.make_async_remote_copy(
                src_ref=outs[g].at[pl.ds(0, ins[g].shape[0]), cols(source)],
                dst_ref=outs[g].at[pl.ds(0, ins[g].shape[0]), cols(source)],
                send_sem=s2.at[source],
                recv_sem=r2.at[source],
                device_id=peer_id(axis, source),
                device_id_type=MESH,
            ).wait_recv()
        for copy in gathers[g]:
            copy.wait_send()


def all_reduce(arrays, group_axes, n, collective_id, block_width, info=None, finish=None):
    extra = 0 if info is None else 8
    shapes = [(a.shape[0] + extra, a.shape[1]) for a in arrays]
    width = shapes[0][1] // n
    scratch = []
    for rows, _ in shapes:
        scratch += [
            pltpu.VMEM((n, rows, width), jnp.float32),
            pltpu.VMEM((n, rows, width), jnp.float32),
            pltpu.SemaphoreType.DMA((n,)),
            pltpu.SemaphoreType.DMA((n,)),
            pltpu.SemaphoreType.DMA((n,)),
            pltpu.SemaphoreType.DMA((n,)),
        ]
        if info is not None:
            scratch.append(pltpu.VMEM((n, rows, width), jnp.float32))
    rules = None
    if finish is not None:
        rules = tuple((rule, len(extra)) for rule, extra in finish)
        arrays = arrays + [a for _, extra in finish for a in extra]
    in_specs = [pl.BlockSpec(memory_space=pltpu.VMEM)] * len(arrays)
    if info is not None:
        in_specs = [pl.BlockSpec(memory_space=pltpu.SMEM)] * len(info) + in_specs
        arrays = list(info) + arrays
    return pl.pallas_call(
        functools.partial(reduce_kernel, n, group_axes, block_width, info is not None, rules),
        out_shape=tuple(jax.ShapeDtypeStruct(s, jnp.float32) for s in shapes),
        in_specs=in_specs,
        out_specs=tuple(pl.BlockSpec(memory_space=pltpu.VMEM) for _ in shapes),
        scratch_shapes=scratch,
        compiler_params=pltpu.CompilerParams(
            collective_id=collective_id, has_side_effects=True, vmem_limit_bytes=16 * 1024 * 1024
        ),
    )(*arrays)


def column_rule(total, x_own, x_dual, cost, capacity, denom):
    x_half = jnp.minimum(jnp.maximum(x_own - x_dual - cost, 0.0), capacity)
    x_own = (x_half + x_dual + total) / denom
    x_dual = x_dual + x_half - x_own
    return jnp.minimum(jnp.maximum(x_own - x_dual - cost, 0.0), capacity)


def row_rule(total, y_state, y_dual, lower, upper, denom):
    y_half = jnp.minimum(jnp.maximum(y_state - y_dual, lower), upper)
    y_anchor = y_half + y_dual
    y_state = y_anchor + (total - y_anchor) / denom
    y_dual = y_dual + y_half - y_state
    return jnp.minimum(jnp.maximum(y_state - y_dual, lower), upper)


def pick_blocks(full, index, blocks, block_width):
    chosen = full[None, :, :block_width]
    for b in range(1, blocks):
        chosen = jnp.where(
            (index == b)[:, None, None], full[None, :, b * block_width : (b + 1) * block_width], chosen
        )
    return chosen


def by_tile(stacked, matrices, tiles, contract, slots):
    results = [
        lax.dot_general(
            stacked, matrices[t], (((1,), (contract,)), ((), ())),
            preferred_element_type=jnp.float32,
        )
        for t in range(matrices.shape[0])
    ]
    chosen = results[0].reshape(slots, -1, stacked.shape[1])
    for t in range(1, len(results)):
        chosen = jnp.where(
            (tiles == t)[:, None, None], results[t].reshape(slots, -1, stacked.shape[1]), chosen
        )
    return chosen


def per_device(
    tile_matrix,
    tile_inverse,
    block_rows,
    block_cols,
    block_tiles,
    block_count,
    column_values,
    column_duals,
    unit_cost,
    capacity,
    row_values,
    row_duals,
    row_lower,
    row_upper,
    block_image,
    image_dual,
    input_dual,
):
    block_width = tile_matrix.shape[1]
    scenarios = column_values.shape[0]
    col_blocks = column_values.shape[1] // block_width
    row_blocks = row_values.shape[1] // block_width
    slot_total = block_rows.shape[2]
    n_row = lax.axis_size("row")
    rows_here = block_rows[0, 0]
    cols_here = block_cols[0, 0]
    tiles_here = block_tiles[0, 0]
    live_slot = jnp.arange(slot_total, dtype=jnp.int32) < block_count[0, 0]
    x_own = column_values
    x_dual = column_duals
    y_state = row_values
    y_dual = row_duals
    images = block_image[0, 0]
    image_duals = image_dual[0, 0]
    input_duals = input_dual[0, 0]
    col_mask = [(live_slot & (cols_here == b))[:, None, None] for b in range(col_blocks)]
    row_mask = [(live_slot & (rows_here == b))[:, None, None] for b in range(row_blocks)]
    col_denom = None
    row_denom = None
    for iteration in range(ITERS):
        x_half = jnp.clip(x_own - x_dual - unit_cost, 0.0, capacity)
        y_half = jnp.clip(y_state - y_dual, row_lower, row_upper)
        y_anchor = y_half + y_dual
        image_gap = (images - image_duals).astype(jnp.bfloat16).reshape(-1, block_width)
        pulled = by_tile(image_gap, tile_matrix, tiles_here, 1, slot_total)
        x_columns = pick_blocks(x_own, cols_here, col_blocks, block_width)
        merged = (x_columns - input_duals + pulled).astype(jnp.bfloat16).reshape(-1, block_width)
        x_proj = by_tile(merged, tile_inverse, tiles_here, 0, slot_total)
        y_proj = by_tile(
            x_proj.astype(jnp.bfloat16).reshape(-1, block_width), tile_matrix, tiles_here, 0,
            slot_total,
        )
        x_terms = x_proj + input_duals
        y_terms = y_proj + image_duals
        col_terms = jnp.concatenate(
            [jnp.sum(jnp.where(m, x_terms, 0.0), axis=0) for m in col_mask], axis=1
        )
        row_terms = jnp.concatenate(
            [jnp.sum(jnp.where(m, y_terms, 0.0), axis=0) for m in row_mask], axis=1
        )
        if iteration == 0:
            slot_info = [cols_here, rows_here, block_count.reshape(1)]
            col_total, row_total = all_reduce(
                [col_terms, row_terms], AXES, n_row, 0, block_width, slot_info
            )
            col_denom = 1.0 + col_total[scenarios : scenarios + 1]
            row_denom = 1.0 + row_total[scenarios : scenarios + 1]
            col_total = col_total[:scenarios]
            row_total = row_total[:scenarios]
        elif iteration == ITERS - 1:
            return all_reduce(
                [col_terms, row_terms],
                AXES,
                n_row,
                1,
                block_width,
                finish=[
                    (column_rule, [x_own, x_dual, unit_cost, capacity, col_denom]),
                    (row_rule, [y_state, y_dual, row_lower, row_upper, row_denom]),
                ],
            )
        else:
            col_total, row_total = all_reduce([col_terms, row_terms], AXES, n_row, 2, block_width)
        x_own = (x_half + x_dual + col_total) / col_denom
        x_dual = x_dual + x_half - x_own
        shift_full = (row_total - y_anchor) / row_denom
        y_state = y_anchor + shift_full
        y_dual = y_dual + y_half - y_state
        input_duals = input_duals + x_proj - pick_blocks(x_own, cols_here, col_blocks, block_width)
        new_images = y_proj + image_duals - pick_blocks(shift_full, rows_here, row_blocks, block_width)
        image_duals = image_duals + y_proj - new_images
        images = new_images
    column_final = jnp.clip(x_own - x_dual - unit_cost, 0.0, capacity)
    row_final = jnp.clip(y_state - y_dual, row_lower, row_upper)
    return (column_final, row_final)


def solution(mesh):
    placed = (
        P(),
        P(),
        P("row", "col", None),
        P("row", "col", None),
        P("row", "col", None),
        P("row", "col"),
        P(None, "col"),
        P(None, "col"),
        P(None, "col"),
        P(None, "col"),
        P(None, "row"),
        P(None, "row"),
        P(None, "row"),
        P(None, "row"),
        P("row", "col", None, None, None),
        P("row", "col", None, None, None),
        P("row", "col", None, None, None),
    )
    return jax.shard_map(
        per_device,
        mesh=mesh,
        in_specs=placed,
        out_specs=(P(None, "col"), P(None, "row")),
        check_vma=False,
    )
```

```python
import functools

import jax
import jax.numpy as jnp
from jax import lax
from jax.experimental import pallas as pl
from jax.experimental.pallas import tpu as pltpu
from jax.sharding import PartitionSpec as P

ITERS = 2
MESH = pl.DeviceIdType.MESH
AXES = ("row", "col")


def peer_id(axis, peer):
    if axis == "row":
        return (peer, lax.axis_index("col"))
    return (lax.axis_index("row"), peer)


def reduce_kernel(n, group_axes, block_width, with_counts, finish, *refs):
    groups = len(group_axes)
    if with_counts:
        info, live_ref, refs = refs[:groups], refs[groups], refs[groups + 1 :]
    ins = refs[:groups]
    refs = refs[groups:]
    operands = []
    if finish is not None:
        for g in range(groups):
            operands.append(refs[: finish[g][1]])
            refs = refs[finish[g][1] :]
    outs = refs[:groups]
    scratch = refs[groups:]
    size = 7 if with_counts else 6
    per = [scratch[size * g : size * g + 6] for g in range(groups)]
    width = ins[0].shape[1] // n
    sources = list(ins)

    def cols(index):
        return pl.ds(pl.multiple_of(index * width, width), width)

    def piece(ref, index):
        if len(ref.shape) == 3:
            return ref.at[index]
        return ref.at[:, cols(index)]

    issue_order = sorted(range(groups), key=lambda g: group_axes[g] != "col")
    barrier = pltpu.get_barrier_semaphore()
    for axis in [group_axes[g] for g in issue_order]:
        me = lax.axis_index(axis)
        for k in range(1, n):
            peer = lax.rem(me + k, n)
            pl.semaphore_signal(barrier, inc=1, device_id=peer_id(axis, peer), device_id_type=MESH)
    if with_counts:
        slots = info[0].shape[0]
        live = live_ref[0]
        for g in range(groups):
            send = scratch[size * g + 6]
            data_rows = ins[g].shape[0]
            extra = send.shape[1] - data_rows
            counts = []
            for b in range(extra):
                count = jnp.int32(0)
                for k in range(slots):
                    count = count + jnp.where(
                        (k < live) & (info[g][k] == b), 1, 0
                    ).astype(jnp.int32)
                counts.append(count)
            count_rows = jnp.concatenate(
                [jnp.full((1, width), c, jnp.int32) for c in counts], axis=0
            ).astype(jnp.float32)
            for p in range(n):
                send[p, :data_rows, :] = ins[g][:, p * width : (p + 1) * width]
                send[p, data_rows:, :] = count_rows
            sources[g] = send
    pl.semaphore_wait(barrier, groups * (n - 1))

    scatter = [None] * groups
    for g in issue_order:
        axis = group_axes[g]
        recv, gathered, s1, r1, s2, r2 = per[g]
        me = lax.axis_index(axis)
        copies = []
        for k in range(1, n):
            peer = lax.rem(me + k, n)
            copy = pltpu.make_async_remote_copy(
                src_ref=piece(sources[g], peer),
                dst_ref=recv.at[me],
                send_sem=s1.at[peer],
                recv_sem=r1.at[me],
                device_id=peer_id(axis, peer),
                device_id_type=MESH,
            )
            copy.start()
            copies.append(copy)
        scatter[g] = copies

    gathers = [None] * groups
    for g in issue_order:
        axis = group_axes[g]
        recv, gathered, s1, r1, s2, r2 = per[g]
        me = lax.axis_index(axis)
        for k in range(1, n):
            source = lax.rem(me + n - k, n)
            pltpu.make_async_remote_copy(
                src_ref=piece(sources[g], source),
                dst_ref=recv.at[source],
                send_sem=s1.at[source],
                recv_sem=r1.at[source],
                device_id=peer_id(axis, source),
                device_id_type=MESH,
            ).wait_recv()
        total = piece(sources[g], me)[...]
        for k in range(1, n):
            total = total + recv[lax.rem(me + k, n)]
        if with_counts:
            data_rows = ins[g].shape[0]
            outs[g][:data_rows, cols(me)] = total[:data_rows]
            blocks = outs[g].shape[1] // block_width
            for b in range(blocks):
                outs[g][data_rows : data_rows + 1, b * block_width : (b + 1) * block_width] = (
                    jnp.tile(total[data_rows + b : data_rows + b + 1, :], (1, block_width // width))
                )
        else:
            if finish is not None:
                total = finish[g][0](total, *[ref[:, cols(me)] for ref in operands[g]])
            outs[g][:, cols(me)] = total
        copies = []
        for k in range(1, n):
            peer = lax.rem(me + k, n)
            copy = pltpu.make_async_remote_copy(
                src_ref=outs[g].at[pl.ds(0, ins[g].shape[0]), cols(me)],
                dst_ref=outs[g].at[pl.ds(0, ins[g].shape[0]), cols(me)],
                send_sem=s2.at[peer],
                recv_sem=r2.at[me],
                device_id=peer_id(axis, peer),
                device_id_type=MESH,
            )
            copy.start()
            copies.append(copy)
        gathers[g] = copies

    for g, axis in enumerate(group_axes):
        recv, gathered, s1, r1, s2, r2 = per[g]
        me = lax.axis_index(axis)
        for copy in scatter[g]:
            copy.wait_send()
        for k in range(1, n):
            source = lax.rem(me + n - k, n)
            pltpu.make_async_remote_copy(
                src_ref=outs[g].at[pl.ds(0, ins[g].shape[0]), cols(source)],
                dst_ref=outs[g].at[pl.ds(0, ins[g].shape[0]), cols(source)],
                send_sem=s2.at[source],
                recv_sem=r2.at[source],
                device_id=peer_id(axis, source),
                device_id_type=MESH,
            ).wait_recv()
        for copy in gathers[g]:
            copy.wait_send()


def all_reduce(arrays, group_axes, n, collective_id, block_width, info=None, finish=None):
    extra = 0 if info is None else 8
    shapes = [(a.shape[0] + extra, a.shape[1]) for a in arrays]
    width = shapes[0][1] // n
    scratch = []
    for rows, _ in shapes:
        scratch += [
            pltpu.VMEM((n, rows, width), jnp.float32),
            pltpu.VMEM((n, rows, width), jnp.float32),
            pltpu.SemaphoreType.DMA((n,)),
            pltpu.SemaphoreType.DMA((n,)),
            pltpu.SemaphoreType.DMA((n,)),
            pltpu.SemaphoreType.DMA((n,)),
        ]
        if info is not None:
            scratch.append(pltpu.VMEM((n, rows, width), jnp.float32))
    rules = None
    if finish is not None:
        rules = tuple((rule, len(extra)) for rule, extra in finish)
        arrays = arrays + [a for _, extra in finish for a in extra]
    in_specs = [pl.BlockSpec(memory_space=pltpu.VMEM)] * len(arrays)
    if info is not None:
        in_specs = [pl.BlockSpec(memory_space=pltpu.SMEM)] * len(info) + in_specs
        arrays = list(info) + arrays
    return pl.pallas_call(
        functools.partial(reduce_kernel, n, group_axes, block_width, info is not None, rules),
        out_shape=tuple(jax.ShapeDtypeStruct(s, jnp.float32) for s in shapes),
        in_specs=in_specs,
        out_specs=tuple(pl.BlockSpec(memory_space=pltpu.VMEM) for _ in shapes),
        scratch_shapes=scratch,
        compiler_params=pltpu.CompilerParams(
            collective_id=collective_id, has_side_effects=True, vmem_limit_bytes=16 * 1024 * 1024
        ),
    )(*arrays)


def column_rule(total, x_own, x_dual, cost, capacity, denom):
    x_half = jnp.minimum(jnp.maximum(x_own - x_dual - cost, 0.0), capacity)
    x_own = (x_half + x_dual + total) / denom
    x_dual = x_dual + x_half - x_own
    return jnp.minimum(jnp.maximum(x_own - x_dual - cost, 0.0), capacity)


def row_rule(total, y_state, y_dual, lower, upper, denom):
    y_half = jnp.minimum(jnp.maximum(y_state - y_dual, lower), upper)
    y_anchor = y_half + y_dual
    y_state = y_anchor + (total - y_anchor) / denom
    y_dual = y_dual + y_half - y_state
    return jnp.minimum(jnp.maximum(y_state - y_dual, lower), upper)


def pick_blocks(full, index, blocks, block_width):
    chosen = full[None, :, :block_width]
    for b in range(1, blocks):
        chosen = jnp.where(
            (index == b)[:, None, None], full[None, :, b * block_width : (b + 1) * block_width], chosen
        )
    return chosen


def by_tile(stacked, matrices, tiles, contract, slots):
    results = [
        lax.dot_general(
            stacked, matrices[t], (((1,), (contract,)), ((), ())),
            preferred_element_type=jnp.float32,
        )
        for t in range(matrices.shape[0])
    ]
    chosen = results[0].reshape(slots, -1, stacked.shape[1])
    for t in range(1, len(results)):
        chosen = jnp.where(
            (tiles == t)[:, None, None], results[t].reshape(slots, -1, stacked.shape[1]), chosen
        )
    return chosen


def per_device(
    tile_matrix,
    tile_inverse,
    block_rows,
    block_cols,
    block_tiles,
    block_count,
    column_values,
    column_duals,
    unit_cost,
    capacity,
    row_values,
    row_duals,
    row_lower,
    row_upper,
    block_image,
    image_dual,
    input_dual,
):
    block_width = tile_matrix.shape[1]
    scenarios = column_values.shape[0]
    col_blocks = column_values.shape[1] // block_width
    row_blocks = row_values.shape[1] // block_width
    slot_total = block_rows.shape[2]
    n_row = lax.axis_size("row")
    rows_here = block_rows[0, 0]
    cols_here = block_cols[0, 0]
    tiles_here = block_tiles[0, 0]
    live_slot = jnp.arange(slot_total, dtype=jnp.int32) < block_count[0, 0]
    x_own = column_values
    x_dual = column_duals
    y_state = row_values
    y_dual = row_duals
    images = block_image[0, 0]
    image_duals = image_dual[0, 0]
    input_duals = input_dual[0, 0]
    col_mask = [(live_slot & (cols_here == b))[:, None, None] for b in range(col_blocks)]
    row_mask = [(live_slot & (rows_here == b))[:, None, None] for b in range(row_blocks)]
    col_denom = None
    row_denom = None
    for iteration in range(ITERS):
        x_half = jnp.clip(x_own - x_dual - unit_cost, 0.0, capacity)
        y_half = jnp.clip(y_state - y_dual, row_lower, row_upper)
        y_anchor = y_half + y_dual
        image_gap = (images - image_duals).astype(jnp.bfloat16).reshape(-1, block_width)
        pulled = by_tile(image_gap, tile_matrix, tiles_here, 1, slot_total)
        x_columns = pick_blocks(x_own, cols_here, col_blocks, block_width)
        merged = (x_columns - input_duals + pulled).astype(jnp.bfloat16).reshape(-1, block_width)
        x_proj = by_tile(merged, tile_inverse, tiles_here, 0, slot_total)
        y_proj = by_tile(
            x_proj.astype(jnp.bfloat16).reshape(-1, block_width), tile_matrix, tiles_here, 0,
            slot_total,
        )
        x_terms = x_proj + input_duals
        y_terms = y_proj + image_duals
        col_terms = jnp.concatenate(
            [jnp.sum(jnp.where(m, x_terms, 0.0), axis=0) for m in col_mask], axis=1
        )
        row_terms = jnp.concatenate(
            [jnp.sum(jnp.where(m, y_terms, 0.0), axis=0) for m in row_mask], axis=1
        )
        if iteration == 0:
            slot_info = [cols_here, rows_here, block_count.reshape(1)]
            col_total, row_total = all_reduce(
                [col_terms, row_terms], AXES, n_row, 0, block_width, slot_info
            )
            col_denom = 1.0 + col_total[scenarios : scenarios + 1]
            row_denom = 1.0 + row_total[scenarios : scenarios + 1]
            col_total = col_total[:scenarios]
            row_total = row_total[:scenarios]
        elif iteration == ITERS - 1:
            return all_reduce(
                [col_terms, row_terms],
                AXES,
                n_row,
                1,
                block_width,
                finish=[
                    (column_rule, [x_own, x_dual, unit_cost, capacity, col_denom]),
                    (row_rule, [y_state, y_dual, row_lower, row_upper, row_denom]),
                ],
            )
        else:
            col_total, row_total = all_reduce([col_terms, row_terms], AXES, n_row, 2, block_width)
        x_own = (x_half + x_dual + col_total) / col_denom
        x_dual = x_dual + x_half - x_own
        shift_full = (row_total - y_anchor) / row_denom
        y_state = y_anchor + shift_full
        y_dual = y_dual + y_half - y_state
        input_duals = input_duals + x_proj - pick_blocks(x_own, cols_here, col_blocks, block_width)
        new_images = y_proj + image_duals - pick_blocks(shift_full, rows_here, row_blocks, block_width)
        image_duals = image_duals + y_proj - new_images
        images = new_images
    column_final = jnp.clip(x_own - x_dual - unit_cost, 0.0, capacity)
    row_final = jnp.clip(y_state - y_dual, row_lower, row_upper)
    return (column_final, row_final)


def solution(mesh):
    placed = (
        P(),
        P(),
        P("row", "col", None),
        P("row", "col", None),
        P("row", "col", None),
        P("row", "col"),
        P(None, "col"),
        P(None, "col"),
        P(None, "col"),
        P(None, "col"),
        P(None, "row"),
        P(None, "row"),
        P(None, "row"),
        P(None, "row"),
        P("row", "col", None, None, None),
        P("row", "col", None, None, None),
        P("row", "col", None, None, None),
    )
    return jax.shard_map(
        per_device,
        mesh=mesh,
        in_specs=placed,
        out_specs=(P(None, "col"), P(None, "row")),
        check_vma=False,
    )
```
